32 devices in a mesh: groups: 2 (over x), facet: 16 (over z, y, core).
Axes of the slice: x: 2, y: 2, z: 4, core: 2. Of those that a mesh axis runs over, the one named last changes fastest.
Arguments:
- facets: bfloat16 [32, 2, 512, 512], P(('groups', 'facet')), parts along dimension 0, may hold values from -6 to 6
- facet_offsets: int32 [32, 2], P(('groups', 'facet')), parts along dimension 0, may hold values from 0 to 511
- subgrid_offsets: int32 [32, 2], P('groups'), parts along dimension 0, may hold values from 0 to 511
- w_terms: float32 [32], P(('groups', 'facet')), parts along dimension 0, may hold values from 2 to 16
- tile_count: int32 [32], P(('groups', 'facet')), parts along dimension 0, may hold values from 1 to 16, as said below
- tile_offsets: int32 [512, 2], P(('groups', 'facet')), parts along dimension 0, may hold values from 0 to 256
- observed: bfloat16 [512, 2, 128, 128], P(('groups', 'facet')), parts along dimension 0, may hold values from -6 to 6
Outputs:
- residual: bfloat16 [512, 2, 128, 128], P(('groups', 'facet')), parts along dimension 0
- facet_update: bfloat16 [32, 2, 512, 512], P(('groups', 'facet')), parts along dimension 0
The draws below stay inside these ranges and needn't reach their ends.
There are 2 independent parts, one for each index of `groups`. The reference program is written for one: setup_inputs(seed, part) draws one part's arguments, and reference() takes and returns one part's arrays. A program takes and returns all parts, laid end to end along the dimension named above; each array names one. Nothing has to cross between parts.
Inputs may be any that keep to these rules, and one draw needn't show every extreme that they name: `tile_count`: live tile slots of each subgrid; some subgrid has all 16 slots live in every draw.
All inputs are finite; a program needn't handle non-finite values.
Results may differ from the reference program's by a relative error of at most 0.017.
Values may be sent and summed in bfloat16 or wider, within the bound.
A program may use at most 64 MiB of HBM per device.

```python
import math
import jax
import jax.numpy as jnp
from jax import lax

F = 512
M = 128
SG = 512
TV = 128
TCAP = 16
FACETS = 16
TILES = 256


def draw_tile_count(key, part):
    keys = jax.random.split(key, 4)
    light = jax.random.randint(keys[0], (FACETS,), 1, max(2, TCAP // 4 + 1))
    heavy = jax.random.randint(keys[1], (FACETS,), max(1, TCAP // 2), TCAP + 1)
    chosen = jax.random.randint(keys[2], (FACETS,), 0, 8) == 0
    counts = jnp.where(chosen, heavy, light)
    fullest = jax.random.randint(keys[3], (), 0, FACETS)
    counts = jnp.where(jnp.arange(FACETS) == fullest, TCAP, counts)
    return counts.astype(jnp.int32)


def plant(array, key, smallest, high):
    longest = array.shape.index(max(array.shape))
    spots = []
    for shift in (0, 1):
        where = [jax.random.randint(jax.random.fold_in(key, axis), (), 0, length) for axis, length in enumerate(array.shape)]
        where[longest] = (where[longest] + shift) % array.shape[longest]
        spots.append(tuple(where))
    return array.at[spots[0]].set(smallest).at[spots[1]].set(high)


def shard_levels(key, extent, cuts, least, largest):
    level = 1.0
    for axis_at, parts in cuts:
        heights = jax.random.uniform(jax.random.fold_in(jax.random.fold_in(key, 6), axis_at), (parts,), jnp.float32, least / len(cuts), largest / len(cuts))
        level = level * jnp.repeat(jnp.exp(heights), extent[axis_at] // parts).reshape((-1,) + (1,) * (len(extent) - 1 - axis_at))
    return level


def scatter_about(rng, dims, scale, bound, cuts=(), kind=jnp.bfloat16):
    drawn = scale * jax.random.normal(rng, dims, jnp.float32)
    if cuts:
        drawn = drawn * shard_levels(rng, dims, cuts, -0.22, 0.18)
    return jnp.clip(drawn, -bound, bound).astype(kind)


def setup_inputs(seed: int = 0, part: int = 0) -> dict:
    key_list = jax.random.split(jax.random.key(seed), 8)
    part_splits = jax.random.split(jax.random.fold_in(key_list[7], part), 8)
    facets = scatter_about(part_splits[0], (FACETS, 2, F, F), 1.0, 6.0, ((0, 16),))
    facet_offsets = plant(jax.random.randint(part_splits[1], (FACETS, 2), 0, F), jax.random.fold_in(part_splits[1], 1), 0, F - 1).astype(jnp.int32)
    subgrid_offsets = plant(jax.random.randint(part_splits[2], (FACETS, 2), 0, F), jax.random.fold_in(part_splits[2], 1), 0, F - 1).astype(jnp.int32)
    w_terms = jnp.clip(jnp.exp(math.log(16.0) - 2.0794415 * jax.random.uniform(part_splits[3], (FACETS,), jnp.float32) ** shard_levels(part_splits[3], (FACETS,), ((0, 16),), -0.2, 0.2)), 2.0, 16.0)
    tile_count = draw_tile_count(jax.random.fold_in(jax.random.fold_in(key_list[7], part), 71), part)
    tile_offsets = plant(jax.random.randint(part_splits[5], (TILES, 2), 0, SG - 2 * TV + 1), jax.random.fold_in(part_splits[5], 1), 0, SG - 2 * TV).astype(jnp.int32)
    observed = scatter_about(part_splits[6], (TILES, 2, TV, TV), 1.0, 6.0, ((0, 16),))
    return {"facets": facets, "facet_offsets": facet_offsets, "subgrid_offsets": subgrid_offsets, "w_terms": w_terms, "tile_count": tile_count, "tile_offsets": tile_offsets, "observed": observed}


TWO_PI = 2.0 * math.pi

def basis_tables():
    index_f = jnp.arange(F, dtype=jnp.int32)
    product = index_f[:, None] * index_f[None, :] % F
    angle = -TWO_PI * product.astype(jnp.float32) / F
    scale = 1.0 / math.sqrt(F)
    return ((jnp.cos(angle) * scale).astype(jnp.bfloat16), (jnp.sin(angle) * scale).astype(jnp.bfloat16))

def padding_tables(facet_count):
    rows = jnp.arange(SG, dtype=jnp.int32)
    columns = jnp.arange(M, dtype=jnp.int32)
    product = rows[:, None] * columns[None, :] % SG
    angle = TWO_PI * product.astype(jnp.float32) / SG
    scale = (M * math.sqrt(facet_count)) ** (-0.5)
    return ((jnp.cos(angle) * scale).astype(jnp.bfloat16), (jnp.sin(angle) * scale).astype(jnp.bfloat16))

def taper_square():
    position = jnp.arange(M, dtype=jnp.float32)
    taper = 0.6 + 0.4 * jnp.sin(math.pi * (position + 0.5) / M)
    return taper[:, None] * taper[None, :]

def kernel_table():
    rows = jnp.arange(TV, dtype=jnp.float32)[:, None]
    columns = jnp.arange(2 * TV, dtype=jnp.float32)[None, :]
    distance = columns - 2.0 * rows - 1.0
    value = 0.75 * jnp.exp(-(distance / 1.5) * (distance / 1.5))
    return jnp.where(jnp.abs(distance) <= 4.0, value, jnp.zeros_like(value)).astype(jnp.bfloat16)

def facet_phase(offset):
    index_m = jnp.arange(M, dtype=jnp.int32)
    total = ((index_m * offset[0])[:, None] + (index_m * offset[1])[None, :]) % F
    angle = TWO_PI * total.astype(jnp.float32) / F
    return (jnp.cos(angle), jnp.sin(angle))

def screen_table(w_value):
    centred = jnp.arange(SG, dtype=jnp.float32) - SG / 2.0
    radius = (centred[:, None] * centred[:, None] + centred[None, :] * centred[None, :]) / (SG * SG)
    angle = TWO_PI * w_value * (jnp.sqrt(1.0 + radius) - 1.0)
    return (jnp.cos(angle), jnp.sin(angle))

def matmul(left, right):
    return jnp.dot(left, right, preferred_element_type=jnp.float32)

def complex_dot(left_real, left_imag, right_real, right_imag):
    real_part = matmul(left_real, right_real) - matmul(left_imag, right_imag)
    imag_part = matmul(left_real, right_imag) + matmul(left_imag, right_real)
    return (real_part, imag_part)

def facet_spectrum(facet, basis_real, basis_imag):
    half_real, half_imag = complex_dot(facet[0], facet[1], basis_real.T, basis_imag.T)
    return complex_dot(basis_real, basis_imag, half_real.astype(jnp.bfloat16), half_imag.astype(jnp.bfloat16))

def extract(spectrum_real, spectrum_imag, offsets, phase_cos, phase_sin, taper2):
    stacked = jnp.stack([spectrum_real, spectrum_imag])
    padded = jnp.concatenate([stacked, stacked[:, :M, :]], axis=1)
    padded = jnp.concatenate([padded, padded[:, :, :M]], axis=2)
    zero = jnp.zeros((), jnp.int32)

    def window(offset):
        return lax.dynamic_slice(padded, (zero, offset[0].astype(jnp.int32), offset[1].astype(jnp.int32)), (2, M, M))
    windows = jax.vmap(window)(offsets)
    real_part = taper2 * (phase_cos * windows[:, 0] - phase_sin * windows[:, 1])
    imag_part = taper2 * (phase_cos * windows[:, 1] + phase_sin * windows[:, 0])
    return jnp.stack([real_part, imag_part], axis=1).astype(jnp.bfloat16)

def subgrid_model(summed, pad_real, pad_imag, screen_cos, screen_sin):
    inner_real, inner_imag = complex_dot(pad_real, pad_imag, summed[0], summed[1])
    image_real, image_imag = complex_dot(inner_real.astype(jnp.bfloat16), inner_imag.astype(jnp.bfloat16), pad_real.T, pad_imag.T)
    model_real = screen_cos * image_real - screen_sin * image_imag
    model_imag = screen_cos * image_imag + screen_sin * image_real
    return jnp.stack([model_real, model_imag]).astype(jnp.bfloat16)

def tile_terms(model, observed_tile, offset, kernel):
    zero = jnp.zeros((), jnp.int32)
    window = lax.dynamic_slice(model, (zero, offset[0].astype(jnp.int32), offset[1].astype(jnp.int32)), (2, 2 * TV, 2 * TV))
    kernel32 = kernel.astype(jnp.float32)
    left = jnp.einsum('jq,cqk->cjk', kernel32, window.astype(jnp.float32)).astype(jnp.bfloat16)
    predicted = jnp.einsum('cjk,lk->cjl', left.astype(jnp.float32), kernel32)
    residual = (observed_tile.astype(jnp.float32) - predicted).astype(jnp.bfloat16)
    back = jnp.einsum('cjl,lk->cjk', residual.astype(jnp.float32), kernel32).astype(jnp.bfloat16)
    spread = jnp.einsum('jq,cjk->cqk', kernel32, back.astype(jnp.float32))
    return (residual, spread)

def add_window(adjoint, spread, offset):
    zero = jnp.zeros((), jnp.int32)
    start = (zero, offset[0].astype(jnp.int32), offset[1].astype(jnp.int32))
    current = lax.dynamic_slice(adjoint, start, spread.shape)
    return lax.dynamic_update_slice(adjoint, current + spread, start)

def back_coefficients(adjoint, pad_real, pad_imag, screen_cos, screen_sin):
    screened_real = (screen_cos * adjoint[0] + screen_sin * adjoint[1]).astype(jnp.bfloat16)
    screened_imag = (screen_cos * adjoint[1] - screen_sin * adjoint[0]).astype(jnp.bfloat16)
    reduced_real = (matmul(pad_real.T, screened_real) + matmul(pad_imag.T, screened_imag)).astype(jnp.bfloat16)
    reduced_imag = (matmul(pad_real.T, screened_imag) - matmul(pad_imag.T, screened_real)).astype(jnp.bfloat16)
    coef_real = matmul(reduced_real, pad_real) + matmul(reduced_imag, pad_imag)
    coef_imag = matmul(reduced_imag, pad_real) - matmul(reduced_real, pad_imag)
    return jnp.stack([coef_real, coef_imag]).astype(jnp.bfloat16)

def facet_back(back_spectrum, basis_real, basis_imag):
    half_real = (matmul(basis_real, back_spectrum[0]) + matmul(basis_imag, back_spectrum[1])).astype(jnp.bfloat16)
    half_imag = (matmul(basis_real, back_spectrum[1]) - matmul(basis_imag, back_spectrum[0])).astype(jnp.bfloat16)
    update_real = matmul(half_real, basis_real) + matmul(half_imag, basis_imag)
    update_imag = matmul(half_imag, basis_real) - matmul(half_real, basis_imag)
    return jnp.stack([update_real, update_imag]).astype(jnp.bfloat16)

def reference(facets, facet_offsets, subgrid_offsets, w_terms, tile_count, tile_offsets, observed):
    facet_count = facets.shape[0]
    basis_real, basis_imag = basis_tables()
    pad_real, pad_imag = padding_tables(facet_count)
    taper2 = taper_square()
    kernel = kernel_table()

    def forward_step(total, inputs):
        facet, offset = inputs
        spectrum_real, spectrum_imag = facet_spectrum(facet, basis_real, basis_imag)
        phase_cos, phase_sin = facet_phase(offset)
        contribution = extract(spectrum_real, spectrum_imag, subgrid_offsets, phase_cos, phase_sin, taper2)
        return (total + contribution.astype(jnp.float32), None)
    summed, _ = lax.scan(forward_step, jnp.zeros((facet_count, 2, M, M), jnp.float32), (facets, facet_offsets))
    observed_dev = observed.reshape(facet_count, TCAP, 2, TV, TV)
    offsets_dev = tile_offsets.reshape(facet_count, TCAP, 2)

    def subgrid_step(inputs):
        summed_one, w_value, count, tile_obs, tile_off = inputs
        screen_cos, screen_sin = screen_table(w_value)
        model = subgrid_model(summed_one.astype(jnp.bfloat16), pad_real, pad_imag, screen_cos, screen_sin)

        def tile_step(adjoint, tile_in):
            observed_tile, offset, slot = tile_in
            residual, spread = tile_terms(model, observed_tile, offset, kernel)
            live = slot < count
            residual = jnp.where(live, residual, jnp.zeros_like(residual))
            spread = jnp.where(live, spread, jnp.zeros_like(spread))
            return (add_window(adjoint, spread, offset), residual)
        adjoint, residuals = lax.scan(tile_step, jnp.zeros((2, SG, SG), jnp.float32), (tile_obs, tile_off, jnp.arange(TCAP, dtype=jnp.int32)))
        return (residuals, back_coefficients(adjoint, pad_real, pad_imag, screen_cos, screen_sin))
    residuals, coefficients = lax.map(subgrid_step, (summed, w_terms, tile_count, observed_dev, offsets_dev))
    index_m = jnp.arange(M, dtype=jnp.int32)
    row_index = (subgrid_offsets[:, 0:1] + index_m[None, :]) % F
    column_index = (subgrid_offsets[:, 1:2] + index_m[None, :]) % F
    coef32 = coefficients.astype(jnp.float32)

    def backward_step(offset):
        phase_cos, phase_sin = facet_phase(offset)
        values_real = taper2 * (phase_cos * coef32[:, 0] + phase_sin * coef32[:, 1])
        values_imag = taper2 * (phase_cos * coef32[:, 1] - phase_sin * coef32[:, 0])
        values = jnp.stack([values_real, values_imag])
        spectrum = jnp.zeros((2, F, F), jnp.float32).at[:, row_index[:, :, None], column_index[:, None, :]].add(values)
        return facet_back(spectrum.astype(jnp.bfloat16), basis_real, basis_imag)
    updates = lax.map(backward_step, facet_offsets)
    return (residuals.reshape(facet_count * TCAP, 2, TV, TV), updates)
```

```python
import functools
import math

import jax
import jax.numpy as jnp
import ml_dtypes
import numpy as np
from jax import lax
from jax.experimental import pallas as pl
from jax.experimental.pallas import tpu as pltpu
from jax.sharding import PartitionSpec as P

F = 512
M = 128
SG = 512
TV = 128
WIDE = F + M

BF16 = jnp.bfloat16
F32 = jnp.float32
TWO_PI = 2.0 * math.pi
MESH = pl.DeviceIdType.MESH
VMEM = pltpu.VMEM
LIMIT = 48 * 1024 * 1024


def basis_table():
    index = np.arange(F)
    angle = -TWO_PI * (index[:, None] * index[None, :] % F) / F
    scale = 1.0 / math.sqrt(F)
    return np.stack([np.cos(angle) * scale, np.sin(angle) * scale]).astype(ml_dtypes.bfloat16)


def padding_table(facet_count):
    angle = TWO_PI * (np.arange(SG)[:, None] * np.arange(M)[None, :] % SG) / SG
    scale = (M * math.sqrt(facet_count)) ** (-0.5)
    return np.stack([np.cos(angle) * scale, np.sin(angle) * scale]).astype(ml_dtypes.bfloat16)


def taper_square():
    taper = 0.6 + 0.4 * np.sin(math.pi * (np.arange(M) + 0.5) / M)
    return (taper[:, None] * taper[None, :]).astype(np.float32)


def dot(left, right):
    return jnp.dot(left, right, preferred_element_type=F32)


def cos_sin_turns(turns):
    quarter = jnp.floor(turns * 4.0 + 0.5)
    y = (turns - quarter * 0.25) * TWO_PI
    y2 = y * y
    sine = y * (1.0 + y2 * (-1.0 / 6 + y2 * (1.0 / 120 + y2 * (-1.0 / 5040 + y2 * (1.0 / 362880)))))
    cosine = 1.0 + y2 * (
        -0.5 + y2 * (1.0 / 24 + y2 * (-1.0 / 720 + y2 * (1.0 / 40320 - y2 * (1.0 / 3628800))))
    )
    which = quarter.astype(jnp.int32) & 3
    odd = (which & 1) == 1
    first = jnp.where(odd, sine, cosine)
    second = jnp.where(odd, cosine, sine)
    cos_value = jnp.where((which == 1) | (which == 2), -first, first)
    sin_value = jnp.where(which >= 2, -second, second)
    return cos_value, sin_value


def tapered_phase(offset_ref, taper_ref):
    rows = lax.broadcasted_iota(jnp.int32, (M, M), 0)
    columns = lax.broadcasted_iota(jnp.int32, (M, M), 1)
    total = (rows * offset_ref[0, 0] + columns * offset_ref[0, 1]) & (F - 1)
    cos_value, sin_value = cos_sin_turns(total.astype(F32) * (1.0 / F))
    taper = taper_ref[...]
    return cos_value * taper, sin_value * taper


def forward_kernel(
    n, foff_h, soff_h, facet_h, basis_h, taper_h, out,
    half, spec, phase, foff, soff, facet, basis, taper, sems
):
    pairs = ((facet_h, facet), (basis_h, basis), (taper_h, taper), (foff_h, foff), (soff_h, soff))
    copies = [pltpu.make_async_copy(src, dst, sems.at[i]) for i, (src, dst) in enumerate(pairs)]
    for copy in copies:
        copy.start()
    for copy in copies:
        copy.wait()
    phase[0], phase[1] = tapered_phase(foff, taper)
    lanes = lax.broadcasted_iota(jnp.int32, (M, M), 1)

    @pl.loop(0, 2)
    def _(c):
        cols = pl.ds(pl.multiple_of(c * 256, 256), 256)
        br, bi = basis[0, :, cols], basis[1, :, cols]
        half[0, :, cols] = (dot(facet[0], br) - dot(facet[1], bi)).astype(BF16)
        half[1, :, cols] = (dot(facet[0], bi) + dot(facet[1], br)).astype(BF16)

    @pl.loop(0, 2)
    def _(c):
        cols = pl.ds(pl.multiple_of(c * 256, 256), 256)
        hr, hi = half[0, :, cols], half[1, :, cols]
        real = dot(basis[0], hr) - dot(basis[1], hi)
        imag = dot(basis[0], hi) + dot(basis[1], hr)
        for side in range(2):
            part = slice(side * M, side * M + M)
            spec[0, c * 2 + side, 0:F] = real[:, part]
            spec[1, c * 2 + side, 0:F] = imag[:, part]

    spec[:, 0 : F // M, F:WIDE] = spec[:, 0 : F // M, 0:M]
    spec[:, F // M] = spec[:, 0]

    @pl.loop(0, n, unroll=4)
    def _(s):
        sx, sy = soff[0, s], soff[1, s]
        tile, offset = sy >> 7, sy & 127
        shift = (M - offset) & 127
        kept = lanes < M - offset
        rows = pl.ds(sx, M)

        def window(plane):
            low = pltpu.roll(spec[plane, tile, rows], shift, 1)
            high = pltpu.roll(spec[plane, tile + 1, rows], shift, 1)
            return jnp.where(kept, low, high)

        real, imag = window(0), window(1)
        pc, ps = phase[0], phase[1]
        out[s & 1, (s >> 1) & 1, s >> 2, 0] = (pc * real - ps * imag).astype(BF16)
        out[s & 1, (s >> 1) & 1, s >> 2, 1] = (pc * imag + ps * real).astype(BF16)


def place(n):
    me = lax.axis_index("facet")
    quads = n // 4
    far_first = [1 + (t + quads // 2 - 1) % (quads - 1) for t in range(quads - 1)]
    return quads, me // 4, lax.rem(me // 2, 2), lax.rem(me, 2), far_first


def index(quad, middle, core):
    return quad * 4 + middle * 2 + core


def greet(peers):
    barrier = pltpu.get_barrier_semaphore()
    for peer in peers:
        pl.semaphore_signal(barrier, inc=1, device_id={"facet": peer}, device_id_type=MESH)
    pl.semaphore_wait(barrier, len(peers))


def send(src, dst, send_sem, recv_sem, peer):
    return pltpu.make_async_remote_copy(
        src_ref=src, dst_ref=dst, send_sem=send_sem, recv_sem=recv_sem,
        device_id={"facet": peer}, device_id_type=MESH,
    )


def fill_screen(w_value, screen):
    @pl.loop(0, 4)
    def _(c):
        rows = pl.ds(pl.multiple_of(c * 128, 128), 128)
        u = (lax.broadcasted_iota(jnp.int32, (128, SG), 0) + (c * 128 - 256)).astype(F32)
        v = (lax.broadcasted_iota(jnp.int32, (128, SG), 1) - 256).astype(F32)
        radius = (u * u + v * v) * (1.0 / (SG * SG))
        cos_value, sin_value = cos_sin_turns(w_value * (jnp.sqrt(1.0 + radius) - 1.0))
        screen[0, rows, :] = cos_value
        screen[1, rows, :] = sin_value


def reduce_kernel(
    n, slots, w_ref, toff, contrib, summed, screen, eu, eu_t, ev, ev_t, near, pair, mid, quad_sum, far,
    near_s, near_r, mid_s, mid_r, far_s, far_r
):
    quads, quad, middle, core, far_first = place(n)
    other = 1 - middle
    sibling, beside = index(quad, middle, 1 - core), index(quad, other, core)
    away = [lax.rem(quad + k, quads) for k in far_first]
    order = away + [quad]
    greet([index(j, middle, core) for j in away] + [beside, sibling])

    def near_copy(half, j):
        return send(contrib.at[1 - core, half, j], near.at[half, j], near_s.at[half, j], near_r.at[half, j], sibling)

    def mid_copy(j):
        return send(pair.at[j], mid.at[j], mid_s.at[j], mid_r.at[j], beside)

    def far_copy(j, slot):
        return send(quad_sum.at[j], far.at[slot], far_s.at[j], far_r.at[slot], index(j, middle, core))

    def near_sum(half, j):
        return contrib[core, half, j].astype(F32) + near[half, j].astype(F32)

    for half in (other, middle):
        for j in order:
            near_copy(half, j).start()
    for j in order:
        near_copy(other, j).wait_recv()
        pair[j] = near_sum(other, j).astype(BF16)
        mid_copy(j).start()
    for j in away:
        near_copy(middle, j).wait_recv()
        mid_copy(j).wait_recv()
        quad_sum[j] = (near_sum(middle, j) + mid[j].astype(F32)).astype(BF16)
        far_copy(j, quad).start()
    fill_screen(w_ref[0], screen)
    fill_edges(slots, toff, eu, eu_t, ev, ev_t)
    near_copy(middle, quad).wait_recv()
    mid_copy(quad).wait_recv()
    total = near_sum(middle, quad) + mid[quad].astype(F32)
    for j in reversed(away):
        far_copy(j, j).wait_recv()
        total = total + far[j].astype(F32)
    summed[...] = total
    for j in order:
        near_copy(other, j).wait_send()
        near_copy(middle, j).wait_send()
        mid_copy(j).wait_send()
    for j in away:
        far_copy(j, quad).wait_send()


def gather_kernel(n, mine, out, near_s, near_r, mid_s, mid_r, far_s, far_r, local):
    quads, quad, middle, core, far_first = place(n)
    other = 1 - middle
    me = index(quad, middle, core)
    sibling, beside = index(quad, middle, 1 - core), index(quad, other, core)
    away = [lax.rem(quad + k, quads) for k in far_first]
    back = [lax.rem(quad + quads - k, quads) for k in far_first]
    greet([index(j, middle, core) for j in away] + [beside, sibling])

    def far_copy(j, slot):
        return send(
            mine, out.at[index(slot, middle, core)], far_s.at[j], far_r.at[slot], index(j, middle, core)
        )

    def mid_copy(j, half):
        piece = out.at[index(j, half, core)]
        return send(piece, piece, mid_s.at[j], mid_r.at[j], beside)

    def near_copy(half, j, side):
        piece = out.at[index(j, half, side)]
        return send(piece, piece, near_s.at[half, j], near_r.at[half, j], sibling)

    for j in away:
        far_copy(j, quad).start()
    mid_own = send(mine, out.at[me], mid_s.at[quad], mid_r.at[quad], beside)
    mid_own.start()
    near_own = send(mine, out.at[me], near_s.at[middle, quad], near_r.at[middle, quad], sibling)
    near_own.start()
    own = pltpu.make_async_copy(mine, out.at[me], local)
    own.start()
    for j in back:
        far_copy(j, j).wait_recv()
        mid_copy(j, middle).start()
        near_copy(middle, j, core).start()
    for j in [quad] + back:
        mid_copy(j, other).wait_recv()
        near_copy(other, j, core).start()
    for half in (middle, other):
        for j in [quad] + back:
            near_copy(half, j, 1 - core).wait_recv()
    for j in away:
        far_copy(j, quad).wait_send()
        mid_copy(j, middle).wait_send()
        near_copy(middle, j, core).wait_send()
        near_copy(other, j, core).wait_send()
    near_copy(other, quad, core).wait_send()
    mid_own.wait_send()
    near_own.wait_send()
    own.wait()


def tap_values():
    taps = np.arange(5, dtype=np.float32)
    value = 0.75 * np.exp(-(taps / 1.5) * (taps / 1.5))
    return [float(x) for x in value.astype(ml_dtypes.bfloat16).astype(np.float32)]


def smooth_table():
    order = np.concatenate([np.arange(0, SG, 2), np.arange(1, SG, 2)])
    distance = np.abs(np.arange(SG)[None, :] - order[:, None])
    taps = np.array(tap_values() + [0.0], np.float32)
    return taps[np.minimum(distance, 5)].astype(ml_dtypes.bfloat16)


def edge_values(position, offset, slot, live):
    distance = jnp.abs(position - offset - 2 * slot - 1)
    value = jnp.zeros(distance.shape, F32)
    for step, tap in enumerate(tap_values()):
        value = jnp.where(distance == step, tap, value)
    inside = (position >= offset) & (position < offset + 2 * TV) & live
    return jnp.where(inside, value, 0.0).astype(BF16)


def row_slot(spot):
    i = spot & 7
    return jnp.where(i < 2, i, i + 120), (i < 2) | (i >= 6)


def column_slot(spot):
    i = (spot + 2) & 7
    return jnp.where(i >= 2, i - 2, i + 126), i < 4


def fill_edges(slots, toff, eu, eu_t, ev, ev_t):
    @pl.loop(0, slots // 2)
    def _(c):
        spot = lax.broadcasted_iota(jnp.int32, (16, SG), 0)
        lane = lax.broadcasted_iota(jnp.int32, (16, SG), 1)
        rows = pl.ds(pl.multiple_of(c * 16, 16), 16)
        first, second, third = 2 * c, 2 * c + 1, (2 * c + 2) & (slots - 1)
        offset = jnp.where(spot < 8, toff[0, first], toff[0, second])
        eu[rows, :] = edge_values(lane, offset, *row_slot(spot))
        offset = jnp.where(spot < 6, toff[1, first], jnp.where(spot < 14, toff[1, second], toff[1, third]))
        ev[rows, :] = edge_values(lane, offset, *column_slot(spot))

    lane = lax.broadcasted_iota(jnp.int32, (1, 8 * slots), 1)
    row_owner, column_owner = lane >> 3, ((lane + 2) & (8 * slots - 1)) >> 3
    row_offset, column_offset = jnp.zeros_like(lane), jnp.zeros_like(lane)
    for t in range(slots):
        row_offset = jnp.where(row_owner == t, toff[0, t], row_offset)
        column_offset = jnp.where(column_owner == t, toff[1, t], column_offset)

    @pl.loop(0, SG // 64)
    def _(c):
        rows = pl.ds(pl.multiple_of(c * 64, 64), 64)
        position = lax.broadcasted_iota(jnp.int32, (64, 8 * slots), 0) + c * 64
        spot = lax.broadcasted_iota(jnp.int32, (64, 8 * slots), 1)
        eu_t[rows, :] = edge_values(position, row_offset, *row_slot(spot))
        ev_t[rows, :] = edge_values(position, column_offset, *column_slot(spot))


def subgrid_kernel(
    slots, count_ref, toff, summed, screen, eu, eu_t, ev, ev_t, pad, pad_t, smooth, smooth_t, observed,
    residual_h, coefficient, inner, model, left, grid, spread, flat, sent, sems
):
    edges = SG // 128
    spread[...] = jnp.zeros_like(spread)
    sr, si = summed[0], summed[1]
    stacked = jnp.concatenate(
        [jnp.concatenate([sr, si], axis=1), jnp.concatenate([-si, sr], axis=1)], axis=0
    ).astype(BF16)
    inner[...] = dot(pad[...], stacked).astype(BF16)

    for c in range(2):
        cols = slice(c * 256, c * 256 + 256)
        late = slice(SG + c * 256, SG + c * 256 + 256)
        real, imag = dot(inner[...], pad_t[:, cols]), dot(inner[...], pad_t[:, late])
        cos_value, sin_value = screen[0, :, cols], screen[1, :, cols]
        model[:, cols] = (cos_value * real - sin_value * imag).astype(BF16)
        model[:, late] = (cos_value * imag + sin_value * real).astype(BF16)

    @pl.loop(0, 4)
    def _(c):
        cols = pl.ds(pl.multiple_of(c * 256, 256), 256)
        left[0:SG, cols] = dot(smooth[...], model[:, cols]).astype(BF16)
        left[SG:, cols] = dot(eu[...], model[:, cols]).astype(BF16)

    for plane in range(2):
        rows = left[:, plane * SG : plane * SG + SG]
        for c in range(2):
            value = dot(rows, smooth_t[:, c * 256 : c * 256 + 256])
            grid[plane, 2 * c] = value[:, 0:128]
            grid[plane, 2 * c + 1] = value[:, 128:256]
        grid[plane, edges] = dot(rows, ev_t[...])

    count = count_ref[0]
    lanes = lax.broadcasted_iota(jnp.int32, (TV, TV), 1)
    subs = lax.broadcasted_iota(jnp.int32, (8, TV), 0)
    rim = (lanes < 2) | (lanes >= TV - 2)
    top, bottom = subs < 2, subs >= 6

    def out_copy(t):
        return pltpu.make_async_copy(sent.at[t], residual_h.at[t], sems.at[t])

    @pl.loop(0, slots, unroll=2)
    def _(t):
        ou, ov = toff[0, t] + 1, toff[1, t] + 1
        rows = pl.ds((ou & 1) * (SG // 2) + (ou >> 1), TV)
        near, across = (ov & 1) * 2, ov >> 1
        back_turn, side_turn = (TV - across) & 127, (TV - t * 8) & 127
        tail = pl.ds(pl.multiple_of(SG + t * 8, 8), 8)
        live = t < count
        blank = jnp.zeros((TV, TV), F32)

        def pick(plane, where_rows, size):
            lane = lanes[0:size]
            middle = jnp.where(lane >= across, grid[plane, near, where_rows], grid[plane, near + 1, where_rows])
            middle = pltpu.roll(middle, back_turn, 1)
            side = pltpu.roll(grid[plane, edges, where_rows], side_turn, 1)
            return jnp.where(rim[0:size], side, middle)

        def place(plane, where_rows, value, size):
            lane = lanes[0:size]
            zero = blank[0:size]
            middle = pltpu.roll(jnp.where(rim[0:size], zero, value), across & 127, 1)
            spread[plane, near, where_rows] += jnp.where(lane >= across, middle, zero)
            spread[plane, near + 1, where_rows] += jnp.where(lane >= across, zero, middle)
            side = pltpu.roll(jnp.where(rim[0:size], value, zero), t * 8, 1)
            spread[plane, edges, where_rows] += side

        for plane in range(2):
            body = pick(plane, rows, TV)
            edge = pick(plane, tail, 8)
            body = jnp.concatenate(
                [jnp.where(top, edge, body[0:8]), body[8 : TV - 8], jnp.where(bottom, edge, body[TV - 8 :])], axis=0
            )
            value = (observed[t, plane].astype(F32) - body).astype(BF16)
            value = jnp.where(live, value, jnp.zeros_like(value))
            sent[t, plane] = value
            value = value.astype(F32)
            zero = blank[0:8]
            edge = jnp.where(top, value[0:8], jnp.where(bottom, value[TV - 8 :], zero))
            body = jnp.concatenate(
                [jnp.where(top, zero, value[0:8]), value[8 : TV - 8], jnp.where(bottom, zero, value[TV - 8 :])], axis=0
            )
            place(plane, rows, body, TV)
            place(plane, tail, edge, 8)
        out_copy(t).start()

    for plane in range(2):
        for k in range(edges + 1):
            flat[plane, :, k * 128 : k * 128 + 128] = spread[plane, k].astype(BF16)
    for plane in range(2):
        for c in range(2):
            cols = slice(c * 256, c * 256 + 256)
            value = dot(flat[plane, :, 0:SG], smooth[:, cols]) + dot(flat[plane, :, SG:], ev[:, cols])
            left[:, plane * SG + c * 256 : plane * SG + c * 256 + 256] = value.astype(BF16)
    for c in range(2):
        cols = slice(c * 256, c * 256 + 256)
        late = slice(SG + c * 256, SG + c * 256 + 256)
        ar = dot(smooth_t[...], left[0:SG, cols]) + dot(eu_t[...], left[SG:, cols])
        ai = dot(smooth_t[...], left[0:SG, late]) + dot(eu_t[...], left[SG:, late])
        sc, ss = screen[0, :, cols], screen[1, :, cols]
        model[:, cols] = (sc * ar + ss * ai).astype(BF16)
        model[:, late] = (sc * ai - ss * ar).astype(BF16)
    reduced = (
        dot(pad_t[:, 0:SG], model[:, 0:SG]) + dot(pad_t[:, SG:], model[:, SG:])
    ).astype(BF16)
    both = dot(reduced, pad[...])
    coefficient[0] = (both[0:M, 0:M] + both[M:, M:]).astype(BF16)
    coefficient[1] = (both[M:, 0:M] - both[0:M, M:]).astype(BF16)

    @pl.loop(0, slots)
    def _(t):
        out_copy(t).wait()


def backward_kernel(n, foff, soff, piece, basis, taper, out, acc, spec, half, phase):
    phase[0], phase[1] = tapered_phase(foff, taper)
    lanes = lax.broadcasted_iota(jnp.int32, (M, M), 1)
    acc[...] = jnp.zeros_like(acc)

    @pl.loop(0, n, unroll=4)
    def _(s):
        sx, sy = soff[0, s], soff[1, s]
        tile, shift = sy >> 7, sy & 127
        rows = pl.ds(sx, M)
        kept = lanes >= shift
        pc, ps = phase[0], phase[1]
        real, imag = piece[s, 0].astype(F32), piece[s, 1].astype(F32)
        blank = jnp.zeros((M, M), F32)
        values = (pc * real + ps * imag, pc * imag - ps * real)
        for plane in range(2):
            turned = pltpu.roll(values[plane], shift, 1)
            acc[plane, tile, rows] += jnp.where(kept, turned, blank)
            acc[plane, tile + 1, rows] += jnp.where(kept, blank, turned)

    acc[:, 0] += acc[:, F // M]
    acc[:, 0 : F // M, 0:M] += acc[:, 0 : F // M, F:WIDE]
    for k in range(F // M):
        spec[:, :, k * M : k * M + M] = acc[:, k, 0:F].astype(BF16)

    @pl.loop(0, 2)
    def _(c):
        cols = pl.ds(pl.multiple_of(c * 256, 256), 256)
        xr, xi = spec[0, :, cols], spec[1, :, cols]
        half[0, :, cols] = (dot(basis[0], xr) + dot(basis[1], xi)).astype(BF16)
        half[1, :, cols] = (dot(basis[0], xi) - dot(basis[1], xr)).astype(BF16)

    @pl.loop(0, 2)
    def _(c):
        cols = pl.ds(pl.multiple_of(c * 256, 256), 256)
        br, bi = basis[0, :, cols], basis[1, :, cols]
        out[0, :, cols] = (dot(half[0], br) + dot(half[1], bi)).astype(BF16)
        out[1, :, cols] = (dot(half[1], br) - dot(half[0], bi)).astype(BF16)


SMEM_SPEC = pl.BlockSpec(memory_space=pltpu.SMEM)
VMEM_SPEC = pl.BlockSpec(memory_space=pltpu.VMEM)
HBM_SPEC = pl.BlockSpec(memory_space=pltpu.HBM)
DMA = pltpu.SemaphoreType.DMA


def per_device(facets, facet_offsets, subgrid_offsets, w_terms, tile_count, tile_offsets, observed):
    n = lax.axis_size("facet")
    quads = n // 4
    soff_t = subgrid_offsets.T
    slots = observed.shape[0]
    basis = jnp.asarray(basis_table())
    real, imag = padding_table(n)
    pad = jnp.asarray(np.concatenate([real, imag], axis=1))
    pad_t = jnp.asarray(np.block([[real.T, imag.T], [-imag.T, real.T]]))
    taper = jnp.asarray(taper_square())
    smooth_np = smooth_table()
    smooth, smooth_t = jnp.asarray(smooth_np), jnp.asarray(np.ascontiguousarray(smooth_np.T))
    plain = pltpu.CompilerParams(vmem_limit_bytes=LIMIT)

    contrib = pl.pallas_call(
        functools.partial(forward_kernel, n),
        out_shape=jax.ShapeDtypeStruct((2, 2, quads, 2, M, M), BF16),
        in_specs=[HBM_SPEC] * 5,
        out_specs=VMEM_SPEC,
        scratch_shapes=[
            VMEM((2, F, F), BF16), VMEM((2, WIDE // M, WIDE, M), F32), VMEM((2, M, M), F32),
            pltpu.SMEM((1, 2), jnp.int32), pltpu.SMEM((2, n), jnp.int32),
            VMEM((2, F, F), BF16), VMEM((2, F, F), BF16), VMEM((M, M), F32), DMA((5,)),
        ],
        compiler_params=plain,
        name="forward",
    )(*[pltpu.with_memory_space_constraint(x, pltpu.HBM) for x in (facet_offsets, soff_t, facets[0], basis, taper)])

    edge_shapes = [(8 * slots, SG), (SG, 8 * slots)] * 2
    summed, screen, *sides = pl.pallas_call(
        functools.partial(reduce_kernel, n, slots),
        out_shape=(
            jax.ShapeDtypeStruct((2, M, M), F32), jax.ShapeDtypeStruct((2, SG, SG), F32),
            *[jax.ShapeDtypeStruct(shape, BF16) for shape in edge_shapes],
        ),
        in_specs=[SMEM_SPEC, SMEM_SPEC, VMEM_SPEC],
        out_specs=(VMEM_SPEC,) * 6,
        scratch_shapes=[VMEM((2, quads, 2, M, M), BF16)]
        + [VMEM((quads, 2, M, M), BF16)] * 4
        + [DMA((2, quads))] * 2
        + [DMA((quads,))] * 4,
        compiler_params=pltpu.CompilerParams(
            vmem_limit_bytes=LIMIT, collective_id=0, has_side_effects=True
        ),
        name="reduce",
    )(w_terms, tile_offsets.T, contrib)

    deep = SG + 8 * slots
    residual, coefficient = pl.pallas_call(
        functools.partial(subgrid_kernel, slots),
        out_shape=(
            jax.ShapeDtypeStruct((slots, 2, TV, TV), BF16),
            jax.ShapeDtypeStruct((2, M, M), BF16),
        ),
        in_specs=[SMEM_SPEC] * 2 + [VMEM_SPEC] * 11,
        out_specs=(HBM_SPEC, VMEM_SPEC),
        scratch_shapes=[
            VMEM((SG, 2 * M), BF16), VMEM((SG, 2 * SG), BF16), VMEM((deep, 2 * SG), BF16),
            VMEM((2, deep // 128, deep, 128), F32), VMEM((2, deep // 128, deep, 128), F32),
            VMEM((2, deep, deep), BF16), VMEM((slots, 2, TV, TV), BF16), DMA((slots,)),
        ],
        compiler_params=plain,
        name="subgrid",
    )(tile_count, tile_offsets.T, summed, screen, *sides, pad, pad_t, smooth, smooth_t, observed)

    piece = pl.pallas_call(
        functools.partial(gather_kernel, n),
        out_shape=jax.ShapeDtypeStruct((n, 2, M, M), BF16),
        in_specs=[VMEM_SPEC],
        out_specs=VMEM_SPEC,
        scratch_shapes=[DMA((2, quads))] * 2 + [DMA((quads,))] * 4 + [DMA],
        compiler_params=pltpu.CompilerParams(
            vmem_limit_bytes=LIMIT, collective_id=1, has_side_effects=True
        ),
        name="gather",
    )(coefficient)

    update = pl.pallas_call(
        functools.partial(backward_kernel, n),
        out_shape=jax.ShapeDtypeStruct((2, F, F), BF16),
        in_specs=[SMEM_SPEC, SMEM_SPEC, VMEM_SPEC, VMEM_SPEC, VMEM_SPEC],
        out_specs=VMEM_SPEC,
        scratch_shapes=[
            VMEM((2, WIDE // M, WIDE, M), F32), VMEM((2, F, F), BF16), VMEM((2, F, F), BF16),
            VMEM((2, M, M), F32),
        ],
        compiler_params=plain,
        name="backward",
    )(facet_offsets, soff_t, piece, basis, taper)
    return (residual, update[None])


def solution(mesh):
    placed = (
        P(("groups", "facet"), None, None, None),
        P(("groups", "facet"), None),
        P("groups", None),
        P(("groups", "facet")),
        P(("groups", "facet")),
        P(("groups", "facet"), None),
        P(("groups", "facet"), None, None, None),
    )
    return jax.shard_map(
        per_device,
        mesh=mesh,
        in_specs=placed,
        out_specs=(
            P(("groups", "facet"), None, None, None),
            P(("groups", "facet"), None, None, None),
        ),
        check_vma=False,
    )
```

```python
import functools
import math

import jax
import jax.numpy as jnp
import ml_dtypes
import numpy as np
from jax import lax
from jax.experimental import pallas as pl
from jax.experimental.pallas import tpu as pltpu
from jax.sharding import PartitionSpec as P

F = 512
M = 128
SG = 512
TV = 128
WIDE = F + M
GROUP = 4

BF16 = jnp.bfloat16
F32 = jnp.float32
TWO_PI = 2.0 * math.pi
MESH = pl.DeviceIdType.MESH
VMEM = pltpu.VMEM
LIMIT = 48 * 1024 * 1024


def basis_table():
    index = np.arange(F)
    angle = -TWO_PI * (index[:, None] * index[None, :] % F) / F
    scale = 1.0 / math.sqrt(F)
    return np.stack([np.cos(angle) * scale, np.sin(angle) * scale]).astype(ml_dtypes.bfloat16)


def padding_table(facet_count):
    angle = TWO_PI * (np.arange(SG)[:, None] * np.arange(M)[None, :] % SG) / SG
    scale = (M * math.sqrt(facet_count)) ** (-0.5)
    return np.stack([np.cos(angle) * scale, np.sin(angle) * scale]).astype(ml_dtypes.bfloat16)


def taper_square():
    taper = 0.6 + 0.4 * np.sin(math.pi * (np.arange(M) + 0.5) / M)
    return (taper[:, None] * taper[None, :]).astype(np.float32)


def dot(left, right):
    return jnp.dot(left, right, preferred_element_type=F32)


def cos_sin_turns(turns):
    quarter = jnp.floor(turns * 4.0 + 0.5)
    y = (turns - quarter * 0.25) * TWO_PI
    y2 = y * y
    sine = y * (1.0 + y2 * (-1.0 / 6 + y2 * (1.0 / 120 + y2 * (-1.0 / 5040 + y2 * (1.0 / 362880)))))
    cosine = 1.0 + y2 * (
        -0.5 + y2 * (1.0 / 24 + y2 * (-1.0 / 720 + y2 * (1.0 / 40320 - y2 * (1.0 / 3628800))))
    )
    which = quarter.astype(jnp.int32) & 3
    odd = (which & 1) == 1
    first = jnp.where(odd, sine, cosine)
    second = jnp.where(odd, cosine, sine)
    cos_value = jnp.where((which == 1) | (which == 2), -first, first)
    sin_value = jnp.where(which >= 2, -second, second)
    return cos_value, sin_value


def tapered_phase(offset_ref, taper_ref):
    rows = lax.broadcasted_iota(jnp.int32, (M, M), 0)
    columns = lax.broadcasted_iota(jnp.int32, (M, M), 1)
    total = (rows * offset_ref[0, 0] + columns * offset_ref[0, 1]) & (F - 1)
    cos_value, sin_value = cos_sin_turns(total.astype(F32) * (1.0 / F))
    taper = taper_ref[...]
    return cos_value * taper, sin_value * taper


def forward_kernel(
    n, foff_h, soff_h, facet_h, basis_h, taper_h, out,
    half, spec, phase, foff, soff, facet, basis, taper, sems
):
    pairs = ((facet_h, facet), (basis_h, basis), (taper_h, taper), (foff_h, foff), (soff_h, soff))
    copies = [pltpu.make_async_copy(src, dst, sems.at[i]) for i, (src, dst) in enumerate(pairs)]
    for copy in copies:
        copy.start()
    for copy in copies:
        copy.wait()
    phase[0], phase[1] = tapered_phase(foff, taper)
    lanes = lax.broadcasted_iota(jnp.int32, (M, M), 1)

    @pl.loop(0, 2)
    def _(c):
        cols = pl.ds(pl.multiple_of(c * 256, 256), 256)
        br, bi = basis[0, :, cols], basis[1, :, cols]
        half[0, :, cols] = (dot(facet[0], br) - dot(facet[1], bi)).astype(BF16)
        half[1, :, cols] = (dot(facet[0], bi) + dot(facet[1], br)).astype(BF16)

    @pl.loop(0, 2)
    def _(c):
        cols = pl.ds(pl.multiple_of(c * 256, 256), 256)
        hr, hi = half[0, :, cols], half[1, :, cols]
        real = dot(basis[0], hr) - dot(basis[1], hi)
        imag = dot(basis[0], hi) + dot(basis[1], hr)
        for side in range(2):
            part = slice(side * M, side * M + M)
            spec[0, c * 2 + side, 0:F] = real[:, part]
            spec[1, c * 2 + side, 0:F] = imag[:, part]

    spec[:, 0 : F // M, F:WIDE] = spec[:, 0 : F // M, 0:M]
    spec[:, F // M] = spec[:, 0]

    @pl.loop(0, n, unroll=4)
    def _(s):
        sx, sy = soff[0, s], soff[1, s]
        tile, offset = sy >> 7, sy & 127
        shift = (M - offset) & 127
        kept = lanes < M - offset
        rows = pl.ds(sx, M)

        def window(plane):
            low = pltpu.roll(spec[plane, tile, rows], shift, 1)
            high = pltpu.roll(spec[plane, tile + 1, rows], shift, 1)
            return jnp.where(kept, low, high)

        real, imag = window(0), window(1)
        pc, ps = phase[0], phase[1]
        out[s & 1, (s >> 1) & 1, s >> 2, 0] = (pc * real - ps * imag).astype(BF16)
        out[s & 1, (s >> 1) & 1, s >> 2, 1] = (pc * imag + ps * real).astype(BF16)


def place(n):
    me = lax.axis_index("facet")
    quads = n // 4
    far_first = [1 + (t + quads // 2 - 1) % (quads - 1) for t in range(quads - 1)]
    return quads, me // 4, lax.rem(me // 2, 2), lax.rem(me, 2), far_first


def index(quad, middle, core):
    return quad * 4 + middle * 2 + core


def greet(peers):
    barrier = pltpu.get_barrier_semaphore()
    for peer in peers:
        pl.semaphore_signal(barrier, inc=1, device_id={"facet": peer}, device_id_type=MESH)
    pl.semaphore_wait(barrier, len(peers))


def send(src, dst, send_sem, recv_sem, peer):
    return pltpu.make_async_remote_copy(
        src_ref=src, dst_ref=dst, send_sem=send_sem, recv_sem=recv_sem,
        device_id={"facet": peer}, device_id_type=MESH,
    )


def fill_screen(w_value, screen):
    @pl.loop(0, 4)
    def _(c):
        rows = pl.ds(pl.multiple_of(c * 128, 128), 128)
        u = (lax.broadcasted_iota(jnp.int32, (128, SG), 0) + (c * 128 - 256)).astype(F32)
        v = (lax.broadcasted_iota(jnp.int32, (128, SG), 1) - 256).astype(F32)
        radius = (u * u + v * v) * (1.0 / (SG * SG))
        cos_value, sin_value = cos_sin_turns(w_value * (jnp.sqrt(1.0 + radius) - 1.0))
        screen[0, rows, :] = cos_value
        screen[1, rows, :] = sin_value


def reduce_kernel(
    n, slots, w_ref, toff, contrib, smooth, smooth_t, summed, screen, wide, wide_t, near, pair, mid, quad_sum, far,
    near_s, near_r, mid_s, mid_r, far_s, far_r
):
    quads, quad, middle, core, far_first = place(n)
    other = 1 - middle
    sibling, beside = index(quad, middle, 1 - core), index(quad, other, core)
    away = [lax.rem(quad + k, quads) for k in far_first]
    order = away + [quad]
    greet([index(j, middle, core) for j in away] + [beside, sibling])

    def near_copy(half, j):
        return send(contrib.at[1 - core, half, j], near.at[half, j], near_s.at[half, j], near_r.at[half, j], sibling)

    def mid_copy(j):
        return send(pair.at[j], mid.at[j], mid_s.at[j], mid_r.at[j], beside)

    def far_copy(j, slot):
        return send(quad_sum.at[j], far.at[slot], far_s.at[j], far_r.at[slot], index(j, middle, core))

    def near_sum(half, j):
        return contrib[core, half, j].astype(F32) + near[half, j].astype(F32)

    for half in (other, middle):
        for j in order:
            near_copy(half, j).start()
    for j in order:
        near_copy(other, j).wait_recv()
        pair[j] = near_sum(other, j).astype(BF16)
        mid_copy(j).start()
    for j in away:
        near_copy(middle, j).wait_recv()
        mid_copy(j).wait_recv()
        quad_sum[j] = (near_sum(middle, j) + mid[j].astype(F32)).astype(BF16)
        far_copy(j, quad).start()
    fill_screen(w_ref[0], screen)
    fill_rows(slots, toff, smooth, smooth_t, wide, wide_t)
    near_copy(middle, quad).wait_recv()
    mid_copy(quad).wait_recv()
    total = near_sum(middle, quad) + mid[quad].astype(F32)
    for j in reversed(away):
        far_copy(j, j).wait_recv()
        total = total + far[j].astype(F32)
    summed[...] = total
    for j in order:
        near_copy(other, j).wait_send()
        near_copy(middle, j).wait_send()
        mid_copy(j).wait_send()
    for j in away:
        far_copy(j, quad).wait_send()


def gather_kernel(n, mine, out, near_s, near_r, mid_s, mid_r, far_s, far_r, local):
    quads, quad, middle, core, far_first = place(n)
    other = 1 - middle
    me = index(quad, middle, core)
    sibling, beside = index(quad, middle, 1 - core), index(quad, other, core)
    away = [lax.rem(quad + k, quads) for k in far_first]
    back = [lax.rem(quad + quads - k, quads) for k in far_first]
    greet([index(j, middle, core) for j in away] + [beside, sibling])

    def far_copy(j, slot):
        return send(
            mine, out.at[index(slot, middle, core)], far_s.at[j], far_r.at[slot], index(j, middle, core)
        )

    def mid_copy(j, half):
        piece = out.at[index(j, half, core)]
        return send(piece, piece, mid_s.at[j], mid_r.at[j], beside)

    def near_copy(half, j, side):
        piece = out.at[index(j, half, side)]
        return send(piece, piece, near_s.at[half, j], near_r.at[half, j], sibling)

    for j in away:
        far_copy(j, quad).start()
    mid_own = send(mine, out.at[me], mid_s.at[quad], mid_r.at[quad], beside)
    mid_own.start()
    near_own = send(mine, out.at[me], near_s.at[middle, quad], near_r.at[middle, quad], sibling)
    near_own.start()
    own = pltpu.make_async_copy(mine, out.at[me], local)
    own.start()
    for j in back:
        far_copy(j, j).wait_recv()
        mid_copy(j, middle).start()
        near_copy(middle, j, core).start()
    for j in [quad] + back:
        mid_copy(j, other).wait_recv()
        near_copy(other, j, core).start()
    for half in (middle, other):
        for j in [quad] + back:
            near_copy(half, j, 1 - core).wait_recv()
    for j in away:
        far_copy(j, quad).wait_send()
        mid_copy(j, middle).wait_send()
        near_copy(middle, j, core).wait_send()
        near_copy(other, j, core).wait_send()
    near_copy(other, quad, core).wait_send()
    mid_own.wait_send()
    near_own.wait_send()
    own.wait()


def tap_values():
    taps = np.arange(5, dtype=np.float32)
    value = 0.75 * np.exp(-(taps / 1.5) * (taps / 1.5))
    return [float(x) for x in value.astype(ml_dtypes.bfloat16).astype(np.float32)]


def smooth_table():
    order = np.concatenate([np.arange(0, SG, 2), np.arange(1, SG, 2)])
    distance = np.abs(np.arange(SG)[None, :] - order[:, None])
    taps = np.array(tap_values() + [0.0], np.float32)
    return taps[np.minimum(distance, 5)].astype(ml_dtypes.bfloat16)


def kernel_table():
    distance = np.abs(np.arange(2 * TV)[None, :] - 2 * np.arange(TV)[:, None] - 1)
    taps = np.array(tap_values() + [0.0], np.float32)
    return taps[np.minimum(distance, 5)].astype(ml_dtypes.bfloat16)


def edge_values(position, offset, spot):
    i = spot & 7
    slot = jnp.where(i < 2, i, i + (TV - 8))
    distance = jnp.abs(position - offset - 2 * slot - 1)
    value = jnp.zeros(distance.shape, F32)
    for step, tap in enumerate(tap_values()):
        value = jnp.where(distance == step, tap, value)
    inside = (position >= offset) & (position < offset + 2 * TV) & ((i < 2) | (i >= 6))
    return jnp.where(inside, value, 0.0).astype(BF16)


def fill_rows(slots, toff, smooth, smooth_t, wide, wide_t):
    wide[0:SG] = smooth[...]
    wide_t[:, 0:SG] = smooth_t[...]

    @pl.loop(0, slots // 2)
    def _(c):
        spot = lax.broadcasted_iota(jnp.int32, (16, SG), 0)
        lane = lax.broadcasted_iota(jnp.int32, (16, SG), 1)
        offset = jnp.where(spot < 8, toff[0, 2 * c], toff[0, 2 * c + 1])
        wide[pl.ds(pl.multiple_of(SG + c * 16, 16), 16), :] = edge_values(lane, offset, spot)

    lane = lax.broadcasted_iota(jnp.int32, (1, 8 * slots), 1)
    offset = jnp.zeros_like(lane)
    for t in range(slots):
        offset = jnp.where(lane >> 3 == t, toff[0, t], offset)

    @pl.loop(0, SG // 64)
    def _(c):
        position = lax.broadcasted_iota(jnp.int32, (64, 8 * slots), 0) + c * 64
        spot = lax.broadcasted_iota(jnp.int32, (64, 8 * slots), 1)
        wide_t[pl.ds(pl.multiple_of(c * 64, 64), 64), SG:] = edge_values(position, offset, spot)


def subgrid_kernel(
    slots, count_ref, toff, summed, screen, wide, wide_t, pad, pad_t, ker, ker_t, observed,
    residual_h, coefficient, inner, model, grid, spread, sent, sems
):
    groups = slots // GROUP
    sr, si = summed[0], summed[1]
    stacked = jnp.concatenate(
        [jnp.concatenate([sr, si], axis=1), jnp.concatenate([-si, sr], axis=1)], axis=0
    ).astype(BF16)
    inner[...] = dot(pad[...], stacked).astype(BF16)

    for c in range(2):
        cols = slice(c * 256, c * 256 + 256)
        late = slice(SG + c * 256, SG + c * 256 + 256)
        real, imag = dot(inner[...], pad_t[:, cols]), dot(inner[...], pad_t[:, late])
        cos_value, sin_value = screen[0, :, cols], screen[1, :, cols]
        model[:, cols] = (cos_value * real - sin_value * imag).astype(BF16)
        model[:, late] = (cos_value * imag + sin_value * real).astype(BF16)

    for plane in range(2):
        for c in range(2):
            start = plane * SG + c * 256
            value = dot(wide[...], model[:, start : start + 256])
            for side in range(2):
                grid[plane, c * 2 + side] = value[:, side * 128 : side * 128 + 128]
                spread[plane, c * 2 + side] = jnp.zeros(spread.shape[2:], F32)

    count = count_ref[0]
    lanes = lax.broadcasted_iota(jnp.int32, (TV, TV), 1)
    subs = lax.broadcasted_iota(jnp.int32, (8, TV), 0)
    top, bottom = subs < 2, subs >= 6

    def out_copy(step):
        tiles = pl.ds(step * GROUP, GROUP)
        return pltpu.make_async_copy(sent.at[tiles], residual_h.at[tiles], sems.at[step])

    filled = (count + GROUP - 1) // GROUP

    @pl.loop(0, filled)
    def _(step):
        slot = [step * GROUP + g for g in range(GROUP)]
        spots, left = [], []
        for t in slot:
            ou, ov = toff[0, t] + 1, toff[1, t]
            rows = pl.ds((ou & 1) * (SG // 2) + (ou >> 1), TV)
            tail = pl.ds(pl.multiple_of(SG + t * 8, 8), 8)
            first, turn = ov >> 7, ov & 127
            tiles = (first, first + 1, jnp.minimum(first + 2, SG // 128 - 1))
            spots.append((rows, tail, tiles, turn))

            def pick(plane, where_rows, size):
                keep = lanes[0:size] >= turn
                part = [grid[plane, k, where_rows] for k in tiles]
                both = [jnp.where(keep, part[k], part[k + 1]) for k in range(2)]
                return jnp.concatenate([pltpu.roll(x, (TV - turn) & 127, 1) for x in both], axis=1)

            for plane in range(2):
                body, edge = pick(plane, rows, TV), pick(plane, tail, 8)
                wide_top = jnp.concatenate([top, top], axis=1)
                wide_bottom = jnp.concatenate([bottom, bottom], axis=1)
                left.append(
                    jnp.concatenate(
                        [
                            jnp.where(wide_top, edge, body[0:8]), body[8 : TV - 8],
                            jnp.where(wide_bottom, edge, body[TV - 8 :]),
                        ],
                        axis=0,
                    ).astype(BF16)
                )
        rest = []
        for g, t in enumerate(slot):
            for plane in range(2):
                predicted = dot(left[g * 2 + plane], ker_t[...])
                value = (observed[t, plane].astype(F32) - predicted).astype(BF16)
                rest.append(jnp.where(t < count, value, jnp.zeros_like(value)))
                sent[t, plane] = rest[-1]
        out_copy(step).start()
        back = [dot(value, ker[...]).astype(BF16).astype(F32) for value in rest]
        for g in range(GROUP):
            rows, tail, tiles, turn = spots[g]
            keep = lanes >= turn
            for plane in range(2):
                value = back[g * 2 + plane]
                one, two = pltpu.roll(value[:, 0:128], turn, 1), pltpu.roll(value[:, 128:], turn, 1)
                blank = jnp.zeros((TV, TV), F32)
                parts = (jnp.where(keep, one, blank), jnp.where(keep, two, one), jnp.where(keep, blank, two))
                for tile, part in zip(tiles, parts):
                    zero = blank[0:8]
                    edge = jnp.where(top, part[0:8], jnp.where(bottom, part[TV - 8 :], zero))
                    body = jnp.concatenate(
                        [jnp.where(top, zero, part[0:8]), part[8 : TV - 8], jnp.where(bottom, zero, part[TV - 8 :])],
                        axis=0,
                    )
                    spread[plane, tile, rows] += body
                    spread[plane, tile, tail] += edge

    @pl.loop(filled, groups)
    def _(step):
        for g in range(GROUP):
            sent[step * GROUP + g] = jnp.zeros(sent.shape[1:], BF16)
        out_copy(step).start()

    for c in range(2):
        cols = slice(c * 256, c * 256 + 256)
        late = slice(SG + c * 256, SG + c * 256 + 256)
        ar, ai = [
            dot(wide_t[...], jnp.concatenate([spread[p, 2 * c], spread[p, 2 * c + 1]], axis=1).astype(BF16))
            for p in range(2)
        ]
        sc, ss = screen[0, :, cols], screen[1, :, cols]
        model[:, cols] = (sc * ar + ss * ai).astype(BF16)
        model[:, late] = (sc * ai - ss * ar).astype(BF16)
    reduced = (
        dot(pad_t[:, 0:SG], model[:, 0:SG]) + dot(pad_t[:, SG:], model[:, SG:])
    ).astype(BF16)
    both = dot(reduced, pad[...])
    coefficient[0] = (both[0:M, 0:M] + both[M:, M:]).astype(BF16)
    coefficient[1] = (both[M:, 0:M] - both[0:M, M:]).astype(BF16)

    @pl.loop(0, groups)
    def _(step):
        out_copy(step).wait()


def backward_kernel(n, foff, soff, piece, basis, taper, out, acc, spec, half, phase):
    phase[0], phase[1] = tapered_phase(foff, taper)
    lanes = lax.broadcasted_iota(jnp.int32, (M, M), 1)
    acc[...] = jnp.zeros_like(acc)

    @pl.loop(0, n, unroll=4)
    def _(s):
        sx, sy = soff[0, s], soff[1, s]
        tile, shift = sy >> 7, sy & 127
        rows = pl.ds(sx, M)
        kept = lanes >= shift
        pc, ps = phase[0], phase[1]
        real, imag = piece[s, 0].astype(F32), piece[s, 1].astype(F32)
        blank = jnp.zeros((M, M), F32)
        values = (pc * real + ps * imag, pc * imag - ps * real)
        for plane in range(2):
            turned = pltpu.roll(values[plane], shift, 1)
            acc[plane, tile, rows] += jnp.where(kept, turned, blank)
            acc[plane, tile + 1, rows] += jnp.where(kept, blank, turned)

    acc[:, 0] += acc[:, F // M]
    acc[:, 0 : F // M, 0:M] += acc[:, 0 : F // M, F:WIDE]
    for k in range(F // M):
        spec[:, :, k * M : k * M + M] = acc[:, k, 0:F].astype(BF16)

    @pl.loop(0, 2)
    def _(c):
        cols = pl.ds(pl.multiple_of(c * 256, 256), 256)
        xr, xi = spec[0, :, cols], spec[1, :, cols]
        half[0, :, cols] = (dot(basis[0], xr) + dot(basis[1], xi)).astype(BF16)
        half[1, :, cols] = (dot(basis[0], xi) - dot(basis[1], xr)).astype(BF16)

    @pl.loop(0, 2)
    def _(c):
        cols = pl.ds(pl.multiple_of(c * 256, 256), 256)
        br, bi = basis[0, :, cols], basis[1, :, cols]
        out[0, :, cols] = (dot(half[0], br) + dot(half[1], bi)).astype(BF16)
        out[1, :, cols] = (dot(half[1], br) - dot(half[0], bi)).astype(BF16)


SMEM_SPEC = pl.BlockSpec(memory_space=pltpu.SMEM)
VMEM_SPEC = pl.BlockSpec(memory_space=pltpu.VMEM)
HBM_SPEC = pl.BlockSpec(memory_space=pltpu.HBM)
DMA = pltpu.SemaphoreType.DMA


def per_device(facets, facet_offsets, subgrid_offsets, w_terms, tile_count, tile_offsets, observed):
    n = lax.axis_size("facet")
    quads = n // 4
    soff_t = subgrid_offsets.T
    slots = observed.shape[0]
    basis = jnp.asarray(basis_table())
    real, imag = padding_table(n)
    pad = jnp.asarray(np.concatenate([real, imag], axis=1))
    pad_t = jnp.asarray(np.block([[real.T, imag.T], [-imag.T, real.T]]))
    taper = jnp.asarray(taper_square())
    smooth_np = smooth_table()
    smooth, smooth_t = jnp.asarray(smooth_np), jnp.asarray(np.ascontiguousarray(smooth_np.T))
    ker_np = kernel_table()
    ker, ker_t = jnp.asarray(ker_np), jnp.asarray(np.ascontiguousarray(ker_np.T))
    plain = pltpu.CompilerParams(vmem_limit_bytes=LIMIT)

    contrib = pl.pallas_call(
        functools.partial(forward_kernel, n),
        out_shape=jax.ShapeDtypeStruct((2, 2, quads, 2, M, M), BF16),
        in_specs=[HBM_SPEC] * 5,
        out_specs=VMEM_SPEC,
        scratch_shapes=[
            VMEM((2, F, F), BF16), VMEM((2, WIDE // M, WIDE, M), F32), VMEM((2, M, M), F32),
            pltpu.SMEM((1, 2), jnp.int32), pltpu.SMEM((2, n), jnp.int32),
            VMEM((2, F, F), BF16), VMEM((2, F, F), BF16), VMEM((M, M), F32), DMA((5,)),
        ],
        compiler_params=plain,
        name="forward",
    )(*[pltpu.with_memory_space_constraint(x, pltpu.HBM) for x in (facet_offsets, soff_t, facets[0], basis, taper)])

    deep = SG + 8 * slots
    summed, screen, wide, wide_t = pl.pallas_call(
        functools.partial(reduce_kernel, n, slots),
        out_shape=(
            jax.ShapeDtypeStruct((2, M, M), F32), jax.ShapeDtypeStruct((2, SG, SG), F32),
            jax.ShapeDtypeStruct((deep, SG), BF16), jax.ShapeDtypeStruct((SG, deep), BF16),
        ),
        in_specs=[SMEM_SPEC, SMEM_SPEC, VMEM_SPEC, VMEM_SPEC, VMEM_SPEC],
        out_specs=(VMEM_SPEC,) * 4,
        scratch_shapes=[VMEM((2, quads, 2, M, M), BF16)]
        + [VMEM((quads, 2, M, M), BF16)] * 4
        + [DMA((2, quads))] * 2
        + [DMA((quads,))] * 4,
        compiler_params=pltpu.CompilerParams(
            vmem_limit_bytes=LIMIT, collective_id=0, has_side_effects=True
        ),
        name="reduce",
    )(w_terms, tile_offsets.T, contrib, smooth, smooth_t)

    residual, coefficient = pl.pallas_call(
        functools.partial(subgrid_kernel, slots),
        out_shape=(
            jax.ShapeDtypeStruct((slots, 2, TV, TV), BF16),
            jax.ShapeDtypeStruct((2, M, M), BF16),
        ),
        in_specs=[SMEM_SPEC] * 2 + [VMEM_SPEC] * 9,
        out_specs=(HBM_SPEC, VMEM_SPEC),
        scratch_shapes=[
            VMEM((SG, 2 * M), BF16), VMEM((SG, 2 * SG), BF16),
            VMEM((2, SG // 128, deep, 128), F32), VMEM((2, SG // 128, deep, 128), F32),
            VMEM((slots, 2, TV, TV), BF16), DMA((slots // GROUP,)),
        ],
        compiler_params=plain,
        name="subgrid",
    )(tile_count, tile_offsets.T, summed, screen, wide, wide_t, pad, pad_t, ker, ker_t, observed)

    piece = pl.pallas_call(
        functools.partial(gather_kernel, n),
        out_shape=jax.ShapeDtypeStruct((n, 2, M, M), BF16),
        in_specs=[VMEM_SPEC],
        out_specs=VMEM_SPEC,
        scratch_shapes=[DMA((2, quads))] * 2 + [DMA((quads,))] * 4 + [DMA],
        compiler_params=pltpu.CompilerParams(
            vmem_limit_bytes=LIMIT, collective_id=1, has_side_effects=True
        ),
        name="gather",
    )(coefficient)

    update = pl.pallas_call(
        functools.partial(backward_kernel, n),
        out_shape=jax.ShapeDtypeStruct((2, F, F), BF16),
        in_specs=[SMEM_SPEC, SMEM_SPEC, VMEM_SPEC, VMEM_SPEC, VMEM_SPEC],
        out_specs=VMEM_SPEC,
        scratch_shapes=[
            VMEM((2, WIDE // M, WIDE, M), F32), VMEM((2, F, F), BF16), VMEM((2, F, F), BF16),
            VMEM((2, M, M), F32),
        ],
        compiler_params=plain,
        name="backward",
    )(facet_offsets, soff_t, piece, basis, taper)
    return (residual, update[None])


def solution(mesh):
    placed = (
        P(("groups", "facet"), None, None, None),
        P(("groups", "facet"), None),
        P("groups", None),
        P(("groups", "facet")),
        P(("groups", "facet")),
        P(("groups", "facet"), None),
        P(("groups", "facet"), None, None, None),
    )
    return jax.shard_map(
        per_device,
        mesh=mesh,
        in_specs=placed,
        out_specs=(
            P(("groups", "facet"), None, None, None),
            P(("groups", "facet"), None, None, None),
        ),
        check_vma=False,
    )
```

```python
import functools
import math

import jax
import jax.numpy as jnp
import ml_dtypes
import numpy as np
from jax import lax
from jax.experimental import pallas as pl
from jax.experimental.pallas import tpu as pltpu
from jax.sharding import PartitionSpec as P

F = 512
M = 128
SG = 512
TV = 128
WIDE = F + M
GROUP = 4

BF16 = jnp.bfloat16
F32 = jnp.float32
TWO_PI = 2.0 * math.pi
MESH = pl.DeviceIdType.MESH
VMEM = pltpu.VMEM
LIMIT = 48 * 1024 * 1024


def basis_table():
    index = np.arange(F)
    angle = -TWO_PI * (index[:, None] * index[None, :] % F) / F
    scale = 1.0 / math.sqrt(F)
    return np.stack([np.cos(angle) * scale, np.sin(angle) * scale]).astype(ml_dtypes.bfloat16)


def padding_table(facet_count):
    angle = TWO_PI * (np.arange(SG)[:, None] * np.arange(M)[None, :] % SG) / SG
    scale = (M * math.sqrt(facet_count)) ** (-0.5)
    return np.stack([np.cos(angle) * scale, np.sin(angle) * scale]).astype(ml_dtypes.bfloat16)


def taper_square():
    taper = 0.6 + 0.4 * np.sin(math.pi * (np.arange(M) + 0.5) / M)
    return (taper[:, None] * taper[None, :]).astype(np.float32)


def dot(left, right):
    return jnp.dot(left, right, preferred_element_type=F32)


def cos_sin_turns(turns):
    quarter = jnp.floor(turns * 4.0 + 0.5)
    y = (turns - quarter * 0.25) * TWO_PI
    y2 = y * y
    sine = y * (1.0 + y2 * (-1.0 / 6 + y2 * (1.0 / 120 + y2 * (-1.0 / 5040 + y2 * (1.0 / 362880)))))
    cosine = 1.0 + y2 * (
        -0.5 + y2 * (1.0 / 24 + y2 * (-1.0 / 720 + y2 * (1.0 / 40320 - y2 * (1.0 / 3628800))))
    )
    which = quarter.astype(jnp.int32) & 3
    odd = (which & 1) == 1
    first = jnp.where(odd, sine, cosine)
    second = jnp.where(odd, cosine, sine)
    cos_value = jnp.where((which == 1) | (which == 2), -first, first)
    sin_value = jnp.where(which >= 2, -second, second)
    return cos_value, sin_value


def tapered_phase(offset_ref, taper_ref):
    rows = lax.broadcasted_iota(jnp.int32, (M, M), 0)
    columns = lax.broadcasted_iota(jnp.int32, (M, M), 1)
    total = (rows * offset_ref[0, 0] + columns * offset_ref[0, 1]) & (F - 1)
    cos_value, sin_value = cos_sin_turns(total.astype(F32) * (1.0 / F))
    taper = taper_ref[...]
    return cos_value * taper, sin_value * taper


def place(n):
    me = lax.axis_index("facet")
    quads = n // 4
    far_first = [1 + (t + quads // 2 - 1) % (quads - 1) for t in range(quads - 1)]
    return quads, me // 4, lax.rem(me // 2, 2), lax.rem(me, 2), far_first


def index(quad, middle, core):
    return quad * 4 + middle * 2 + core


def greet(peers):
    barrier = pltpu.get_barrier_semaphore()
    for peer in peers:
        pl.semaphore_signal(barrier, inc=1, device_id={"facet": peer}, device_id_type=MESH)
    pl.semaphore_wait(barrier, len(peers))


def send(src, dst, send_sem, recv_sem, peer):
    return pltpu.make_async_remote_copy(
        src_ref=src, dst_ref=dst, send_sem=send_sem, recv_sem=recv_sem,
        device_id={"facet": peer}, device_id_type=MESH,
    )


def fill_screen(w_value, screen):
    @pl.loop(0, 4)
    def _(c):
        rows = pl.ds(pl.multiple_of(c * 128, 128), 128)
        u = (lax.broadcasted_iota(jnp.int32, (128, SG), 0) + (c * 128 - 256)).astype(F32)
        v = (lax.broadcasted_iota(jnp.int32, (128, SG), 1) - 256).astype(F32)
        radius = (u * u + v * v) * (1.0 / (SG * SG))
        cos_value, sin_value = cos_sin_turns(w_value * (jnp.sqrt(1.0 + radius) - 1.0))
        screen[0, rows, :] = cos_value
        screen[1, rows, :] = sin_value


def gather_kernel(n, mine, out, near_s, near_r, mid_s, mid_r, far_s, far_r, local):
    quads, quad, middle, core, far_first = place(n)
    other = 1 - middle
    me = index(quad, middle, core)
    sibling, beside = index(quad, middle, 1 - core), index(quad, other, core)
    away = [lax.rem(quad + k, quads) for k in far_first]
    back = [lax.rem(quad + quads - k, quads) for k in far_first]
    greet([index(j, middle, core) for j in away] + [beside, sibling])

    def far_copy(j, slot):
        return send(
            mine, out.at[index(slot, middle, core)], far_s.at[j], far_r.at[slot], index(j, middle, core)
        )

    def mid_copy(j, half):
        piece = out.at[index(j, half, core)]
        return send(piece, piece, mid_s.at[j], mid_r.at[j], beside)

    def near_copy(half, j, side):
        piece = out.at[index(j, half, side)]
        return send(piece, piece, near_s.at[half, j], near_r.at[half, j], sibling)

    for j in away:
        far_copy(j, quad).start()
    mid_own = send(mine, out.at[me], mid_s.at[quad], mid_r.at[quad], beside)
    mid_own.start()
    near_own = send(mine, out.at[me], near_s.at[middle, quad], near_r.at[middle, quad], sibling)
    near_own.start()
    own = pltpu.make_async_copy(mine, out.at[me], local)
    own.start()
    for j in back:
        far_copy(j, j).wait_recv()
        mid_copy(j, middle).start()
        near_copy(middle, j, core).start()
    for j in [quad] + back:
        mid_copy(j, other).wait_recv()
        near_copy(other, j, core).start()
    for half in (middle, other):
        for j in [quad] + back:
            near_copy(half, j, 1 - core).wait_recv()
    for j in away:
        far_copy(j, quad).wait_send()
        mid_copy(j, middle).wait_send()
        near_copy(middle, j, core).wait_send()
        near_copy(other, j, core).wait_send()
    near_copy(other, quad, core).wait_send()
    mid_own.wait_send()
    near_own.wait_send()
    own.wait()


def tap_values():
    taps = np.arange(5, dtype=np.float32)
    value = 0.75 * np.exp(-(taps / 1.5) * (taps / 1.5))
    return [float(x) for x in value.astype(ml_dtypes.bfloat16).astype(np.float32)]


def smooth_table():
    order = np.concatenate([np.arange(0, SG, 2), np.arange(1, SG, 2)])
    distance = np.abs(np.arange(SG)[None, :] - order[:, None])
    taps = np.array(tap_values() + [0.0], np.float32)
    return taps[np.minimum(distance, 5)].astype(ml_dtypes.bfloat16)


def kernel_table():
    distance = np.abs(np.arange(2 * TV)[None, :] - 2 * np.arange(TV)[:, None] - 1)
    taps = np.array(tap_values() + [0.0], np.float32)
    return taps[np.minimum(distance, 5)].astype(ml_dtypes.bfloat16)


def edge_values(position, offset, spot):
    i = spot & 7
    slot = jnp.where(i < 2, i, i + (TV - 8))
    distance = jnp.abs(position - offset - 2 * slot - 1)
    value = jnp.zeros(distance.shape, F32)
    for step, tap in enumerate(tap_values()):
        value = jnp.where(distance == step, tap, value)
    inside = (position >= offset) & (position < offset + 2 * TV) & ((i < 2) | (i >= 6))
    return jnp.where(inside, value, 0.0).astype(BF16)


def fill_rows(slots, toff, wide, wide_t):
    @pl.loop(0, slots // 2)
    def _(c):
        spot = lax.broadcasted_iota(jnp.int32, (16, SG), 0)
        lane = lax.broadcasted_iota(jnp.int32, (16, SG), 1)
        offset = jnp.where(spot < 8, toff[0, 2 * c], toff[0, 2 * c + 1])
        wide[pl.ds(pl.multiple_of(SG + c * 16, 16), 16), :] = edge_values(lane, offset, spot)

    lane = lax.broadcasted_iota(jnp.int32, (1, 8 * slots), 1)
    offset = jnp.zeros_like(lane)
    for t in range(slots):
        offset = jnp.where(lane >> 3 == t, toff[0, t], offset)

    @pl.loop(0, SG // 64)
    def _(c):
        position = lax.broadcasted_iota(jnp.int32, (64, 8 * slots), 0) + c * 64
        spot = lax.broadcasted_iota(jnp.int32, (64, 8 * slots), 1)
        wide_t[pl.ds(pl.multiple_of(c * 64, 64), 64), SG:] = edge_values(position, offset, spot)


def forward_kernel(
    n, slots, w_ref, foff_h, soff_h, toff_h, facet_h, basis_h, taper_h, smooth_h, smooth_t_h,
    summed, screen, wide, wide_t,
    half, spec, phase, foff, soff, toff, facet, basis, taper,
    outgoing, own, near, pair, mid, quad_sum, relay, far,
    load_s, near_s, near_r, mid_s, mid_r, relay_s, relay_r, far_s, far_r
):
    pairs = (
        (foff_h, foff), (taper_h, taper), (basis_h, basis), (facet_h, facet), (soff_h, soff),
        (toff_h, toff), (smooth_h, wide.at[0:SG]), (smooth_t_h, wide_t.at[:, 0:SG]),
    )
    loads = [pltpu.make_async_copy(src, dst, load_s.at[i]) for i, (src, dst) in enumerate(pairs)]
    for load in loads:
        load.start()

    quads = n // 4
    me = lax.axis_index("facet")
    quad, middle, core = me // 4, lax.rem(me // 2, 2), lax.rem(me, 2)
    other, odd, group = 1 - middle, lax.rem(quad, 2), quad // 2
    mate = quad + 1 - 2 * odd
    sibling, beside = index(quad, middle, 1 - core), index(quad, other, core)
    high = quad // (quads // 2)
    inner_side = jnp.where(high == odd, 0, 1)

    def turn(k):
        spot = quads - 2 - inner_side
        far_k = jnp.where(k > spot, k - 1, k)
        down = quads - 1 - far_k
        down = jnp.where(down < 2 * group + 2, down - 2, down)
        up = jnp.where(far_k >= 2 * group, far_k + 2, far_k)
        j = jnp.where(k == spot, mate, jnp.where(high == 1, up, down))
        return jnp.where(k == quads - 1, quad, j)

    barrier = pltpu.get_barrier_semaphore()
    peers = [index(lax.rem(quad + k, quads), middle, core) for k in range(1, quads)] + [beside, sibling]
    for peer in peers:
        pl.semaphore_signal(barrier, inc=1, device_id={"facet": peer}, device_id_type=MESH)

    loads[0].wait()
    loads[1].wait()
    phase[0], phase[1] = tapered_phase(foff, taper)
    lanes = lax.broadcasted_iota(jnp.int32, (M, M), 1)
    loads[2].wait()
    loads[3].wait()

    @pl.loop(0, 2)
    def _(c):
        cols = pl.ds(pl.multiple_of(c * 256, 256), 256)
        br, bi = basis[0, :, cols], basis[1, :, cols]
        half[0, :, cols] = (dot(facet[0], br) - dot(facet[1], bi)).astype(BF16)
        half[1, :, cols] = (dot(facet[0], bi) + dot(facet[1], br)).astype(BF16)

    @pl.loop(0, 2)
    def _(c):
        cols = pl.ds(pl.multiple_of(c * 256, 256), 256)
        hr, hi = half[0, :, cols], half[1, :, cols]
        real = dot(basis[0], hr) - dot(basis[1], hi)
        imag = dot(basis[0], hi) + dot(basis[1], hr)
        for side in range(2):
            part = slice(side * M, side * M + M)
            for plane, value in enumerate((real, imag)):
                spec[plane, c * 2 + side, 0:F] = value[:, part]
                spec[plane, c * 2 + side, F:WIDE] = value[0:M, part]

    spec[:, F // M] = spec[:, 0]
    loads[4].wait()

    def cut(s, target, where):
        sx, sy = soff[0, s], soff[1, s]
        tile, offset = sy >> 7, sy & 127
        rows = pl.ds(sx, M)

        def window(plane):
            value = jnp.where(lanes >= offset, spec[plane, tile, rows], spec[plane, tile + 1, rows])
            return pltpu.roll(value, (M - offset) & 127, 1)

        real, imag = window(0), window(1)
        pc, ps = phase[0], phase[1]
        target[where[0], where[1], 0] = (pc * real - ps * imag).astype(BF16)
        target[where[0], where[1], 1] = (pc * imag + ps * real).astype(BF16)

    def near_copy(h, j):
        return send(outgoing.at[h, j], near.at[h, j], near_s.at[h, j], near_r.at[h, j], sibling)

    def mid_copy(j):
        return send(pair.at[j], mid.at[j], mid_s.at[j], mid_r.at[j], beside)

    def relay_copy(j):
        return send(quad_sum.at[j], relay.at[j], relay_s.at[j], relay_r.at[j], index(mate, middle, core))

    def far_copy(j, slot):
        return send(quad_sum.at[j], far.at[slot], far_s.at[j], far_r.at[slot], index(j, middle, core))

    def is_mate(j):
        return j == mate

    def is_gate(j):
        return (j != mate) & (odd == jnp.where(j > quad, 1, 0))

    def is_outer(j):
        return (j != mate) & (odd != jnp.where(j > quad, 1, 0))

    def near_sum(h, j):
        return own[h, j].astype(F32) + near[h, j].astype(F32)

    pl.semaphore_wait(barrier, len(peers))

    @pl.loop(0, quads)
    def _(k):
        j = turn(k)
        cut(index(j, other, 1 - core), outgoing, (0, j))
        near_copy(0, j).start()

    @pl.loop(0, quads)
    def _(k):
        j = turn(k)
        cut(index(j, other, core), own, (0, j))

    @pl.loop(0, quads)
    def _(k):
        j = turn(k)
        near_copy(0, j).wait_recv()
        pair[j] = near_sum(0, j).astype(BF16)
        mid_copy(j).start()

    @pl.loop(0, quads)
    def _(k):
        j = turn(k)
        cut(index(j, middle, 1 - core), outgoing, (1, j))
        near_copy(1, j).start()

    @pl.loop(0, quads)
    def _(k):
        j = turn(k)
        cut(index(j, middle, core), own, (1, j))

    fill_screen(w_ref[0], screen)

    @pl.loop(0, quads - 1)
    def _(k):
        j = turn(k)
        near_copy(1, j).wait_recv()
        mid_copy(j).wait_recv()

        @pl.when(is_gate(j))
        def _():
            relay_copy(j).wait_recv()
            quad_sum[j] = (near_sum(1, j) + mid[j].astype(F32) + relay[j].astype(F32)).astype(BF16)
            far_copy(j, group).start()

        @pl.when(is_mate(j))
        def _():
            quad_sum[j] = (near_sum(1, j) + mid[j].astype(F32)).astype(BF16)
            far_copy(j, group).start()

        @pl.when(is_outer(j))
        def _():
            quad_sum[j] = (near_sum(1, j) + mid[j].astype(F32)).astype(BF16)
            relay_copy(j).start()

    loads[5].wait()
    fill_rows(slots, toff, wide, wide_t)
    near_copy(1, quad).wait_recv()
    mid_copy(quad).wait_recv()
    summed[...] = near_sum(1, quad) + mid[quad].astype(F32)
    for step in range(quads // 2):
        slot = lax.rem(group + step, quads // 2)
        far_copy(quad, slot).wait_recv()
        summed[...] += far[slot].astype(F32)
    loads[6].wait()
    loads[7].wait()

    @pl.loop(0, quads)
    def _(k):
        j = turn(k)
        near_copy(0, j).wait_send()
        near_copy(1, j).wait_send()
        mid_copy(j).wait_send()

    @pl.loop(0, quads - 1)
    def _(k):
        j = turn(k)

        @pl.when(is_outer(j))
        def _():
            relay_copy(j).wait_send()

        @pl.when(jnp.logical_not(is_outer(j)))
        def _():
            far_copy(j, group).wait_send()


def subgrid_kernel(
    slots, count_ref, toff_h, summed, screen, wide, wide_t, pad, pad_t, ker, ker_t, observed,
    residual_h, coefficient, inner, model, grid, spread, sent, toff, sems, load_s
):
    load = pltpu.make_async_copy(toff_h, toff, load_s)
    load.start()
    groups = slots // GROUP
    sr, si = summed[0], summed[1]
    stacked = jnp.concatenate(
        [jnp.concatenate([sr, si], axis=1), jnp.concatenate([-si, sr], axis=1)], axis=0
    ).astype(BF16)
    inner[...] = dot(pad[...], stacked).astype(BF16)

    for c in range(2):
        cols = slice(c * 256, c * 256 + 256)
        late = slice(SG + c * 256, SG + c * 256 + 256)
        real, imag = dot(inner[...], pad_t[:, cols]), dot(inner[...], pad_t[:, late])
        cos_value, sin_value = screen[0, :, cols], screen[1, :, cols]
        model[:, cols] = (cos_value * real - sin_value * imag).astype(BF16)
        model[:, late] = (cos_value * imag + sin_value * real).astype(BF16)

    for plane in range(2):
        for c in range(2):
            start = plane * SG + c * 256
            value = dot(wide[...], model[:, start : start + 256])
            for side in range(2):
                grid[plane, c * 2 + side] = value[:, side * 128 : side * 128 + 128]
                spread[plane, c * 2 + side] = jnp.zeros(spread.shape[2:], F32)

    load.wait()
    count = count_ref[0]
    lanes = lax.broadcasted_iota(jnp.int32, (TV, TV), 1)
    subs = lax.broadcasted_iota(jnp.int32, (8, TV), 0)
    top, bottom = subs < 2, subs >= 6

    def out_copy(step):
        tiles = pl.ds(step * GROUP, GROUP)
        return pltpu.make_async_copy(sent.at[tiles], residual_h.at[tiles], sems.at[step])

    filled = (count + GROUP - 1) // GROUP

    @pl.loop(0, filled)
    def _(step):
        slot = [step * GROUP + g for g in range(GROUP)]
        spots, left = [], []
        for t in slot:
            ou, ov = toff[0, t] + 1, toff[1, t]
            rows = pl.ds((ou & 1) * (SG // 2) + (ou >> 1), TV)
            tail = pl.ds(pl.multiple_of(SG + t * 8, 8), 8)
            first, turn = ov >> 7, ov & 127
            tiles = (first, first + 1, jnp.minimum(first + 2, SG // 128 - 1))
            spots.append((rows, tail, tiles, turn))

            def pick(plane, where_rows, size):
                keep = lanes[0:size] >= turn
                part = [grid[plane, k, where_rows] for k in tiles]
                both = [jnp.where(keep, part[k], part[k + 1]) for k in range(2)]
                return jnp.concatenate([pltpu.roll(x, (TV - turn) & 127, 1) for x in both], axis=1)

            for plane in range(2):
                body, edge = pick(plane, rows, TV), pick(plane, tail, 8)
                wide_top = jnp.concatenate([top, top], axis=1)
                wide_bottom = jnp.concatenate([bottom, bottom], axis=1)
                left.append(
                    jnp.concatenate(
                        [
                            jnp.where(wide_top, edge, body[0:8]), body[8 : TV - 8],
                            jnp.where(wide_bottom, edge, body[TV - 8 :]),
                        ],
                        axis=0,
                    ).astype(BF16)
                )
        rest = []
        for g, t in enumerate(slot):
            for plane in range(2):
                predicted = dot(left[g * 2 + plane], ker_t[...])
                value = (observed[t, plane].astype(F32) - predicted).astype(BF16)
                rest.append(jnp.where(t < count, value, jnp.zeros_like(value)))
                sent[t, plane] = rest[-1]
        out_copy(step).start()
        back = [dot(value, ker[...]).astype(BF16).astype(F32) for value in rest]
        for g in range(GROUP):
            rows, tail, tiles, turn = spots[g]
            keep = lanes >= turn
            for plane in range(2):
                value = back[g * 2 + plane]
                one, two = pltpu.roll(value[:, 0:128], turn, 1), pltpu.roll(value[:, 128:], turn, 1)
                blank = jnp.zeros((TV, TV), F32)
                parts = (jnp.where(keep, one, blank), jnp.where(keep, two, one), jnp.where(keep, blank, two))
                for tile, part in zip(tiles, parts):
                    zero = blank[0:8]
                    edge = jnp.where(top, part[0:8], jnp.where(bottom, part[TV - 8 :], zero))
                    body = jnp.concatenate(
                        [jnp.where(top, zero, part[0:8]), part[8 : TV - 8], jnp.where(bottom, zero, part[TV - 8 :])],
                        axis=0,
                    )
                    spread[plane, tile, rows] += body
                    spread[plane, tile, tail] += edge

    @pl.loop(filled, groups)
    def _(step):
        for g in range(GROUP):
            sent[step * GROUP + g] = jnp.zeros(sent.shape[1:], BF16)
        out_copy(step).start()

    for c in range(2):
        cols = slice(c * 256, c * 256 + 256)
        late = slice(SG + c * 256, SG + c * 256 + 256)
        ar, ai = [
            dot(wide_t[...], jnp.concatenate([spread[p, 2 * c], spread[p, 2 * c + 1]], axis=1).astype(BF16))
            for p in range(2)
        ]
        sc, ss = screen[0, :, cols], screen[1, :, cols]
        model[:, cols] = (sc * ar + ss * ai).astype(BF16)
        model[:, late] = (sc * ai - ss * ar).astype(BF16)
    reduced = (
        dot(pad_t[:, 0:SG], model[:, 0:SG]) + dot(pad_t[:, SG:], model[:, SG:])
    ).astype(BF16)
    both = dot(reduced, pad[...])
    coefficient[0] = (both[0:M, 0:M] + both[M:, M:]).astype(BF16)
    coefficient[1] = (both[M:, 0:M] - both[0:M, M:]).astype(BF16)

    @pl.loop(0, groups)
    def _(step):
        out_copy(step).wait()


def backward_kernel(n, foff, soff, piece, basis, taper, out, acc, spec, half, phase):
    phase[0], phase[1] = tapered_phase(foff, taper)
    lanes = lax.broadcasted_iota(jnp.int32, (M, M), 1)
    acc[...] = jnp.zeros_like(acc)

    @pl.loop(0, n, unroll=4)
    def _(s):
        sx, sy = soff[0, s], soff[1, s]
        tile, shift = sy >> 7, sy & 127
        rows = pl.ds(sx, M)
        kept = lanes >= shift
        pc, ps = phase[0], phase[1]
        real, imag = piece[s, 0].astype(F32), piece[s, 1].astype(F32)
        blank = jnp.zeros((M, M), F32)
        values = (pc * real + ps * imag, pc * imag - ps * real)
        for plane in range(2):
            turned = pltpu.roll(values[plane], shift, 1)
            acc[plane, tile, rows] += jnp.where(kept, turned, blank)
            acc[plane, tile + 1, rows] += jnp.where(kept, blank, turned)

    acc[:, 0] += acc[:, F // M]
    acc[:, 0 : F // M, 0:M] += acc[:, 0 : F // M, F:WIDE]
    for k in range(F // M):
        spec[:, :, k * M : k * M + M] = acc[:, k, 0:F].astype(BF16)

    @pl.loop(0, 2)
    def _(c):
        cols = pl.ds(pl.multiple_of(c * 256, 256), 256)
        xr, xi = spec[0, :, cols], spec[1, :, cols]
        half[0, :, cols] = (dot(basis[0], xr) + dot(basis[1], xi)).astype(BF16)
        half[1, :, cols] = (dot(basis[0], xi) - dot(basis[1], xr)).astype(BF16)

    @pl.loop(0, 2)
    def _(c):
        cols = pl.ds(pl.multiple_of(c * 256, 256), 256)
        br, bi = basis[0, :, cols], basis[1, :, cols]
        out[0, :, cols] = (dot(half[0], br) + dot(half[1], bi)).astype(BF16)
        out[1, :, cols] = (dot(half[1], br) - dot(half[0], bi)).astype(BF16)


SMEM_SPEC = pl.BlockSpec(memory_space=pltpu.SMEM)
VMEM_SPEC = pl.BlockSpec(memory_space=pltpu.VMEM)
HBM_SPEC = pl.BlockSpec(memory_space=pltpu.HBM)
DMA = pltpu.SemaphoreType.DMA


def per_device(facets, facet_offsets, subgrid_offsets, w_terms, tile_count, tile_offsets, observed):
    n = lax.axis_size("facet")
    quads = n // 4
    soff_t, toff_t = subgrid_offsets.T, tile_offsets.T
    slots = observed.shape[0]
    basis = jnp.asarray(basis_table())
    real, imag = padding_table(n)
    pad = jnp.asarray(np.concatenate([real, imag], axis=1))
    pad_t = jnp.asarray(np.block([[real.T, imag.T], [-imag.T, real.T]]))
    taper = jnp.asarray(taper_square())
    smooth_np = smooth_table()
    smooth, smooth_t = jnp.asarray(smooth_np), jnp.asarray(np.ascontiguousarray(smooth_np.T))
    ker_np = kernel_table()
    ker, ker_t = jnp.asarray(ker_np), jnp.asarray(np.ascontiguousarray(ker_np.T))
    plain = pltpu.CompilerParams(vmem_limit_bytes=LIMIT)

    deep = SG + 8 * slots
    piece_shape = (2, M, M)
    in_hbm = [
        pltpu.with_memory_space_constraint(x, pltpu.HBM)
        for x in (facet_offsets, soff_t, toff_t, facets[0], basis, taper, smooth, smooth_t)
    ]
    summed, screen, wide, wide_t = pl.pallas_call(
        functools.partial(forward_kernel, n, slots),
        out_shape=(
            jax.ShapeDtypeStruct((2, M, M), F32), jax.ShapeDtypeStruct((2, SG, SG), F32),
            jax.ShapeDtypeStruct((deep, SG), BF16), jax.ShapeDtypeStruct((SG, deep), BF16),
        ),
        in_specs=[SMEM_SPEC] + [HBM_SPEC] * 8,
        out_specs=(VMEM_SPEC,) * 4,
        scratch_shapes=[
            VMEM((2, F, F), BF16), VMEM((2, WIDE // M, WIDE, M), F32), VMEM((2, M, M), F32),
            pltpu.SMEM((1, 2), jnp.int32), pltpu.SMEM((2, n), jnp.int32),
            pltpu.SMEM((2, slots), jnp.int32),
            VMEM((2, F, F), BF16), VMEM((2, F, F), BF16), VMEM((M, M), F32),
            *[VMEM((2, quads, *piece_shape), BF16)] * 3,
            *[VMEM((quads, *piece_shape), BF16)] * 4, VMEM((quads // 2, *piece_shape), BF16),
            DMA((8,)), *[DMA((2, quads))] * 2, *[DMA((quads,))] * 5, DMA((quads // 2,)),
        ],
        compiler_params=pltpu.CompilerParams(
            vmem_limit_bytes=LIMIT, collective_id=0, has_side_effects=True
        ),
        name="forward",
    )(w_terms, *in_hbm)

    residual, coefficient = pl.pallas_call(
        functools.partial(subgrid_kernel, slots),
        out_shape=(
            jax.ShapeDtypeStruct((slots, 2, TV, TV), BF16),
            jax.ShapeDtypeStruct((2, M, M), BF16),
        ),
        in_specs=[SMEM_SPEC, HBM_SPEC] + [VMEM_SPEC] * 9,
        out_specs=(HBM_SPEC, VMEM_SPEC),
        scratch_shapes=[
            VMEM((SG, 2 * M), BF16), VMEM((SG, 2 * SG), BF16),
            VMEM((2, SG // 128, deep, 128), F32), VMEM((2, SG // 128, deep, 128), F32),
            VMEM((slots, 2, TV, TV), BF16),
            pltpu.SMEM((2, slots), jnp.int32), DMA((slots // GROUP,)), DMA,
        ],
        compiler_params=plain,
        name="subgrid",
    )(tile_count, in_hbm[2], summed, screen, wide, wide_t, pad, pad_t, ker, ker_t, observed)

    piece = pl.pallas_call(
        functools.partial(gather_kernel, n),
        out_shape=jax.ShapeDtypeStruct((n, 2, M, M), BF16),
        in_specs=[VMEM_SPEC],
        out_specs=VMEM_SPEC,
        scratch_shapes=[DMA((2, quads))] * 2 + [DMA((quads,))] * 4 + [DMA],
        compiler_params=pltpu.CompilerParams(
            vmem_limit_bytes=LIMIT, collective_id=1, has_side_effects=True
        ),
        name="gather",
    )(coefficient)

    update = pl.pallas_call(
        functools.partial(backward_kernel, n),
        out_shape=jax.ShapeDtypeStruct((2, F, F), BF16),
        in_specs=[SMEM_SPEC, SMEM_SPEC, VMEM_SPEC, VMEM_SPEC, VMEM_SPEC],
        out_specs=VMEM_SPEC,
        scratch_shapes=[
            VMEM((2, WIDE // M, WIDE, M), F32), VMEM((2, F, F), BF16), VMEM((2, F, F), BF16),
            VMEM((2, M, M), F32),
        ],
        compiler_params=plain,
        name="backward",
    )(facet_offsets, soff_t, piece, basis, taper)
    return (residual, update[None])


def solution(mesh):
    placed = (
        P(("groups", "facet"), None, None, None),
        P(("groups", "facet"), None),
        P("groups", None),
        P(("groups", "facet")),
        P(("groups", "facet")),
        P(("groups", "facet"), None),
        P(("groups", "facet"), None, None, None),
    )
    return jax.shard_map(
        per_device,
        mesh=mesh,
        in_specs=placed,
        out_specs=(
            P(("groups", "facet"), None, None, None),
            P(("groups", "facet"), None, None, None),
        ),
        check_vma=False,
    )
```

```python
import functools
import math

import jax
import jax.numpy as jnp
import ml_dtypes
import numpy as np
from jax import lax
from jax.experimental import pallas as pl
from jax.experimental.pallas import tpu as pltpu
from jax.sharding import PartitionSpec as P

F = 512
M = 128
SG = 512
TV = 128
WIDE = F + M
GROUP = 4

BF16 = jnp.bfloat16
F32 = jnp.float32
TWO_PI = 2.0 * math.pi
MESH = pl.DeviceIdType.MESH
VMEM = pltpu.VMEM
LIMIT = 48 * 1024 * 1024


def basis_table():
    index = np.arange(F)
    angle = -TWO_PI * (index[:, None] * index[None, :] % F) / F
    scale = 1.0 / math.sqrt(F)
    return np.stack([np.cos(angle) * scale, np.sin(angle) * scale]).astype(ml_dtypes.bfloat16)


def padding_table(facet_count):
    angle = TWO_PI * (np.arange(SG)[:, None] * np.arange(M)[None, :] % SG) / SG
    scale = (M * math.sqrt(facet_count)) ** (-0.5)
    return np.stack([np.cos(angle) * scale, np.sin(angle) * scale]).astype(ml_dtypes.bfloat16)


def taper_square():
    taper = 0.6 + 0.4 * np.sin(math.pi * (np.arange(M) + 0.5) / M)
    return (taper[:, None] * taper[None, :]).astype(np.float32)


def dot(left, right):
    return jnp.dot(left, right, preferred_element_type=F32)


def cos_sin_turns(turns):
    quarter = jnp.floor(turns * 4.0 + 0.5)
    y = (turns - quarter * 0.25) * TWO_PI
    y2 = y * y
    sine = y * (1.0 + y2 * (-1.0 / 6 + y2 * (1.0 / 120 + y2 * (-1.0 / 5040 + y2 * (1.0 / 362880)))))
    cosine = 1.0 + y2 * (
        -0.5 + y2 * (1.0 / 24 + y2 * (-1.0 / 720 + y2 * (1.0 / 40320 - y2 * (1.0 / 3628800))))
    )
    which = quarter.astype(jnp.int32) & 3
    odd = (which & 1) == 1
    first = jnp.where(odd, sine, cosine)
    second = jnp.where(odd, cosine, sine)
    cos_value = jnp.where((which == 1) | (which == 2), -first, first)
    sin_value = jnp.where(which >= 2, -second, second)
    return cos_value, sin_value


def tapered_phase(offset_ref, taper_ref):
    rows = lax.broadcasted_iota(jnp.int32, (M, M), 0)
    columns = lax.broadcasted_iota(jnp.int32, (M, M), 1)
    total = (rows * offset_ref[0, 0] + columns * offset_ref[0, 1]) & (F - 1)
    cos_value, sin_value = cos_sin_turns(total.astype(F32) * (1.0 / F))
    taper = taper_ref[...]
    return cos_value * taper, sin_value * taper


def place(n):
    me = lax.axis_index("facet")
    quads = n // 4
    far_first = [1 + (t + quads // 2 - 1) % (quads - 1) for t in range(quads - 1)]
    return quads, me // 4, lax.rem(me // 2, 2), lax.rem(me, 2), far_first


def index(quad, middle, core):
    return quad * 4 + middle * 2 + core


def greet(peers):
    barrier = pltpu.get_barrier_semaphore()
    for peer in peers:
        pl.semaphore_signal(barrier, inc=1, device_id={"facet": peer}, device_id_type=MESH)
    pl.semaphore_wait(barrier, len(peers))


def send(src, dst, send_sem, recv_sem, peer):
    return pltpu.make_async_remote_copy(
        src_ref=src, dst_ref=dst, send_sem=send_sem, recv_sem=recv_sem,
        device_id={"facet": peer}, device_id_type=MESH,
    )


def fill_screen(w_value, screen):
    @pl.loop(0, 4)
    def _(c):
        rows = pl.ds(pl.multiple_of(c * 128, 128), 128)
        u = (lax.broadcasted_iota(jnp.int32, (128, SG), 0) + (c * 128 - 256)).astype(F32)
        v = (lax.broadcasted_iota(jnp.int32, (128, SG), 1) - 256).astype(F32)
        radius = (u * u + v * v) * (1.0 / (SG * SG))
        cos_value, sin_value = cos_sin_turns(w_value * (jnp.sqrt(1.0 + radius) - 1.0))
        screen[0, rows, :] = cos_value
        screen[1, rows, :] = sin_value


def tap_values():
    taps = np.arange(5, dtype=np.float32)
    value = 0.75 * np.exp(-(taps / 1.5) * (taps / 1.5))
    return [float(x) for x in value.astype(ml_dtypes.bfloat16).astype(np.float32)]


def smooth_table():
    order = np.concatenate([np.arange(0, SG, 2), np.arange(1, SG, 2)])
    distance = np.abs(np.arange(SG)[None, :] - order[:, None])
    taps = np.array(tap_values() + [0.0], np.float32)
    return taps[np.minimum(distance, 5)].astype(ml_dtypes.bfloat16)


def kernel_table():
    distance = np.abs(np.arange(2 * TV)[None, :] - 2 * np.arange(TV)[:, None] - 1)
    taps = np.array(tap_values() + [0.0], np.float32)
    return taps[np.minimum(distance, 5)].astype(ml_dtypes.bfloat16)


def edge_values(position, offset, spot):
    i = spot & 7
    slot = jnp.where(i < 2, i, i + (TV - 8))
    distance = jnp.abs(position - offset - 2 * slot - 1)
    value = jnp.zeros(distance.shape, F32)
    for step, tap in enumerate(tap_values()):
        value = jnp.where(distance == step, tap, value)
    inside = (position >= offset) & (position < offset + 2 * TV) & ((i < 2) | (i >= 6))
    return jnp.where(inside, value, 0.0).astype(BF16)


def fill_rows(slots, toff, wide, wide_t):
    @pl.loop(0, slots // 2)
    def _(c):
        spot = lax.broadcasted_iota(jnp.int32, (16, SG), 0)
        lane = lax.broadcasted_iota(jnp.int32, (16, SG), 1)
        offset = jnp.where(spot < 8, toff[0, 2 * c], toff[0, 2 * c + 1])
        wide[pl.ds(pl.multiple_of(SG + c * 16, 16), 16), :] = edge_values(lane, offset, spot)

    lane = lax.broadcasted_iota(jnp.int32, (1, 8 * slots), 1)
    offset = jnp.zeros_like(lane)
    for t in range(slots):
        offset = jnp.where(lane >> 3 == t, toff[0, t], offset)

    @pl.loop(0, SG // 64)
    def _(c):
        position = lax.broadcasted_iota(jnp.int32, (64, 8 * slots), 0) + c * 64
        spot = lax.broadcasted_iota(jnp.int32, (64, 8 * slots), 1)
        wide_t[pl.ds(pl.multiple_of(c * 64, 64), 64), SG:] = edge_values(position, offset, spot)


def forward_kernel(
    n, slots, w_ref, foff_h, soff_h, toff_h, facet_h, basis_h, taper_h, smooth_h, smooth_t_h,
    summed, screen, wide, wide_t,
    half, spec, phase, foff, soff, toff, facet, basis, taper,
    outgoing, own, near, pair, mid, quad_sum, relay, far,
    load_s, near_s, near_r, mid_s, mid_r, relay_s, relay_r, far_s, far_r
):
    pairs = (
        (foff_h, foff), (taper_h, taper), (basis_h, basis), (facet_h, facet), (soff_h, soff),
        (toff_h, toff), (smooth_h, wide.at[0:SG]), (smooth_t_h, wide_t.at[:, 0:SG]),
    )
    loads = [pltpu.make_async_copy(src, dst, load_s.at[i]) for i, (src, dst) in enumerate(pairs)]
    for load in loads:
        load.start()

    quads = n // 4
    me = lax.axis_index("facet")
    quad, middle, core = me // 4, lax.rem(me // 2, 2), lax.rem(me, 2)
    other, odd, group = 1 - middle, lax.rem(quad, 2), quad // 2
    mate = quad + 1 - 2 * odd
    sibling, beside = index(quad, middle, 1 - core), index(quad, other, core)
    high = quad // (quads // 2)
    inner_side = jnp.where(high == odd, 0, 1)

    def turn(k):
        spot = quads - 2 - inner_side
        far_k = jnp.where(k > spot, k - 1, k)
        down = quads - 1 - far_k
        down = jnp.where(down < 2 * group + 2, down - 2, down)
        up = jnp.where(far_k >= 2 * group, far_k + 2, far_k)
        j = jnp.where(k == spot, mate, jnp.where(high == 1, up, down))
        return jnp.where(k == quads - 1, quad, j)

    barrier = pltpu.get_barrier_semaphore()
    peers = [index(lax.rem(quad + k, quads), middle, core) for k in range(1, quads)] + [beside, sibling]
    for peer in peers:
        pl.semaphore_signal(barrier, inc=1, device_id={"facet": peer}, device_id_type=MESH)

    loads[0].wait()
    loads[1].wait()
    phase[0], phase[1] = tapered_phase(foff, taper)
    lanes = lax.broadcasted_iota(jnp.int32, (M, M), 1)
    loads[2].wait()
    loads[3].wait()

    @pl.loop(0, 2)
    def _(c):
        cols = pl.ds(pl.multiple_of(c * 256, 256), 256)
        br, bi = basis[0, :, cols], basis[1, :, cols]
        half[0, :, cols] = (dot(facet[0], br) - dot(facet[1], bi)).astype(BF16)
        half[1, :, cols] = (dot(facet[0], bi) + dot(facet[1], br)).astype(BF16)

    @pl.loop(0, 2)
    def _(c):
        cols = pl.ds(pl.multiple_of(c * 256, 256), 256)
        hr, hi = half[0, :, cols], half[1, :, cols]
        real = dot(basis[0], hr) - dot(basis[1], hi)
        imag = dot(basis[0], hi) + dot(basis[1], hr)
        for side in range(2):
            part = slice(side * M, side * M + M)
            for plane, value in enumerate((real, imag)):
                spec[plane, c * 2 + side, 0:F] = value[:, part]
                spec[plane, c * 2 + side, F:WIDE] = value[0:M, part]

    spec[:, F // M] = spec[:, 0]
    loads[4].wait()

    def cut(s, target, where):
        sx, sy = soff[0, s], soff[1, s]
        tile, offset = sy >> 7, sy & 127
        rows = pl.ds(sx, M)

        def window(plane):
            value = jnp.where(lanes >= offset, spec[plane, tile, rows], spec[plane, tile + 1, rows])
            return pltpu.roll(value, (M - offset) & 127, 1)

        real, imag = window(0), window(1)
        pc, ps = phase[0], phase[1]
        target[where[0], where[1], 0] = (pc * real - ps * imag).astype(BF16)
        target[where[0], where[1], 1] = (pc * imag + ps * real).astype(BF16)

    def near_copy(h, j):
        return send(outgoing.at[h, j], near.at[h, j], near_s.at[h, j], near_r.at[h, j], sibling)

    def mid_copy(j, p):
        return send(pair.at[j, p], mid.at[j, p], mid_s.at[j, p], mid_r.at[j, p], beside)

    def relay_copy(j, p):
        return send(
            quad_sum.at[j, p], relay.at[j, p], relay_s.at[j, p], relay_r.at[j, p], index(mate, middle, core)
        )

    def far_copy(j, slot, p):
        return send(quad_sum.at[j, p], far.at[slot, p], far_s.at[j, p], far_r.at[slot, p], index(j, middle, core))

    def is_mate(j):
        return j == mate

    def is_gate(j):
        return (j != mate) & (odd == jnp.where(j > quad, 1, 0))

    def is_outer(j):
        return (j != mate) & (odd != jnp.where(j > quad, 1, 0))

    def near_sum(h, j, p):
        return own[h, j, p].astype(F32) + near[h, j, p].astype(F32)

    def mid_sum(j, p):
        return near_sum(1, j, p) + mid[j, p].astype(F32)

    pl.semaphore_wait(barrier, len(peers))

    @pl.loop(0, quads)
    def _(k):
        j = turn(k)
        cut(index(j, other, 1 - core), outgoing, (0, j))
        near_copy(0, j).start()

    @pl.loop(0, quads)
    def _(k):
        j = turn(k)
        cut(index(j, other, core), own, (0, j))

    @pl.loop(0, quads)
    def _(k):
        j = turn(k)
        near_copy(0, j).wait_recv()
        for p in range(2):
            pair[j, p] = near_sum(0, j, p).astype(BF16)
            mid_copy(j, p).start()

    @pl.loop(0, quads)
    def _(k):
        j = turn(k)
        cut(index(j, middle, 1 - core), outgoing, (1, j))
        near_copy(1, j).start()

    @pl.loop(0, quads)
    def _(k):
        j = turn(k)
        cut(index(j, middle, core), own, (1, j))

    fill_screen(w_ref[0], screen)

    @pl.loop(0, quads - 1)
    def _(k):
        j = turn(k)
        near_copy(1, j).wait_recv()
        for p in range(2):
            mid_copy(j, p).wait_recv()

            @pl.when(is_gate(j))
            def _():
                relay_copy(j, p).wait_recv()
                quad_sum[j, p] = (mid_sum(j, p) + relay[j, p].astype(F32)).astype(BF16)
                far_copy(j, group, p).start()

            @pl.when(is_mate(j))
            def _():
                quad_sum[j, p] = mid_sum(j, p).astype(BF16)
                far_copy(j, group, p).start()

            @pl.when(is_outer(j))
            def _():
                quad_sum[j, p] = mid_sum(j, p).astype(BF16)
                relay_copy(j, p).start()

    loads[5].wait()
    fill_rows(slots, toff, wide, wide_t)
    near_copy(1, quad).wait_recv()
    for p in range(2):
        mid_copy(quad, p).wait_recv()
        summed[p] = mid_sum(quad, p)
    for step in range(quads // 2):
        slot = lax.rem(group + step, quads // 2)
        for p in range(2):
            far_copy(quad, slot, p).wait_recv()
            summed[p] += far[slot, p].astype(F32)
    loads[6].wait()
    loads[7].wait()

    @pl.loop(0, quads)
    def _(k):
        j = turn(k)
        near_copy(0, j).wait_send()
        near_copy(1, j).wait_send()
        for p in range(2):
            mid_copy(j, p).wait_send()

    @pl.loop(0, quads - 1)
    def _(k):
        j = turn(k)
        for p in range(2):

            @pl.when(is_outer(j))
            def _():
                relay_copy(j, p).wait_send()

            @pl.when(jnp.logical_not(is_outer(j)))
            def _():
                far_copy(j, group, p).wait_send()


def subgrid_kernel(
    slots, count_ref, toff_h, summed, screen, wide, wide_t, pad, pad_t, ker, ker_t, observed,
    residual_h, coefficient, inner, model, grid, spread, sent, toff, sems, load_s
):
    load = pltpu.make_async_copy(toff_h, toff, load_s)
    load.start()
    groups = slots // GROUP
    sr, si = summed[0], summed[1]
    stacked = jnp.concatenate(
        [jnp.concatenate([sr, si], axis=1), jnp.concatenate([-si, sr], axis=1)], axis=0
    ).astype(BF16)
    inner[...] = dot(pad[...], stacked).astype(BF16)

    for c in range(2):
        cols = slice(c * 256, c * 256 + 256)
        late = slice(SG + c * 256, SG + c * 256 + 256)
        real, imag = dot(inner[...], pad_t[:, cols]), dot(inner[...], pad_t[:, late])
        cos_value, sin_value = screen[0, :, cols], screen[1, :, cols]
        model[:, cols] = (cos_value * real - sin_value * imag).astype(BF16)
        model[:, late] = (cos_value * imag + sin_value * real).astype(BF16)

    for plane in range(2):
        for c in range(2):
            start = plane * SG + c * 256
            value = dot(wide[...], model[:, start : start + 256])
            for side in range(2):
                grid[plane, c * 2 + side] = value[:, side * 128 : side * 128 + 128]
                spread[plane, c * 2 + side] = jnp.zeros(spread.shape[2:], F32)

    load.wait()
    count = count_ref[0]
    lanes = lax.broadcasted_iota(jnp.int32, (TV, TV), 1)
    subs = lax.broadcasted_iota(jnp.int32, (8, TV), 0)
    top, bottom = subs < 2, subs >= 6

    def out_copy(step):
        tiles = pl.ds(step * GROUP, GROUP)
        return pltpu.make_async_copy(sent.at[tiles], residual_h.at[tiles], sems.at[step])

    filled = (count + GROUP - 1) // GROUP

    @pl.loop(0, filled)
    def _(step):
        slot = [step * GROUP + g for g in range(GROUP)]
        spots, left = [], []
        for t in slot:
            ou, ov = toff[0, t] + 1, toff[1, t]
            rows = pl.ds((ou & 1) * (SG // 2) + (ou >> 1), TV)
            tail = pl.ds(pl.multiple_of(SG + t * 8, 8), 8)
            first, turn = ov >> 7, ov & 127
            tiles = (first, first + 1, jnp.minimum(first + 2, SG // 128 - 1))
            spots.append((rows, tail, tiles, turn))

            def pick(plane, where_rows, size):
                keep = lanes[0:size] >= turn
                part = [grid[plane, k, where_rows] for k in tiles]
                both = [jnp.where(keep, part[k], part[k + 1]) for k in range(2)]
                return jnp.concatenate([pltpu.roll(x, (TV - turn) & 127, 1) for x in both], axis=1)

            for plane in range(2):
                body, edge = pick(plane, rows, TV), pick(plane, tail, 8)
                wide_top = jnp.concatenate([top, top], axis=1)
                wide_bottom = jnp.concatenate([bottom, bottom], axis=1)
                left.append(
                    jnp.concatenate(
                        [
                            jnp.where(wide_top, edge, body[0:8]), body[8 : TV - 8],
                            jnp.where(wide_bottom, edge, body[TV - 8 :]),
                        ],
                        axis=0,
                    ).astype(BF16)
                )
        rest = []
        for g, t in enumerate(slot):
            for plane in range(2):
                predicted = dot(left[g * 2 + plane], ker_t[...])
                value = (observed[t, plane].astype(F32) - predicted).astype(BF16)
                rest.append(jnp.where(t < count, value, jnp.zeros_like(value)))
                sent[t, plane] = rest[-1]
        out_copy(step).start()
        back = [dot(value, ker[...]).astype(BF16).astype(F32) for value in rest]
        for g in range(GROUP):
            rows, tail, tiles, turn = spots[g]
            keep = lanes >= turn
            for plane in range(2):
                value = back[g * 2 + plane]
                one, two = pltpu.roll(value[:, 0:128], turn, 1), pltpu.roll(value[:, 128:], turn, 1)
                blank = jnp.zeros((TV, TV), F32)
                parts = (jnp.where(keep, one, blank), jnp.where(keep, two, one), jnp.where(keep, blank, two))
                for tile, part in zip(tiles, parts):
                    zero = blank[0:8]
                    edge = jnp.where(top, part[0:8], jnp.where(bottom, part[TV - 8 :], zero))
                    body = jnp.concatenate(
                        [jnp.where(top, zero, part[0:8]), part[8 : TV - 8], jnp.where(bottom, zero, part[TV - 8 :])],
                        axis=0,
                    )
                    spread[plane, tile, rows] += body
                    spread[plane, tile, tail] += edge

    @pl.loop(filled, groups)
    def _(step):
        for g in range(GROUP):
            sent[step * GROUP + g] = jnp.zeros(sent.shape[1:], BF16)
        out_copy(step).start()

    for c in range(2):
        cols = slice(c * 256, c * 256 + 256)
        late = slice(SG + c * 256, SG + c * 256 + 256)
        ar, ai = [
            dot(wide_t[...], jnp.concatenate([spread[p, 2 * c], spread[p, 2 * c + 1]], axis=1).astype(BF16))
            for p in range(2)
        ]
        sc, ss = screen[0, :, cols], screen[1, :, cols]
        model[:, cols] = (sc * ar + ss * ai).astype(BF16)
        model[:, late] = (sc * ai - ss * ar).astype(BF16)
    reduced = (
        dot(pad_t[:, 0:SG], model[:, 0:SG]) + dot(pad_t[:, SG:], model[:, SG:])
    ).astype(BF16)
    both = dot(reduced, pad[...])
    coefficient[0] = (both[0:M, 0:M] + both[M:, M:]).astype(BF16)
    coefficient[1] = (both[M:, 0:M] - both[0:M, M:]).astype(BF16)

    @pl.loop(0, groups)
    def _(step):
        out_copy(step).wait()


def gather_kernel(
    n, mine, foff_h, soff_h, taper, turned, out, arrived, phase, foff, soff,
    near_s, near_r, mid_s, mid_r, far_s, far_r, local, load_s
):
    quads = n // 4
    me = lax.axis_index("facet")
    quad, middle, core = me // 4, lax.rem(me // 2, 2), lax.rem(me, 2)
    other, odd, group = 1 - middle, lax.rem(quad, 2), quad // 2
    mate = quad + 1 - 2 * odd
    sibling, beside = index(quad, middle, 1 - core), index(quad, other, core)
    loads = [pltpu.make_async_copy(foff_h, foff, load_s.at[0]), pltpu.make_async_copy(soff_h, soff, load_s.at[1])]
    for load in loads:
        load.start()

    barrier = pltpu.get_barrier_semaphore()
    peers = [index(lax.rem(quad + k, quads), middle, core) for k in range(1, quads)] + [beside, sibling]
    for peer in peers:
        pl.semaphore_signal(barrier, inc=1, device_id={"facet": peer}, device_id_type=MESH)
    pl.semaphore_wait(barrier, len(peers))

    low = quad < quads // 2

    def turn(k):
        far_k = quads - 2 - k
        down = quads - 1 - far_k
        down = jnp.where(down < 2 * group + 2, down - 2, down)
        up = jnp.where(far_k >= 2 * group, far_k + 2, far_k)
        return jnp.where(k == 0, mate, jnp.where(low, down, up))

    def is_gate(j):
        return (j != mate) & (odd == jnp.where(j > quad, 1, 0))

    def far_copy(source, slot, to, p):
        spot = index(slot, middle, core)
        return send(source.at[p], arrived.at[spot, p], far_s.at[to, p], far_r.at[slot, p], index(to, middle, core))

    def relay_copy(j, p):
        spot = index(j, middle, core)
        return send(
            arrived.at[spot, p], arrived.at[spot, p], far_s.at[quads + j, p], far_r.at[j, p],
            index(mate, middle, core),
        )

    def mid_copy(j, h, p):
        piece = arrived.at[index(j, h, core), p]
        return send(piece, piece, mid_s.at[j, p], mid_r.at[j, p], beside)

    def near_copy(h, j, side, p):
        piece = arrived.at[index(j, h, side), p]
        return send(piece, piece, near_s.at[h, j, p], near_r.at[h, j, p], sibling)

    def mid_own(p):
        return send(mine.at[p], arrived.at[me, p], mid_s.at[quad, p], mid_r.at[quad, p], beside)

    def near_own(p):
        return send(
            mine.at[p], arrived.at[me, p], near_s.at[middle, quad, p], near_r.at[middle, quad, p], sibling
        )

    def far_target(i):
        return jnp.where(i >= group, i + 1, i)

    def first_hop(i):
        g = far_target(i)
        return 2 * g + jnp.where(g < group, 1, 0)

    own = pltpu.make_async_copy(mine, arrived.at[me], local)
    own.start()
    for p in range(2):
        mid_own(p).start()
    for i in range(quads // 2 - 1):
        for p in range(2):
            far_copy(mine, quad, first_hop(i), p).start()
    for p in range(2):
        far_copy(mine, quad, mate, p).start()
        near_own(p).start()

    for load in loads:
        load.wait()
    phase[0], phase[1] = tapered_phase(foff, taper)
    own.wait()

    def transform(spot):
        pc, ps = phase[0], phase[1]
        real, imag = arrived[spot, 0].astype(F32), arrived[spot, 1].astype(F32)
        both = jnp.concatenate([pc * real + ps * imag, pc * imag - ps * real], axis=1).astype(BF16)
        lane = lax.broadcasted_iota(jnp.int32, (8, F), 1)
        cos_value, sin_value = cos_sin_turns(((lane * soff[1, spot]) & (F - 1)).astype(F32) * (1.0 / F))
        for c in range(F // 256):
            cols, late = slice(c * 256, c * 256 + 256), slice(F + c * 256, F + c * 256 + 256)
            real = dot(both, turned[:, cols]).reshape(M // 8, 8, 256)
            imag = dot(both, turned[:, late]).reshape(M // 8, 8, 256)
            cv, sv = cos_value[None, :, cols], sin_value[None, :, cols]
            out[spot, :, cols] = (cv * real - sv * imag).reshape(M, 256).astype(BF16)
            out[spot, :, late] = (cv * imag + sv * real).reshape(M, 256).astype(BF16)

    transform(me)
    for p in range(2):
        near_copy(middle, quad, 1 - core, p).wait_recv()
    transform(sibling)

    def take_far(j):
        for p in range(2):
            far_copy(mine, j, j, p).wait_recv()

            @pl.when(is_gate(j))
            def _():
                relay_copy(j, p).start()

            mid_copy(j, middle, p).start()
            near_copy(middle, j, core, p).start()

    def take_mid(j):
        for p in range(2):
            mid_copy(j, other, p).wait_recv()
            near_copy(other, j, core, p).start()

    def take_near(h, j):
        for p in range(2):
            near_copy(h, j, 1 - core, p).wait_recv()
        transform(index(j, h, 1 - core))

    @pl.loop(0, quads - 1)
    def _(k):
        j = turn(k)
        before = jnp.where(k == 0, quad, turn(jnp.maximum(k - 1, 0)))
        take_far(j)
        take_mid(before)
        transform(index(j, middle, core))
        transform(index(before, other, core))
        take_near(middle, j)
        take_near(other, before)

    last = turn(quads - 2)
    take_mid(last)
    transform(index(last, other, core))
    take_near(other, last)

    for p in range(2):
        mid_own(p).wait_send()
        near_own(p).wait_send()
        far_copy(mine, quad, mate, p).wait_send()
        near_copy(other, quad, core, p).wait_send()
        for i in range(quads // 2 - 1):
            far_copy(mine, quad, first_hop(i), p).wait_send()

    @pl.loop(0, quads - 1)
    def _(k):
        j = turn(k)
        for p in range(2):
            mid_copy(j, middle, p).wait_send()
            near_copy(middle, j, core, p).wait_send()
            near_copy(other, j, core, p).wait_send()

            @pl.when(is_gate(j))
            def _():
                relay_copy(j, p).wait_send()


def backward_kernel(n, soff, pieces, basis, out_h, acc, flat, out, sems):
    acc[...] = jnp.zeros_like(acc)

    @pl.loop(0, n, unroll=2)
    def _(s):
        rows = pl.ds(soff[0, s], M)
        for plane in range(2):
            for k in range(F // M):
                acc[plane, k, rows] += pieces[s, :, plane * F + k * M : plane * F + k * M + M].astype(F32)

    for plane in range(2):
        for k in range(F // M):
            cols = slice(plane * F + k * M, plane * F + k * M + M)
            flat[0:M, cols] = (acc[plane, k, 0:M] + acc[plane, k, F:WIDE]).astype(BF16)
            flat[M:F, cols] = acc[plane, k, M:F].astype(BF16)

    copies = []
    for plane in range(2):
        for half in range(2):
            rows = slice(half * 256, half * 256 + 256)
            br, bi = basis[0, rows], basis[1, rows]
            if plane == 0:
                value = dot(br, flat[:, 0:F]) + dot(bi, flat[:, F:])
            else:
                value = dot(br, flat[:, F:]) - dot(bi, flat[:, 0:F])
            out[plane, rows] = value.astype(BF16)
            copies.append(
                pltpu.make_async_copy(out.at[plane, rows], out_h.at[plane, rows], sems.at[plane, half])
            )
            copies[-1].start()
    for copy in copies:
        copy.wait()


SMEM_SPEC = pl.BlockSpec(memory_space=pltpu.SMEM)
VMEM_SPEC = pl.BlockSpec(memory_space=pltpu.VMEM)
HBM_SPEC = pl.BlockSpec(memory_space=pltpu.HBM)
DMA = pltpu.SemaphoreType.DMA


def per_device(facets, facet_offsets, subgrid_offsets, w_terms, tile_count, tile_offsets, observed):
    n = lax.axis_size("facet")
    quads = n // 4
    soff_t, toff_t = subgrid_offsets.T, tile_offsets.T
    slots = observed.shape[0]
    basis_np = basis_table()
    basis = jnp.asarray(basis_np)
    br, bi = basis_np[:, :M]
    turned = jnp.asarray(np.block([[br, -bi], [bi, br]]))
    real, imag = padding_table(n)
    pad = jnp.asarray(np.concatenate([real, imag], axis=1))
    pad_t = jnp.asarray(np.block([[real.T, imag.T], [-imag.T, real.T]]))
    taper = jnp.asarray(taper_square())
    smooth_np = smooth_table()
    smooth, smooth_t = jnp.asarray(smooth_np), jnp.asarray(np.ascontiguousarray(smooth_np.T))
    ker_np = kernel_table()
    ker, ker_t = jnp.asarray(ker_np), jnp.asarray(np.ascontiguousarray(ker_np.T))
    plain = pltpu.CompilerParams(vmem_limit_bytes=LIMIT)

    deep = SG + 8 * slots
    piece_shape = (2, M, M)
    in_hbm = [
        pltpu.with_memory_space_constraint(x, pltpu.HBM)
        for x in (facet_offsets, soff_t, toff_t, facets[0], basis, taper, smooth, smooth_t)
    ]
    summed, screen, wide, wide_t = pl.pallas_call(
        functools.partial(forward_kernel, n, slots),
        out_shape=(
            jax.ShapeDtypeStruct((2, M, M), F32), jax.ShapeDtypeStruct((2, SG, SG), F32),
            jax.ShapeDtypeStruct((deep, SG), BF16), jax.ShapeDtypeStruct((SG, deep), BF16),
        ),
        in_specs=[SMEM_SPEC] + [HBM_SPEC] * 8,
        out_specs=(VMEM_SPEC,) * 4,
        scratch_shapes=[
            VMEM((2, F, F), BF16), VMEM((2, WIDE // M, WIDE, M), F32), VMEM((2, M, M), F32),
            pltpu.SMEM((1, 2), jnp.int32), pltpu.SMEM((2, n), jnp.int32),
            pltpu.SMEM((2, slots), jnp.int32),
            VMEM((2, F, F), BF16), VMEM((2, F, F), BF16), VMEM((M, M), F32),
            *[VMEM((2, quads, *piece_shape), BF16)] * 3,
            *[VMEM((quads, *piece_shape), BF16)] * 4, VMEM((quads // 2, *piece_shape), BF16),
            DMA((8,)), *[DMA((2, quads))] * 2, *[DMA((quads, 2))] * 5, DMA((quads // 2, 2)),
        ],
        compiler_params=pltpu.CompilerParams(
            vmem_limit_bytes=LIMIT, collective_id=0, has_side_effects=True
        ),
        name="forward",
    )(w_terms, *in_hbm)

    residual, coefficient = pl.pallas_call(
        functools.partial(subgrid_kernel, slots),
        out_shape=(
            jax.ShapeDtypeStruct((slots, 2, TV, TV), BF16),
            jax.ShapeDtypeStruct((2, M, M), BF16),
        ),
        in_specs=[SMEM_SPEC, HBM_SPEC] + [VMEM_SPEC] * 9,
        out_specs=(HBM_SPEC, VMEM_SPEC),
        scratch_shapes=[
            VMEM((SG, 2 * M), BF16), VMEM((SG, 2 * SG), BF16),
            VMEM((2, SG // 128, deep, 128), F32), VMEM((2, SG // 128, deep, 128), F32),
            VMEM((slots, 2, TV, TV), BF16),
            pltpu.SMEM((2, slots), jnp.int32), DMA((slots // GROUP,)), DMA,
        ],
        compiler_params=plain,
        name="subgrid",
    )(tile_count, in_hbm[2], summed, screen, wide, wide_t, pad, pad_t, ker, ker_t, observed)

    pieces = pl.pallas_call(
        functools.partial(gather_kernel, n),
        out_shape=jax.ShapeDtypeStruct((n, M, 2 * F), BF16),
        in_specs=[VMEM_SPEC, HBM_SPEC, HBM_SPEC, VMEM_SPEC, VMEM_SPEC],
        out_specs=VMEM_SPEC,
        scratch_shapes=[
            VMEM((n, 2, M, M), BF16), VMEM((2, M, M), F32),
            pltpu.SMEM((1, 2), jnp.int32), pltpu.SMEM((2, n), jnp.int32),
            *[DMA((2, quads, 2))] * 2, *[DMA((quads, 2))] * 2, DMA((2 * quads, 2)), DMA((quads, 2)), DMA, DMA((2,)),
        ],
        compiler_params=pltpu.CompilerParams(
            vmem_limit_bytes=LIMIT, collective_id=1, has_side_effects=True
        ),
        name="gather",
    )(coefficient, in_hbm[0], in_hbm[1], taper, turned)

    update = pl.pallas_call(
        functools.partial(backward_kernel, n),
        out_shape=jax.ShapeDtypeStruct((2, F, F), BF16),
        in_specs=[SMEM_SPEC, VMEM_SPEC, VMEM_SPEC],
        out_specs=HBM_SPEC,
        scratch_shapes=[
            VMEM((2, F // M, WIDE, M), F32), VMEM((F, 2 * F), BF16), VMEM((2, F, F), BF16), DMA((2, 2)),
        ],
        compiler_params=plain,
        name="backward",
    )(soff_t, pieces, basis)
    return (residual, update[None])


def solution(mesh):
    placed = (
        P(("groups", "facet"), None, None, None),
        P(("groups", "facet"), None),
        P("groups", None),
        P(("groups", "facet")),
        P(("groups", "facet")),
        P(("groups", "facet"), None),
        P(("groups", "facet"), None, None, None),
    )
    return jax.shard_map(
        per_device,
        mesh=mesh,
        in_specs=placed,
        out_specs=(
            P(("groups", "facet"), None, None, None),
            P(("groups", "facet"), None, None, None),
        ),
        check_vma=False,
    )
```

```python
import functools
import math

import jax
import jax.numpy as jnp
import ml_dtypes
import numpy as np
from jax import lax
from jax.experimental import pallas as pl
from jax.experimental.pallas import tpu as pltpu
from jax.sharding import PartitionSpec as P

F = 512
M = 128
SG = 512
TV = 128
WIDE = F + M
GROUP = 4

BF16 = jnp.bfloat16
F32 = jnp.float32
TWO_PI = 2.0 * math.pi
MESH = pl.DeviceIdType.MESH
VMEM = pltpu.VMEM
MIB = 1024 * 1024


def basis_table():
    index = np.arange(F)
    angle = -TWO_PI * (index[:, None] * index[None, :] % F) / F
    scale = 1.0 / math.sqrt(F)
    return np.stack([np.cos(angle) * scale, np.sin(angle) * scale]).astype(ml_dtypes.bfloat16)


def padding_table(facet_count):
    angle = TWO_PI * (np.arange(SG)[:, None] * np.arange(M)[None, :] % SG) / SG
    scale = (M * math.sqrt(facet_count)) ** (-0.5)
    return np.stack([np.cos(angle) * scale, np.sin(angle) * scale]).astype(ml_dtypes.bfloat16)


def taper_square():
    taper = 0.6 + 0.4 * np.sin(math.pi * (np.arange(M) + 0.5) / M)
    return (taper[:, None] * taper[None, :]).astype(np.float32)


def dot(left, right):
    return jnp.dot(left, right, preferred_element_type=F32)


def cos_sin_turns(turns):
    quarter = jnp.floor(turns * 4.0 + 0.5)
    y = (turns - quarter * 0.25) * TWO_PI
    y2 = y * y
    sine = y * (1.0 + y2 * (-1.0 / 6 + y2 * (1.0 / 120 + y2 * (-1.0 / 5040 + y2 * (1.0 / 362880)))))
    cosine = 1.0 + y2 * (
        -0.5 + y2 * (1.0 / 24 + y2 * (-1.0 / 720 + y2 * (1.0 / 40320 - y2 * (1.0 / 3628800))))
    )
    which = quarter.astype(jnp.int32) & 3
    odd = (which & 1) == 1
    first = jnp.where(odd, sine, cosine)
    second = jnp.where(odd, cosine, sine)
    cos_value = jnp.where((which == 1) | (which == 2), -first, first)
    sin_value = jnp.where(which >= 2, -second, second)
    return cos_value, sin_value


def tapered_phase(offset_ref, taper_ref):
    rows = lax.broadcasted_iota(jnp.int32, (M, M), 0)
    columns = lax.broadcasted_iota(jnp.int32, (M, M), 1)
    total = (rows * offset_ref[0, 0] + columns * offset_ref[0, 1]) & (F - 1)
    cos_value, sin_value = cos_sin_turns(total.astype(F32) * (1.0 / F))
    taper = taper_ref[...]
    return cos_value * taper, sin_value * taper


def place(n):
    me = lax.axis_index("facet")
    quads = n // 4
    far_first = [1 + (t + quads // 2 - 1) % (quads - 1) for t in range(quads - 1)]
    return quads, me // 4, lax.rem(me // 2, 2), lax.rem(me, 2), far_first


def index(quad, middle, core):
    return quad * 4 + middle * 2 + core


def greet(peers):
    barrier = pltpu.get_barrier_semaphore()
    for peer in peers:
        pl.semaphore_signal(barrier, inc=1, device_id={"facet": peer}, device_id_type=MESH)
    pl.semaphore_wait(barrier, len(peers))


def send(src, dst, send_sem, recv_sem, peer):
    return pltpu.make_async_remote_copy(
        src_ref=src, dst_ref=dst, send_sem=send_sem, recv_sem=recv_sem,
        device_id={"facet": peer}, device_id_type=MESH,
    )


def fill_screen(w_value, screen):
    @pl.loop(0, 4)
    def _(c):
        rows = pl.ds(pl.multiple_of(c * 128, 128), 128)
        u = (lax.broadcasted_iota(jnp.int32, (128, SG), 0) + (c * 128 - 256)).astype(F32)
        v = (lax.broadcasted_iota(jnp.int32, (128, SG), 1) - 256).astype(F32)
        radius = (u * u + v * v) * (1.0 / (SG * SG))
        cos_value, sin_value = cos_sin_turns(w_value * (jnp.sqrt(1.0 + radius) - 1.0))
        screen[0, rows, :] = cos_value
        screen[1, rows, :] = sin_value


def tap_values():
    taps = np.arange(5, dtype=np.float32)
    value = 0.75 * np.exp(-(taps / 1.5) * (taps / 1.5))
    return [float(x) for x in value.astype(ml_dtypes.bfloat16).astype(np.float32)]


def smooth_table():
    order = np.concatenate([np.arange(0, SG, 2), np.arange(1, SG, 2)])
    distance = np.abs(np.arange(SG)[None, :] - order[:, None])
    taps = np.array(tap_values() + [0.0], np.float32)
    return taps[np.minimum(distance, 5)].astype(ml_dtypes.bfloat16)


def kernel_table():
    distance = np.abs(np.arange(2 * TV)[None, :] - 2 * np.arange(TV)[:, None] - 1)
    taps = np.array(tap_values() + [0.0], np.float32)
    return taps[np.minimum(distance, 5)].astype(ml_dtypes.bfloat16)


def edge_values(position, offset, spot):
    i = spot & 7
    slot = jnp.where(i < 2, i, i + (TV - 8))
    distance = jnp.abs(position - offset - 2 * slot - 1)
    value = jnp.zeros(distance.shape, F32)
    for step, tap in enumerate(tap_values()):
        value = jnp.where(distance == step, tap, value)
    inside = (position >= offset) & (position < offset + 2 * TV) & ((i < 2) | (i >= 6))
    return jnp.where(inside, value, 0.0).astype(BF16)


def fill_rows(slots, toff, wide, wide_t):
    @pl.loop(0, slots // 2)
    def _(c):
        spot = lax.broadcasted_iota(jnp.int32, (16, SG), 0)
        lane = lax.broadcasted_iota(jnp.int32, (16, SG), 1)
        offset = jnp.where(spot < 8, toff[0, 2 * c], toff[0, 2 * c + 1])
        wide[pl.ds(pl.multiple_of(SG + c * 16, 16), 16), :] = edge_values(lane, offset, spot)

    lane = lax.broadcasted_iota(jnp.int32, (1, 8 * slots), 1)
    offset = jnp.zeros_like(lane)
    for t in range(slots):
        offset = jnp.where(lane >> 3 == t, toff[0, t], offset)

    @pl.loop(0, SG // 64)
    def _(c):
        position = lax.broadcasted_iota(jnp.int32, (64, 8 * slots), 0) + c * 64
        spot = lax.broadcasted_iota(jnp.int32, (64, 8 * slots), 1)
        wide_t[pl.ds(pl.multiple_of(c * 64, 64), 64), SG:] = edge_values(position, offset, spot)


def forward_kernel(
    n, slots, w_ref, foff_h, soff_h, toff_h, facet_h, basis_h, taper_h, smooth_h, smooth_t_h,
    pad_h, pad_t_h, ker_h, ker_t_h, turned_h, observed_h,
    summed, screen, wide, wide_t, basis, taper, pad, pad_t, ker, ker_t, turned, observed,
    half, spec, phase, foff, soff, toff, facet,
    outgoing, own, near, pair, mid, quad_sum, relay, far,
    load_s, near_s, near_r, mid_s, mid_r, relay_s, relay_r, far_s, far_r
):
    pairs = (
        (foff_h, foff), (taper_h, taper), (basis_h, basis), (facet_h, facet), (soff_h, soff),
        (toff_h, toff), (smooth_h, wide.at[0:SG]), (smooth_t_h, wide_t.at[:, 0:SG]), (observed_h, observed),
        (pad_h, pad), (pad_t_h, pad_t), (ker_h, ker), (ker_t_h, ker_t), (turned_h, turned),
    )
    loads = [pltpu.make_async_copy(src, dst, load_s.at[i]) for i, (src, dst) in enumerate(pairs)]
    for load in loads[:6]:
        load.start()

    quads = n // 4
    me = lax.axis_index("facet")
    quad, middle, core = me // 4, lax.rem(me // 2, 2), lax.rem(me, 2)
    other, odd, group = 1 - middle, lax.rem(quad, 2), quad // 2
    mate = quad + 1 - 2 * odd
    sibling, beside = index(quad, middle, 1 - core), index(quad, other, core)
    high = quad // (quads // 2)
    inner_side = jnp.where(high == odd, 0, 1)

    def turn(k):
        spot = quads - 2 - inner_side
        far_k = jnp.where(k > spot, k - 1, k)
        down = quads - 1 - far_k
        down = jnp.where(down < 2 * group + 2, down - 2, down)
        up = jnp.where(far_k >= 2 * group, far_k + 2, far_k)
        j = jnp.where(k == spot, mate, jnp.where(high == 1, up, down))
        return jnp.where(k == quads - 1, quad, j)

    barrier = pltpu.get_barrier_semaphore()
    peers = [index(lax.rem(quad + k, quads), middle, core) for k in range(1, quads)] + [beside, sibling]
    for peer in peers:
        pl.semaphore_signal(barrier, inc=1, device_id={"facet": peer}, device_id_type=MESH)

    loads[0].wait()
    loads[1].wait()
    phase[0], phase[1] = tapered_phase(foff, taper)
    lanes = lax.broadcasted_iota(jnp.int32, (M, M), 1)
    loads[2].wait()
    loads[3].wait()
    for load in loads[6:]:
        load.start()

    @pl.loop(0, 2)
    def _(c):
        cols = pl.ds(pl.multiple_of(c * 256, 256), 256)
        br, bi = basis[0, :, cols], basis[1, :, cols]
        half[0, :, cols] = (dot(facet[0], br) - dot(facet[1], bi)).astype(BF16)
        half[1, :, cols] = (dot(facet[0], bi) + dot(facet[1], br)).astype(BF16)

    @pl.loop(0, 2)
    def _(c):
        cols = pl.ds(pl.multiple_of(c * 256, 256), 256)
        hr, hi = half[0, :, cols], half[1, :, cols]
        real = dot(basis[0], hr) - dot(basis[1], hi)
        imag = dot(basis[0], hi) + dot(basis[1], hr)
        for side in range(2):
            part = slice(side * M, side * M + M)
            for plane, value in enumerate((real, imag)):
                spec[plane, c * 2 + side, 0:F] = value[:, part]
                spec[plane, c * 2 + side, F:WIDE] = value[0:M, part]

    spec[:, F // M] = spec[:, 0]
    loads[4].wait()

    def cut(s, target, where):
        sx, sy = soff[0, s], soff[1, s]
        tile, offset = sy >> 7, sy & 127
        rows = pl.ds(sx, M)

        def window(plane):
            value = jnp.where(lanes >= offset, spec[plane, tile, rows], spec[plane, tile + 1, rows])
            return pltpu.roll(value, (M - offset) & 127, 1)

        real, imag = window(0), window(1)
        pc, ps = phase[0], phase[1]
        target[where[0], where[1], 0] = (pc * real - ps * imag).astype(BF16)
        target[where[0], where[1], 1] = (pc * imag + ps * real).astype(BF16)

    def near_copy(h, j):
        return send(outgoing.at[h, j], near.at[h, j], near_s.at[h, j], near_r.at[h, j], sibling)

    def mid_copy(j, p):
        return send(pair.at[j, p], mid.at[j, p], mid_s.at[j, p], mid_r.at[j, p], beside)

    def relay_copy(j, p):
        return send(
            quad_sum.at[j, p], relay.at[j, p], relay_s.at[j, p], relay_r.at[j, p], index(mate, middle, core)
        )

    def far_copy(j, slot, p):
        return send(quad_sum.at[j, p], far.at[slot, p], far_s.at[j, p], far_r.at[slot, p], index(j, middle, core))

    def is_mate(j):
        return j == mate

    def is_gate(j):
        return (j != mate) & (odd == jnp.where(j > quad, 1, 0))

    def is_outer(j):
        return (j != mate) & (odd != jnp.where(j > quad, 1, 0))

    def near_sum(h, j, p):
        return own[h, j, p].astype(F32) + near[h, j, p].astype(F32)

    def mid_sum(j, p):
        return near_sum(1, j, p) + mid[j, p].astype(F32)

    pl.semaphore_wait(barrier, len(peers))

    @pl.loop(0, quads)
    def _(k):
        j = turn(k)
        cut(index(j, other, 1 - core), outgoing, (0, j))
        near_copy(0, j).start()

    @pl.loop(0, quads)
    def _(k):
        j = turn(k)
        cut(index(j, other, core), own, (0, j))

    @pl.loop(0, quads)
    def _(k):
        j = turn(k)
        near_copy(0, j).wait_recv()
        for p in range(2):
            pair[j, p] = near_sum(0, j, p).astype(BF16)
            mid_copy(j, p).start()

    @pl.loop(0, quads)
    def _(k):
        j = turn(k)
        cut(index(j, middle, 1 - core), outgoing, (1, j))
        near_copy(1, j).start()

    @pl.loop(0, quads)
    def _(k):
        j = turn(k)
        cut(index(j, middle, core), own, (1, j))

    fill_screen(w_ref[0], screen)

    @pl.loop(0, quads - 1)
    def _(k):
        j = turn(k)
        near_copy(1, j).wait_recv()
        for p in range(2):
            mid_copy(j, p).wait_recv()

            @pl.when(is_gate(j))
            def _():
                relay_copy(j, p).wait_recv()
                quad_sum[j, p] = (mid_sum(j, p) + relay[j, p].astype(F32)).astype(BF16)
                far_copy(j, group, p).start()

            @pl.when(is_mate(j))
            def _():
                quad_sum[j, p] = mid_sum(j, p).astype(BF16)
                far_copy(j, group, p).start()

            @pl.when(is_outer(j))
            def _():
                quad_sum[j, p] = mid_sum(j, p).astype(BF16)
                relay_copy(j, p).start()

    loads[5].wait()
    fill_rows(slots, toff, wide, wide_t)
    near_copy(1, quad).wait_recv()
    for p in range(2):
        mid_copy(quad, p).wait_recv()
        summed[p] = mid_sum(quad, p)
    for step in range(quads // 2):
        slot = lax.rem(group + step, quads // 2)
        for p in range(2):
            far_copy(quad, slot, p).wait_recv()
            summed[p] += far[slot, p].astype(F32)
    for load in loads[6:]:
        load.wait()

    @pl.loop(0, quads)
    def _(k):
        j = turn(k)
        near_copy(0, j).wait_send()
        near_copy(1, j).wait_send()
        for p in range(2):
            mid_copy(j, p).wait_send()

    @pl.loop(0, quads - 1)
    def _(k):
        j = turn(k)
        for p in range(2):

            @pl.when(is_outer(j))
            def _():
                relay_copy(j, p).wait_send()

            @pl.when(jnp.logical_not(is_outer(j)))
            def _():
                far_copy(j, group, p).wait_send()


def subgrid_kernel(
    slots, count_ref, toff_h, summed, screen, wide, wide_t, pad, pad_t, ker, ker_t, observed,
    residual_h, coefficient, inner, model, grid, spread, sent, toff, sems, load_s
):
    load = pltpu.make_async_copy(toff_h, toff, load_s)
    load.start()
    groups = slots // GROUP
    sr, si = summed[0], summed[1]
    stacked = jnp.concatenate(
        [jnp.concatenate([sr, si], axis=1), jnp.concatenate([-si, sr], axis=1)], axis=0
    ).astype(BF16)
    inner[...] = dot(pad[...], stacked).astype(BF16)

    for c in range(2):
        cols = slice(c * 256, c * 256 + 256)
        late = slice(SG + c * 256, SG + c * 256 + 256)
        real, imag = dot(inner[...], pad_t[:, cols]), dot(inner[...], pad_t[:, late])
        cos_value, sin_value = screen[0, :, cols], screen[1, :, cols]
        model[:, cols] = (cos_value * real - sin_value * imag).astype(BF16)
        model[:, late] = (cos_value * imag + sin_value * real).astype(BF16)

    for plane in range(2):
        for c in range(2):
            start = plane * SG + c * 256
            value = dot(wide[...], model[:, start : start + 256])
            for side in range(2):
                grid[plane, c * 2 + side] = value[:, side * 128 : side * 128 + 128]
                spread[plane, c * 2 + side] = jnp.zeros(spread.shape[2:], F32)

    load.wait()
    count = count_ref[0]
    lanes = lax.broadcasted_iota(jnp.int32, (TV, TV), 1)
    subs = lax.broadcasted_iota(jnp.int32, (8, TV), 0)
    top, bottom = subs < 2, subs >= 6

    def out_copy(step):
        tiles = pl.ds(step * GROUP, GROUP)
        return pltpu.make_async_copy(sent.at[tiles], residual_h.at[tiles], sems.at[step])

    filled = (count + GROUP - 1) // GROUP

    @pl.loop(0, filled)
    def _(step):
        slot = [step * GROUP + g for g in range(GROUP)]
        spots, left = [], []
        for t in slot:
            ou, ov = toff[0, t] + 1, toff[1, t]
            rows = pl.ds((ou & 1) * (SG // 2) + (ou >> 1), TV)
            tail = pl.ds(pl.multiple_of(SG + t * 8, 8), 8)
            first, turn = ov >> 7, ov & 127
            tiles = (first, first + 1, jnp.minimum(first + 2, SG // 128 - 1))
            spots.append((rows, tail, tiles, turn))

            def pick(plane, where_rows, size):
                keep = lanes[0:size] >= turn
                part = [grid[plane, k, where_rows] for k in tiles]
                both = [jnp.where(keep, part[k], part[k + 1]) for k in range(2)]
                return jnp.concatenate([pltpu.roll(x, (TV - turn) & 127, 1) for x in both], axis=1)

            for plane in range(2):
                body, edge = pick(plane, rows, TV), pick(plane, tail, 8)
                wide_top = jnp.concatenate([top, top], axis=1)
                wide_bottom = jnp.concatenate([bottom, bottom], axis=1)
                left.append(
                    jnp.concatenate(
                        [
                            jnp.where(wide_top, edge, body[0:8]), body[8 : TV - 8],
                            jnp.where(wide_bottom, edge, body[TV - 8 :]),
                        ],
                        axis=0,
                    ).astype(BF16)
                )
        rest = []
        for g, t in enumerate(slot):
            for plane in range(2):
                predicted = dot(left[g * 2 + plane], ker_t[...])
                value = (observed[t, plane].astype(F32) - predicted).astype(BF16)
                rest.append(jnp.where(t < count, value, jnp.zeros_like(value)))
                sent[t, plane] = rest[-1]
        out_copy(step).start()
        back = [dot(value, ker[...]).astype(BF16).astype(F32) for value in rest]
        for g in range(GROUP):
            rows, tail, tiles, turn = spots[g]
            keep = lanes >= turn
            for plane in range(2):
                value = back[g * 2 + plane]
                one, two = pltpu.roll(value[:, 0:128], turn, 1), pltpu.roll(value[:, 128:], turn, 1)
                blank = jnp.zeros((TV, TV), F32)
                parts = (jnp.where(keep, one, blank), jnp.where(keep, two, one), jnp.where(keep, blank, two))
                for tile, part in zip(tiles, parts):
                    zero = blank[0:8]
                    edge = jnp.where(top, part[0:8], jnp.where(bottom, part[TV - 8 :], zero))
                    body = jnp.concatenate(
                        [jnp.where(top, zero, part[0:8]), part[8 : TV - 8], jnp.where(bottom, zero, part[TV - 8 :])],
                        axis=0,
                    )
                    spread[plane, tile, rows] += body
                    spread[plane, tile, tail] += edge

    @pl.loop(filled, groups)
    def _(step):
        for g in range(GROUP):
            sent[step * GROUP + g] = jnp.zeros(sent.shape[1:], BF16)
        out_copy(step).start()

    for c in range(2):
        cols = slice(c * 256, c * 256 + 256)
        late = slice(SG + c * 256, SG + c * 256 + 256)
        ar, ai = [
            dot(wide_t[...], jnp.concatenate([spread[p, 2 * c], spread[p, 2 * c + 1]], axis=1).astype(BF16))
            for p in range(2)
        ]
        sc, ss = screen[0, :, cols], screen[1, :, cols]
        model[:, cols] = (sc * ar + ss * ai).astype(BF16)
        model[:, late] = (sc * ai - ss * ar).astype(BF16)
    reduced = (
        dot(pad_t[:, 0:SG], model[:, 0:SG]) + dot(pad_t[:, SG:], model[:, SG:])
    ).astype(BF16)
    both = dot(reduced, pad[...])
    coefficient[0] = (both[0:M, 0:M] + both[M:, M:]).astype(BF16)
    coefficient[1] = (both[M:, 0:M] - both[0:M, M:]).astype(BF16)

    @pl.loop(0, groups)
    def _(step):
        out_copy(step).wait()


def gather_kernel(
    n, mine, foff_h, soff_h, taper, turned, out, arrived, phase, foff, soff,
    near_s, near_r, mid_s, mid_r, far_s, far_r, local, load_s
):
    quads = n // 4
    me = lax.axis_index("facet")
    quad, middle, core = me // 4, lax.rem(me // 2, 2), lax.rem(me, 2)
    other, odd, group = 1 - middle, lax.rem(quad, 2), quad // 2
    mate = quad + 1 - 2 * odd
    sibling, beside = index(quad, middle, 1 - core), index(quad, other, core)
    loads = [pltpu.make_async_copy(foff_h, foff, load_s.at[0]), pltpu.make_async_copy(soff_h, soff, load_s.at[1])]
    for load in loads:
        load.start()

    barrier = pltpu.get_barrier_semaphore()
    peers = [index(lax.rem(quad + k, quads), middle, core) for k in range(1, quads)] + [beside, sibling]
    for peer in peers:
        pl.semaphore_signal(barrier, inc=1, device_id={"facet": peer}, device_id_type=MESH)
    pl.semaphore_wait(barrier, len(peers))

    low = quad < quads // 2
    gate_side = jnp.where(low == (odd == 1), 1, 0)

    def turn(k):
        far_k = quads - 2 - jnp.where(k > gate_side, k, k + 1)
        down = quads - 1 - far_k
        down = jnp.where(down < 2 * group + 2, down - 2, down)
        up = jnp.where(far_k >= 2 * group, far_k + 2, far_k)
        return jnp.where(k == gate_side, mate, jnp.where(low, down, up))

    def event(i):
        return jnp.where(i == 0, quad, turn(i - 1))

    def is_gate(j):
        return (j != mate) & (odd == jnp.where(j > quad, 1, 0))

    def far_copy(source, slot, to, p):
        spot = index(slot, middle, core)
        return send(source.at[p], arrived.at[spot, p], far_s.at[to, p], far_r.at[slot, p], index(to, middle, core))

    def relay_copy(j, p):
        spot = index(j, middle, core)
        return send(
            arrived.at[spot, p], arrived.at[spot, p], far_s.at[quads + j, p], far_r.at[j, p],
            index(mate, middle, core),
        )

    def mid_copy(j, h, p):
        piece = arrived.at[index(j, h, core), p]
        return send(piece, piece, mid_s.at[j, p], mid_r.at[j, p], beside)

    def near_copy(h, j, side, p):
        piece = arrived.at[index(j, h, side), p]
        return send(piece, piece, near_s.at[h, j, p], near_r.at[h, j, p], sibling)

    def mid_own(p):
        return send(mine.at[p], arrived.at[me, p], mid_s.at[quad, p], mid_r.at[quad, p], beside)

    def near_own(p):
        return send(
            mine.at[p], arrived.at[me, p], near_s.at[middle, quad, p], near_r.at[middle, quad, p], sibling
        )

    def far_target(i):
        return jnp.where(i >= group, i + 1, i)

    def first_hop(i):
        g = far_target(i)
        return 2 * g + jnp.where(g < group, 1, 0)

    own = pltpu.make_async_copy(mine, arrived.at[me], local)
    own.start()
    for p in range(2):
        mid_own(p).start()
    for i in range(quads // 2 - 1):
        for p in range(2):
            far_copy(mine, quad, first_hop(i), p).start()
    for p in range(2):
        far_copy(mine, quad, mate, p).start()
        near_own(p).start()

    for load in loads:
        load.wait()
    phase[0], phase[1] = tapered_phase(foff, taper)
    own.wait()

    def transform(spot):
        pc, ps = phase[0], phase[1]
        real, imag = arrived[spot, 0].astype(F32), arrived[spot, 1].astype(F32)
        both = jnp.concatenate([pc * real + ps * imag, pc * imag - ps * real], axis=1).astype(BF16)
        lane = lax.broadcasted_iota(jnp.int32, (8, F), 1)
        cos_value, sin_value = cos_sin_turns(((lane * soff[1, spot]) & (F - 1)).astype(F32) * (1.0 / F))
        for c in range(F // 256):
            cols, late = slice(c * 256, c * 256 + 256), slice(F + c * 256, F + c * 256 + 256)
            real = dot(both, turned[:, cols]).reshape(M // 8, 8, 256)
            imag = dot(both, turned[:, late]).reshape(M // 8, 8, 256)
            cv, sv = cos_value[None, :, cols], sin_value[None, :, cols]
            out[spot, :, cols] = (cv * real - sv * imag).reshape(M, 256).astype(BF16)
            out[spot, :, late] = (cv * imag + sv * real).reshape(M, 256).astype(BF16)

    transform(me)

    def take_far(j):
        for p in range(2):
            far_copy(mine, j, j, p).wait_recv()

            @pl.when(is_gate(j))
            def _():
                relay_copy(j, p).start()

            mid_copy(j, middle, p).start()
            near_copy(middle, j, core, p).start()

    def take_mid(j):
        for p in range(2):
            mid_copy(j, other, p).wait_recv()
            near_copy(other, j, core, p).start()

    def wait_near(h, j):
        for p in range(2):
            near_copy(h, j, 1 - core, p).wait_recv()

    first, last = event(1), event(quads - 1)
    take_far(first)
    take_mid(quad)
    wait_near(middle, quad)
    transform(index(first, middle, core))
    transform(index(quad, other, core))
    transform(sibling)

    @pl.loop(2, quads)
    def _(i):
        j, before, earlier = event(i), event(i - 1), event(i - 2)
        take_far(j)
        take_mid(before)
        wait_near(middle, before)
        wait_near(other, earlier)
        transform(index(j, middle, core))
        transform(index(before, other, core))
        transform(index(before, middle, 1 - core))
        transform(index(earlier, other, 1 - core))

    take_mid(last)
    wait_near(middle, last)
    wait_near(other, event(quads - 2))
    transform(index(last, other, core))
    transform(index(last, middle, 1 - core))
    transform(index(event(quads - 2), other, 1 - core))
    wait_near(other, last)
    transform(index(last, other, 1 - core))

    for p in range(2):
        mid_own(p).wait_send()
        near_own(p).wait_send()
        far_copy(mine, quad, mate, p).wait_send()
        near_copy(other, quad, core, p).wait_send()
        for i in range(quads // 2 - 1):
            far_copy(mine, quad, first_hop(i), p).wait_send()

    @pl.loop(0, quads - 1)
    def _(k):
        j = turn(k)
        for p in range(2):
            mid_copy(j, middle, p).wait_send()
            near_copy(middle, j, core, p).wait_send()
            near_copy(other, j, core, p).wait_send()

            @pl.when(is_gate(j))
            def _():
                relay_copy(j, p).wait_send()


def backward_kernel(n, soff, pieces, basis, out_h, acc, flat, out, sems):
    acc[...] = jnp.zeros_like(acc)

    @pl.loop(0, n, unroll=2)
    def _(s):
        rows = pl.ds(soff[0, s], M)
        for plane in range(2):
            for k in range(F // M):
                acc[plane, k, rows] += pieces[s, :, plane * F + k * M : plane * F + k * M + M].astype(F32)

    for plane in range(2):
        for k in range(F // M):
            cols = slice(plane * F + k * M, plane * F + k * M + M)
            flat[0:M, cols] = (acc[plane, k, 0:M] + acc[plane, k, F:WIDE]).astype(BF16)
            flat[M:F, cols] = acc[plane, k, M:F].astype(BF16)

    copies = []
    for plane in range(2):
        for half in range(2):
            rows = slice(half * 256, half * 256 + 256)
            br, bi = basis[0, rows], basis[1, rows]
            if plane == 0:
                value = dot(br, flat[:, 0:F]) + dot(bi, flat[:, F:])
            else:
                value = dot(br, flat[:, F:]) - dot(bi, flat[:, 0:F])
            out[plane, rows] = value.astype(BF16)
            copies.append(
                pltpu.make_async_copy(out.at[plane, rows], out_h.at[plane, rows], sems.at[plane, half])
            )
            copies[-1].start()
    for copy in copies:
        copy.wait()


SMEM_SPEC = pl.BlockSpec(memory_space=pltpu.SMEM)
VMEM_SPEC = pl.BlockSpec(memory_space=pltpu.VMEM)
HBM_SPEC = pl.BlockSpec(memory_space=pltpu.HBM)
DMA = pltpu.SemaphoreType.DMA


def per_device(facets, facet_offsets, subgrid_offsets, w_terms, tile_count, tile_offsets, observed):
    n = lax.axis_size("facet")
    quads = n // 4
    soff_t, toff_t = subgrid_offsets.T, tile_offsets.T
    slots = observed.shape[0]
    basis_np = basis_table()
    basis = jnp.asarray(basis_np)
    br, bi = basis_np[:, :M]
    turned = jnp.asarray(np.block([[br, -bi], [bi, br]]))
    real, imag = padding_table(n)
    pad = jnp.asarray(np.concatenate([real, imag], axis=1))
    pad_t = jnp.asarray(np.block([[real.T, imag.T], [-imag.T, real.T]]))
    taper = jnp.asarray(taper_square())
    smooth_np = smooth_table()
    smooth, smooth_t = jnp.asarray(smooth_np), jnp.asarray(np.ascontiguousarray(smooth_np.T))
    ker_np = kernel_table()
    ker, ker_t = jnp.asarray(ker_np), jnp.asarray(np.ascontiguousarray(ker_np.T))
    plain = pltpu.CompilerParams(vmem_limit_bytes=24 * MIB)

    deep = SG + 8 * slots
    piece_shape = (2, M, M)
    tables = (basis, taper, smooth, smooth_t, pad, pad_t, ker, ker_t, turned)
    in_hbm = [
        pltpu.with_memory_space_constraint(x, pltpu.HBM)
        for x in (facet_offsets, soff_t, toff_t, facets[0], *tables, observed)
    ]
    held = (basis, taper, pad, pad_t, ker, ker_t, turned, observed)
    summed, screen, wide, wide_t, basis, taper, pad, pad_t, ker, ker_t, turned, observed = pl.pallas_call(
        functools.partial(forward_kernel, n, slots),
        out_shape=(
            jax.ShapeDtypeStruct((2, M, M), F32), jax.ShapeDtypeStruct((2, SG, SG), F32),
            jax.ShapeDtypeStruct((deep, SG), BF16), jax.ShapeDtypeStruct((SG, deep), BF16),
            *[jax.ShapeDtypeStruct(x.shape, x.dtype) for x in held],
        ),
        in_specs=[SMEM_SPEC] + [HBM_SPEC] * 14,
        out_specs=(VMEM_SPEC,) * 12,
        scratch_shapes=[
            VMEM((2, F, F), BF16), VMEM((2, WIDE // M, WIDE, M), F32), VMEM((2, M, M), F32),
            pltpu.SMEM((1, 2), jnp.int32), pltpu.SMEM((2, n), jnp.int32),
            pltpu.SMEM((2, slots), jnp.int32),
            VMEM((2, F, F), BF16),
            *[VMEM((2, quads, *piece_shape), BF16)] * 3,
            *[VMEM((quads, *piece_shape), BF16)] * 4, VMEM((quads // 2, *piece_shape), BF16),
            DMA((14,)), *[DMA((2, quads))] * 2, *[DMA((quads, 2))] * 5, DMA((quads // 2, 2)),
        ],
        compiler_params=pltpu.CompilerParams(
            vmem_limit_bytes=32 * MIB, collective_id=0, has_side_effects=True
        ),
        name="forward",
    )(w_terms, *in_hbm)

    residual, coefficient = pl.pallas_call(
        functools.partial(subgrid_kernel, slots),
        out_shape=(
            jax.ShapeDtypeStruct((slots, 2, TV, TV), BF16),
            jax.ShapeDtypeStruct((2, M, M), BF16),
        ),
        in_specs=[SMEM_SPEC, HBM_SPEC] + [VMEM_SPEC] * 9,
        out_specs=(HBM_SPEC, VMEM_SPEC),
        scratch_shapes=[
            VMEM((SG, 2 * M), BF16), VMEM((SG, 2 * SG), BF16),
            VMEM((2, SG // 128, deep, 128), F32), VMEM((2, SG // 128, deep, 128), F32),
            VMEM((slots, 2, TV, TV), BF16),
            pltpu.SMEM((2, slots), jnp.int32), DMA((slots // GROUP,)), DMA,
        ],
        compiler_params=plain,
        name="subgrid",
    )(tile_count, in_hbm[2], summed, screen, wide, wide_t, pad, pad_t, ker, ker_t, observed)

    pieces = pl.pallas_call(
        functools.partial(gather_kernel, n),
        out_shape=jax.ShapeDtypeStruct((n, M, 2 * F), BF16),
        in_specs=[VMEM_SPEC, HBM_SPEC, HBM_SPEC, VMEM_SPEC, VMEM_SPEC],
        out_specs=VMEM_SPEC,
        scratch_shapes=[
            VMEM((n, 2, M, M), BF16), VMEM((2, M, M), F32),
            pltpu.SMEM((1, 2), jnp.int32), pltpu.SMEM((2, n), jnp.int32),
            *[DMA((2, quads, 2))] * 2, *[DMA((quads, 2))] * 2, DMA((2 * quads, 2)), DMA((quads, 2)), DMA, DMA((2,)),
        ],
        compiler_params=pltpu.CompilerParams(
            vmem_limit_bytes=24 * MIB, collective_id=1, has_side_effects=True
        ),
        name="gather",
    )(coefficient, in_hbm[0], in_hbm[1], taper, turned)

    update = pl.pallas_call(
        functools.partial(backward_kernel, n),
        out_shape=jax.ShapeDtypeStruct((2, F, F), BF16),
        in_specs=[SMEM_SPEC, VMEM_SPEC, VMEM_SPEC],
        out_specs=HBM_SPEC,
        scratch_shapes=[
            VMEM((2, F // M, WIDE, M), F32), VMEM((F, 2 * F), BF16), VMEM((2, F, F), BF16), DMA((2, 2)),
        ],
        compiler_params=plain,
        name="backward",
    )(soff_t, pieces, basis)
    return (residual, update[None])


def solution(mesh):
    placed = (
        P(("groups", "facet"), None, None, None),
        P(("groups", "facet"), None),
        P("groups", None),
        P(("groups", "facet")),
        P(("groups", "facet")),
        P(("groups", "facet"), None),
        P(("groups", "facet"), None, None, None),
    )
    return jax.shard_map(
        per_device,
        mesh=mesh,
        in_specs=placed,
        out_specs=(
            P(("groups", "facet"), None, None, None),
            P(("groups", "facet"), None, None, None),
        ),
        check_vma=False,
    )
```

```python
import functools
import math

import jax
import jax.numpy as jnp
import ml_dtypes
import numpy as np
from jax import lax
from jax.experimental import pallas as pl
from jax.experimental.pallas import tpu as pltpu
from jax.sharding import PartitionSpec as P

F = 512
M = 128
SG = 512
TV = 128
WIDE = F + M
GROUP = 4

BF16 = jnp.bfloat16
F32 = jnp.float32
TWO_PI = 2.0 * math.pi
MESH = pl.DeviceIdType.MESH
VMEM = pltpu.VMEM
MIB = 1024 * 1024


def basis_table():
    index = np.arange(F)
    angle = -TWO_PI * (index[:, None] * index[None, :] % F) / F
    scale = 1.0 / math.sqrt(F)
    return np.stack([np.cos(angle) * scale, np.sin(angle) * scale]).astype(ml_dtypes.bfloat16)


def padding_table(facet_count):
    angle = TWO_PI * (np.arange(SG)[:, None] * np.arange(M)[None, :] % SG) / SG
    scale = (M * math.sqrt(facet_count)) ** (-0.5)
    return np.stack([np.cos(angle) * scale, np.sin(angle) * scale]).astype(ml_dtypes.bfloat16)


def taper_square():
    taper = 0.6 + 0.4 * np.sin(math.pi * (np.arange(M) + 0.5) / M)
    return (taper[:, None] * taper[None, :]).astype(np.float32)


def dot(left, right):
    return jnp.dot(left, right, preferred_element_type=F32)


def dot_t(left, right):
    return lax.dot_general(left, right, (((1,), (1,)), ((), ())), preferred_element_type=F32)


def cos_sin_turns(turns):
    quarter = jnp.floor(turns * 4.0 + 0.5)
    y = (turns - quarter * 0.25) * TWO_PI
    y2 = y * y
    sine = y * (1.0 + y2 * (-1.0 / 6 + y2 * (1.0 / 120 + y2 * (-1.0 / 5040 + y2 * (1.0 / 362880)))))
    cosine = 1.0 + y2 * (
        -0.5 + y2 * (1.0 / 24 + y2 * (-1.0 / 720 + y2 * (1.0 / 40320 - y2 * (1.0 / 3628800))))
    )
    which = quarter.astype(jnp.int32) & 3
    odd = (which & 1) == 1
    first = jnp.where(odd, sine, cosine)
    second = jnp.where(odd, cosine, sine)
    cos_value = jnp.where((which == 1) | (which == 2), -first, first)
    sin_value = jnp.where(which >= 2, -second, second)
    return cos_value, sin_value


def tapered_phase(offset_ref, taper_ref):
    rows = lax.broadcasted_iota(jnp.int32, (M, M), 0)
    columns = lax.broadcasted_iota(jnp.int32, (M, M), 1)
    total = (rows * offset_ref[0, 0] + columns * offset_ref[0, 1]) & (F - 1)
    cos_value, sin_value = cos_sin_turns(total.astype(F32) * (1.0 / F))
    taper = taper_ref[...]
    return cos_value * taper, sin_value * taper


def place(n):
    me = lax.axis_index("facet")
    quads = n // 4
    far_first = [1 + (t + quads // 2 - 1) % (quads - 1) for t in range(quads - 1)]
    return quads, me // 4, lax.rem(me // 2, 2), lax.rem(me, 2), far_first


def index(quad, middle, core):
    return quad * 4 + middle * 2 + core


def greet(peers):
    barrier = pltpu.get_barrier_semaphore()
    for peer in peers:
        pl.semaphore_signal(barrier, inc=1, device_id={"facet": peer}, device_id_type=MESH)
    pl.semaphore_wait(barrier, len(peers))


def send(src, dst, send_sem, recv_sem, peer):
    return pltpu.make_async_remote_copy(
        src_ref=src, dst_ref=dst, send_sem=send_sem, recv_sem=recv_sem,
        device_id={"facet": peer}, device_id_type=MESH,
    )


def fill_screen(w_value, screen):
    @pl.loop(0, 4)
    def _(c):
        rows = pl.ds(pl.multiple_of(c * 128, 128), 128)
        u = (lax.broadcasted_iota(jnp.int32, (128, SG), 0) + (c * 128 - 256)).astype(F32)
        v = (lax.broadcasted_iota(jnp.int32, (128, SG), 1) - 256).astype(F32)
        radius = (u * u + v * v) * (1.0 / (SG * SG))
        cos_value, sin_value = cos_sin_turns(w_value * (jnp.sqrt(1.0 + radius) - 1.0))
        screen[0, rows, :] = cos_value
        screen[1, rows, :] = sin_value


def tap_values():
    taps = np.arange(5, dtype=np.float32)
    value = 0.75 * np.exp(-(taps / 1.5) * (taps / 1.5))
    return [float(x) for x in value.astype(ml_dtypes.bfloat16).astype(np.float32)]


def smooth_table():
    order = np.concatenate([np.arange(0, SG, 2), np.arange(1, SG, 2)])
    distance = np.abs(np.arange(SG)[None, :] - order[:, None])
    taps = np.array(tap_values() + [0.0], np.float32)
    return taps[np.minimum(distance, 5)].astype(ml_dtypes.bfloat16)


def kernel_table():
    distance = np.abs(np.arange(2 * TV)[None, :] - 2 * np.arange(TV)[:, None] - 1)
    taps = np.array(tap_values() + [0.0], np.float32)
    return taps[np.minimum(distance, 5)].astype(ml_dtypes.bfloat16)


def edge_values(position, offset, spot):
    i = spot & 7
    slot = jnp.where(i < 2, i, i + (TV - 8))
    distance = jnp.abs(position - offset - 2 * slot - 1)
    value = jnp.zeros(distance.shape, F32)
    for step, tap in enumerate(tap_values()):
        value = jnp.where(distance == step, tap, value)
    inside = (position >= offset) & (position < offset + 2 * TV) & ((i < 2) | (i >= 6))
    return jnp.where(inside, value, 0.0).astype(BF16)


def fill_rows(slots, toff, wide, wide_t):
    @pl.loop(0, slots // 2)
    def _(c):
        spot = lax.broadcasted_iota(jnp.int32, (16, SG), 0)
        lane = lax.broadcasted_iota(jnp.int32, (16, SG), 1)
        offset = jnp.where(spot < 8, toff[0, 2 * c], toff[0, 2 * c + 1])
        wide[pl.ds(pl.multiple_of(SG + c * 16, 16), 16), :] = edge_values(lane, offset, spot)

    lane = lax.broadcasted_iota(jnp.int32, (1, 8 * slots), 1)
    offset = jnp.zeros_like(lane)
    for t in range(slots):
        offset = jnp.where(lane >> 3 == t, toff[0, t], offset)

    @pl.loop(0, SG // 64)
    def _(c):
        position = lax.broadcasted_iota(jnp.int32, (64, 8 * slots), 0) + c * 64
        spot = lax.broadcasted_iota(jnp.int32, (64, 8 * slots), 1)
        wide_t[pl.ds(pl.multiple_of(c * 64, 64), 64), SG:] = edge_values(position, offset, spot)


def forward_kernel(
    n, slots, w_ref, foff_h, soff_h, toff_h, facet_h, basis_h, taper_h, smooth_h, smooth_t_h,
    pad_h, pad_t_h, ker_h, ker_t_h, turned_h, observed_h,
    summed, screen, wide, wide_t, basis, taper, pad, pad_t, ker, ker_t, turned, observed, wave,
    spec, phase, foff, soff, toff, facet,
    outgoing, own, near, pair, mid, quad_sum, relay, far,
    load_s, near_s, near_r, mid_s, mid_r, relay_s, relay_r, far_s, far_r
):
    pairs = (
        (foff_h, foff), (taper_h, taper), (soff_h, soff), (basis_h, basis), (facet_h, facet),
        (toff_h, toff), (turned_h, turned), (smooth_h, wide.at[0:SG]), (smooth_t_h, wide_t.at[:, 0:SG]), (observed_h, observed),
        (pad_h, pad), (pad_t_h, pad_t), (ker_h, ker), (ker_t_h, ker_t),
    )
    loads = [pltpu.make_async_copy(src, dst, load_s.at[i]) for i, (src, dst) in enumerate(pairs)]
    for load in loads[:7]:
        load.start()

    quads = n // 4
    me = lax.axis_index("facet")
    quad, middle, core = me // 4, lax.rem(me // 2, 2), lax.rem(me, 2)
    other, odd, group = 1 - middle, lax.rem(quad, 2), quad // 2
    mate = quad + 1 - 2 * odd
    sibling, beside = index(quad, middle, 1 - core), index(quad, other, core)
    high = quad // (quads // 2)
    inner_side = jnp.where(high == odd, 0, 1)

    def turn(k):
        spot = quads - 2 - inner_side
        far_k = jnp.where(k > spot, k - 1, k)
        down = quads - 1 - far_k
        down = jnp.where(down < 2 * group + 2, down - 2, down)
        up = jnp.where(far_k >= 2 * group, far_k + 2, far_k)
        j = jnp.where(k == spot, mate, jnp.where(high == 1, up, down))
        return jnp.where(k == quads - 1, quad, j)

    barrier = pltpu.get_barrier_semaphore()
    peers = [index(lax.rem(quad + k, quads), middle, core) for k in range(1, quads)] + [beside, sibling]
    for peer in peers:
        pl.semaphore_signal(barrier, inc=1, device_id={"facet": peer}, device_id_type=MESH)

    loads[0].wait()
    loads[1].wait()
    phase[0], phase[1] = tapered_phase(foff, taper)
    loads[2].wait()
    lane = lax.broadcasted_iota(jnp.int32, (8, F), 1)

    @pl.loop(0, n, unroll=2)
    def _(s):
        turns = ((lane * soff[1, s]) & (F - 1)).astype(F32) * (1.0 / F)
        wave[s, 0], wave[s, 1] = cos_sin_turns(turns)

    loads[3].wait()
    loads[4].wait()
    for load in loads[7:]:
        load.start()

    @pl.loop(0, 2)
    def _(c):
        cols = pl.ds(pl.multiple_of(c * 256, 256), 256)
        xr, xi = facet[0, :, cols], facet[1, :, cols]
        real = dot(basis[0], xr) - dot(basis[1], xi)
        imag = dot(basis[0], xi) + dot(basis[1], xr)
        for side in range(2):
            part = slice(side * M, side * M + M)
            for plane, value in enumerate((real, imag)):
                spec[plane, c * 2 + side, 0:F] = value[:, part]
                spec[plane, c * 2 + side, F:WIDE] = value[0:M, part]

    loads[6].wait()

    def cut(s, target, where):
        rows = pl.ds(soff[0, s], M)
        real, imag = [], []
        for tile in range(F // M):
            part = slice(tile * M, tile * M + M)
            cv, sv = wave[s, 0, :, part][None], wave[s, 1, :, part][None]
            r = spec[0, tile, rows].reshape(M // 8, 8, M)
            i = spec[1, tile, rows].reshape(M // 8, 8, M)
            real.append((cv * r + sv * i).reshape(M, M).astype(BF16))
            imag.append((cv * i - sv * r).reshape(M, M).astype(BF16))
        both = dot_t(jnp.concatenate(real + imag, axis=1), turned[...])
        real, imag = both[:, 0:M], both[:, M:]
        pc, ps = phase[0], phase[1]
        target[where[0], where[1], 0] = (pc * real - ps * imag).astype(BF16)
        target[where[0], where[1], 1] = (pc * imag + ps * real).astype(BF16)

    def near_copy(h, j):
        return send(outgoing.at[h, j], near.at[h, j], near_s.at[h, j], near_r.at[h, j], sibling)

    def mid_copy(j, p):
        return send(pair.at[j, p], mid.at[j, p], mid_s.at[j, p], mid_r.at[j, p], beside)

    def relay_copy(j, p):
        return send(
            quad_sum.at[j, p], relay.at[j, p], relay_s.at[j, p], relay_r.at[j, p], index(mate, middle, core)
        )

    def far_copy(j, slot, p):
        return send(quad_sum.at[j, p], far.at[slot, p], far_s.at[j, p], far_r.at[slot, p], index(j, middle, core))

    def is_mate(j):
        return j == mate

    def is_gate(j):
        return (j != mate) & (odd == jnp.where(j > quad, 1, 0))

    def is_outer(j):
        return (j != mate) & (odd != jnp.where(j > quad, 1, 0))

    def near_sum(h, j, p):
        return own[h, j, p].astype(F32) + near[h, j, p].astype(F32)

    def mid_sum(j, p):
        return near_sum(1, j, p) + mid[j, p].astype(F32)

    pl.semaphore_wait(barrier, len(peers))

    def give(h, half, j):
        cut(index(j, half, 1 - core), outgoing, (h, j))
        near_copy(h, j).start()

    def keep(h, half, j):
        cut(index(j, half, core), own, (h, j))

    def pass_on(j):
        near_copy(0, j).wait_recv()
        for p in range(2):
            pair[j, p] = near_sum(0, j, p).astype(BF16)
            mid_copy(j, p).start()

    give(0, other, turn(0))
    keep(0, other, turn(0))

    @pl.loop(0, quads - 1)
    def _(k):
        give(0, other, turn(k + 1))
        pass_on(turn(k))
        keep(0, other, turn(k + 1))

    pass_on(turn(quads - 1))

    @pl.loop(0, quads)
    def _(k):
        give(1, middle, turn(k))
        keep(1, middle, turn(k))

    fill_screen(w_ref[0], screen)

    @pl.loop(0, quads - 1)
    def _(k):
        j = turn(k)
        near_copy(1, j).wait_recv()
        for p in range(2):
            mid_copy(j, p).wait_recv()

            @pl.when(is_gate(j))
            def _():
                relay_copy(j, p).wait_recv()
                quad_sum[j, p] = (mid_sum(j, p) + relay[j, p].astype(F32)).astype(BF16)
                far_copy(j, group, p).start()

            @pl.when(is_mate(j))
            def _():
                quad_sum[j, p] = mid_sum(j, p).astype(BF16)
                far_copy(j, group, p).start()

            @pl.when(is_outer(j))
            def _():
                quad_sum[j, p] = mid_sum(j, p).astype(BF16)
                relay_copy(j, p).start()

    loads[5].wait()
    fill_rows(slots, toff, wide, wide_t)
    near_copy(1, quad).wait_recv()
    for p in range(2):
        mid_copy(quad, p).wait_recv()
        summed[p] = mid_sum(quad, p)
    for step in range(quads // 2):
        slot = lax.rem(group + step, quads // 2)
        for p in range(2):
            far_copy(quad, slot, p).wait_recv()
            summed[p] += far[slot, p].astype(F32)
    for load in loads[7:]:
        load.wait()

    @pl.loop(0, quads)
    def _(k):
        j = turn(k)
        near_copy(0, j).wait_send()
        near_copy(1, j).wait_send()
        for p in range(2):
            mid_copy(j, p).wait_send()

    @pl.loop(0, quads - 1)
    def _(k):
        j = turn(k)
        for p in range(2):

            @pl.when(is_outer(j))
            def _():
                relay_copy(j, p).wait_send()

            @pl.when(jnp.logical_not(is_outer(j)))
            def _():
                far_copy(j, group, p).wait_send()


def subgrid_kernel(
    slots, count_ref, toff_h, summed, screen, wide, wide_t, pad, pad_t, ker, ker_t, observed,
    residual_h, coefficient, inner, model, grid, spread, sent, toff, sems, load_s
):
    load = pltpu.make_async_copy(toff_h, toff, load_s)
    load.start()
    groups = slots // GROUP
    sr, si = summed[0], summed[1]
    stacked = jnp.concatenate(
        [jnp.concatenate([sr, si], axis=1), jnp.concatenate([-si, sr], axis=1)], axis=0
    ).astype(BF16)
    inner[...] = dot(pad[...], stacked).astype(BF16)

    for c in range(2):
        cols = slice(c * 256, c * 256 + 256)
        late = slice(SG + c * 256, SG + c * 256 + 256)
        real, imag = dot(inner[...], pad_t[:, cols]), dot(inner[...], pad_t[:, late])
        cos_value, sin_value = screen[0, :, cols], screen[1, :, cols]
        model[:, cols] = (cos_value * real - sin_value * imag).astype(BF16)
        model[:, late] = (cos_value * imag + sin_value * real).astype(BF16)

    for plane in range(2):
        for c in range(2):
            start = plane * SG + c * 256
            value = dot(wide[...], model[:, start : start + 256])
            for side in range(2):
                grid[plane, c * 2 + side] = value[:, side * 128 : side * 128 + 128]
                spread[plane, c * 2 + side] = jnp.zeros(spread.shape[2:], F32)

    load.wait()
    count = count_ref[0]
    lanes = lax.broadcasted_iota(jnp.int32, (TV, TV), 1)
    subs = lax.broadcasted_iota(jnp.int32, (8, TV), 0)
    top, bottom = subs < 2, subs >= 6

    def out_copy(step):
        tiles = pl.ds(step * GROUP, GROUP)
        return pltpu.make_async_copy(sent.at[tiles], residual_h.at[tiles], sems.at[step])

    filled = (count + GROUP - 1) // GROUP

    @pl.loop(0, filled)
    def _(step):
        slot = [step * GROUP + g for g in range(GROUP)]
        spots, left = [], []
        for t in slot:
            ou, ov = toff[0, t] + 1, toff[1, t]
            rows = pl.ds((ou & 1) * (SG // 2) + (ou >> 1), TV)
            tail = pl.ds(pl.multiple_of(SG + t * 8, 8), 8)
            first, turn = ov >> 7, ov & 127
            tiles = (first, first + 1, jnp.minimum(first + 2, SG // 128 - 1))
            spots.append((rows, tail, tiles, turn))

            def pick(plane, where_rows, size):
                keep = lanes[0:size] >= turn
                part = [grid[plane, k, where_rows] for k in tiles]
                both = [jnp.where(keep, part[k], part[k + 1]) for k in range(2)]
                return jnp.concatenate([pltpu.roll(x, (TV - turn) & 127, 1) for x in both], axis=1)

            for plane in range(2):
                body, edge = pick(plane, rows, TV), pick(plane, tail, 8)
                wide_top = jnp.concatenate([top, top], axis=1)
                wide_bottom = jnp.concatenate([bottom, bottom], axis=1)
                left.append(
                    jnp.concatenate(
                        [
                            jnp.where(wide_top, edge, body[0:8]), body[8 : TV - 8],
                            jnp.where(wide_bottom, edge, body[TV - 8 :]),
                        ],
                        axis=0,
                    ).astype(BF16)
                )
        rest = []
        for g, t in enumerate(slot):
            for plane in range(2):
                predicted = dot(left[g * 2 + plane], ker_t[...])
                value = (observed[t, plane].astype(F32) - predicted).astype(BF16)
                rest.append(jnp.where(t < count, value, jnp.zeros_like(value)))
                sent[t, plane] = rest[-1]
        out_copy(step).start()
        back = [dot(value, ker[...]).astype(BF16).astype(F32) for value in rest]
        for g in range(GROUP):
            rows, tail, tiles, turn = spots[g]
            keep = lanes >= turn
            for plane in range(2):
                value = back[g * 2 + plane]
                one, two = pltpu.roll(value[:, 0:128], turn, 1), pltpu.roll(value[:, 128:], turn, 1)
                blank = jnp.zeros((TV, TV), F32)
                parts = (jnp.where(keep, one, blank), jnp.where(keep, two, one), jnp.where(keep, blank, two))
                for tile, part in zip(tiles, parts):
                    zero = blank[0:8]
                    edge = jnp.where(top, part[0:8], jnp.where(bottom, part[TV - 8 :], zero))
                    body = jnp.concatenate(
                        [jnp.where(top, zero, part[0:8]), part[8 : TV - 8], jnp.where(bottom, zero, part[TV - 8 :])],
                        axis=0,
                    )
                    spread[plane, tile, rows] += body
                    spread[plane, tile, tail] += edge

    @pl.loop(filled, groups)
    def _(step):
        for g in range(GROUP):
            sent[step * GROUP + g] = jnp.zeros(sent.shape[1:], BF16)
        out_copy(step).start()

    for c in range(2):
        cols = slice(c * 256, c * 256 + 256)
        late = slice(SG + c * 256, SG + c * 256 + 256)
        ar, ai = [
            dot(wide_t[...], jnp.concatenate([spread[p, 2 * c], spread[p, 2 * c + 1]], axis=1).astype(BF16))
            for p in range(2)
        ]
        sc, ss = screen[0, :, cols], screen[1, :, cols]
        model[:, cols] = (sc * ar + ss * ai).astype(BF16)
        model[:, late] = (sc * ai - ss * ar).astype(BF16)
    reduced = (
        dot(pad_t[:, 0:SG], model[:, 0:SG]) + dot(pad_t[:, SG:], model[:, SG:])
    ).astype(BF16)
    both = dot(reduced, pad[...])
    coefficient[0] = (both[0:M, 0:M] + both[M:, M:]).astype(BF16)
    coefficient[1] = (both[M:, 0:M] - both[0:M, M:]).astype(BF16)

    @pl.loop(0, groups)
    def _(step):
        out_copy(step).wait()


def gather_kernel(
    n, mine, foff_h, taper, turned, wave, out, arrived, phase, foff,
    near_s, near_r, mid_s, mid_r, far_s, far_r, local, load_s
):
    quads = n // 4
    me = lax.axis_index("facet")
    quad, middle, core = me // 4, lax.rem(me // 2, 2), lax.rem(me, 2)
    other = 1 - middle
    sibling, beside = index(quad, middle, 1 - core), index(quad, other, core)
    load = pltpu.make_async_copy(foff_h, foff, load_s)
    load.start()

    barrier = pltpu.get_barrier_semaphore()
    peers = [index(lax.rem(quad + k, quads), middle, core) for k in range(1, quads)] + [beside, sibling]
    for peer in peers:
        pl.semaphore_signal(barrier, inc=1, device_id={"facet": peer}, device_id_type=MESH)
    pl.semaphore_wait(barrier, len(peers))

    def away(k):
        return lax.rem(quad + 1 + lax.rem(k + quads // 2 - 1, quads - 1), quads)

    def event(i):
        back = lax.rem(quad + quads - 1 - lax.rem(i + quads // 2 - 2, quads - 1), quads)
        return jnp.where(i == 0, quad, back)

    def far_copy(slot, to):
        spot = index(slot, middle, core)
        return send(mine, arrived.at[spot], far_s.at[to], far_r.at[slot], index(to, middle, core))

    def mid_copy(j, h):
        piece = arrived.at[index(j, h, core)]
        return send(piece, piece, mid_s.at[j], mid_r.at[j], beside)

    def near_copy(h, j, side):
        piece = arrived.at[index(j, h, side)]
        return send(piece, piece, near_s.at[h, j], near_r.at[h, j], sibling)

    mid_own = send(mine, arrived.at[me], mid_s.at[quad], mid_r.at[quad], beside)
    near_own = send(mine, arrived.at[me], near_s.at[middle, quad], near_r.at[middle, quad], sibling)

    own = pltpu.make_async_copy(mine, arrived.at[me], local)
    own.start()
    for k in range(quads - 1):
        far_copy(quad, away(k)).start()
    mid_own.start()
    near_own.start()

    load.wait()
    phase[0], phase[1] = tapered_phase(foff, taper)
    own.wait()

    def transform(spot):
        pc, ps = phase[0], phase[1]
        real, imag = arrived[spot, 0].astype(F32), arrived[spot, 1].astype(F32)
        both = jnp.concatenate([pc * real + ps * imag, pc * imag - ps * real], axis=1).astype(BF16)
        for c in range(F // 256):
            cols, late = slice(c * 256, c * 256 + 256), slice(F + c * 256, F + c * 256 + 256)
            real = dot(both, turned[:, cols]).reshape(M // 8, 8, 256)
            imag = dot(both, turned[:, late]).reshape(M // 8, 8, 256)
            cv, sv = wave[spot, 0, :, cols][None], wave[spot, 1, :, cols][None]
            out[spot, :, cols] = (cv * real - sv * imag).reshape(M, 256).astype(BF16)
            out[spot, :, late] = (cv * imag + sv * real).reshape(M, 256).astype(BF16)

    transform(me)

    def take_far(j):
        far_copy(j, j).wait_recv()
        mid_copy(j, middle).start()
        near_copy(middle, j, core).start()

    def take_mid(j):
        mid_copy(j, other).wait_recv()
        near_copy(other, j, core).start()

    def wait_near(h, j):
        near_copy(h, j, 1 - core).wait_recv()

    def step(i, far, mid, late):
        one, two, three = event(i), event(jnp.maximum(i - 2, 0)), event(jnp.maximum(i - 3, 0))
        if far:
            take_far(one)
        if mid:
            take_mid(two)
            wait_near(middle, two)
        if late:
            wait_near(other, three)
        if far:
            transform(index(one, middle, core))
        if mid:
            transform(index(two, other, core))
            transform(index(two, middle, 1 - core))
        if late:
            transform(index(three, other, 1 - core))

    step(1, True, False, False)
    step(2, True, True, False)

    @pl.loop(3, quads)
    def _(i):
        step(i, True, True, True)

    step(quads, False, True, True)
    step(quads + 1, False, True, True)
    step(quads + 2, False, False, True)
    mid_own.wait_send()
    near_own.wait_send()
    near_copy(other, quad, core).wait_send()

    @pl.loop(1, quads)
    def _(i):
        j = event(i)
        far_copy(quad, j).wait_send()
        mid_copy(j, middle).wait_send()
        near_copy(middle, j, core).wait_send()
        near_copy(other, j, core).wait_send()


def backward_kernel(n, soff, pieces, basis, out_h, acc, flat, out, sems):
    acc[...] = jnp.zeros_like(acc)

    @pl.loop(0, n, unroll=2)
    def _(s):
        rows = pl.ds(soff[0, s], M)
        for plane in range(2):
            for k in range(F // M):
                acc[plane, k, rows] += pieces[s, :, plane * F + k * M : plane * F + k * M + M].astype(F32)

    for plane in range(2):
        for k in range(F // M):
            cols = slice(plane * F + k * M, plane * F + k * M + M)
            flat[0:M, cols] = (acc[plane, k, 0:M] + acc[plane, k, F:WIDE]).astype(BF16)
            flat[M:F, cols] = acc[plane, k, M:F].astype(BF16)

    copies = []
    for plane in range(2):
        for half in range(2):
            rows = slice(half * 256, half * 256 + 256)
            br, bi = basis[0, rows], basis[1, rows]
            if plane == 0:
                value = dot(br, flat[:, 0:F]) + dot(bi, flat[:, F:])
            else:
                value = dot(br, flat[:, F:]) - dot(bi, flat[:, 0:F])
            out[plane, rows] = value.astype(BF16)
            copies.append(
                pltpu.make_async_copy(out.at[plane, rows], out_h.at[plane, rows], sems.at[plane, half])
            )
            copies[-1].start()
    for copy in copies:
        copy.wait()


SMEM_SPEC = pl.BlockSpec(memory_space=pltpu.SMEM)
VMEM_SPEC = pl.BlockSpec(memory_space=pltpu.VMEM)
HBM_SPEC = pl.BlockSpec(memory_space=pltpu.HBM)
DMA = pltpu.SemaphoreType.DMA


def per_device(facets, facet_offsets, subgrid_offsets, w_terms, tile_count, tile_offsets, observed):
    n = lax.axis_size("facet")
    quads = n // 4
    soff_t, toff_t = subgrid_offsets.T, tile_offsets.T
    slots = observed.shape[0]
    basis_np = basis_table()
    basis = jnp.asarray(basis_np)
    br, bi = basis_np[:, :M]
    turned = jnp.asarray(np.block([[br, -bi], [bi, br]]))
    real, imag = padding_table(n)
    pad = jnp.asarray(np.concatenate([real, imag], axis=1))
    pad_t = jnp.asarray(np.block([[real.T, imag.T], [-imag.T, real.T]]))
    taper = jnp.asarray(taper_square())
    smooth_np = smooth_table()
    smooth, smooth_t = jnp.asarray(smooth_np), jnp.asarray(np.ascontiguousarray(smooth_np.T))
    ker_np = kernel_table()
    ker, ker_t = jnp.asarray(ker_np), jnp.asarray(np.ascontiguousarray(ker_np.T))
    plain = pltpu.CompilerParams(vmem_limit_bytes=24 * MIB)

    deep = SG + 8 * slots
    piece_shape = (2, M, M)
    tables = (basis, taper, smooth, smooth_t, pad, pad_t, ker, ker_t, turned)
    in_hbm = [
        pltpu.with_memory_space_constraint(x, pltpu.HBM)
        for x in (facet_offsets, soff_t, toff_t, facets[0], *tables, observed)
    ]
    held = (basis, taper, pad, pad_t, ker, ker_t, turned, observed)
    summed, screen, wide, wide_t, basis, taper, pad, pad_t, ker, ker_t, turned, observed, wave = pl.pallas_call(
        functools.partial(forward_kernel, n, slots),
        out_shape=(
            jax.ShapeDtypeStruct((2, M, M), F32), jax.ShapeDtypeStruct((2, SG, SG), F32),
            jax.ShapeDtypeStruct((deep, SG), BF16), jax.ShapeDtypeStruct((SG, deep), BF16),
            *[jax.ShapeDtypeStruct(x.shape, x.dtype) for x in held],
            jax.ShapeDtypeStruct((n, 2, 8, F), F32),
        ),
        in_specs=[SMEM_SPEC] + [HBM_SPEC] * 14,
        out_specs=(VMEM_SPEC,) * 13,
        scratch_shapes=[
            VMEM((2, F // M, WIDE, M), F32), VMEM((2, M, M), F32),
            pltpu.SMEM((1, 2), jnp.int32), pltpu.SMEM((2, n), jnp.int32),
            pltpu.SMEM((2, slots), jnp.int32),
            VMEM((2, F, F), BF16),
            *[VMEM((2, quads, *piece_shape), BF16)] * 3,
            *[VMEM((quads, *piece_shape), BF16)] * 4, VMEM((quads // 2, *piece_shape), BF16),
            DMA((14,)), *[DMA((2, quads))] * 2, *[DMA((quads, 2))] * 5, DMA((quads // 2, 2)),
        ],
        compiler_params=pltpu.CompilerParams(
            vmem_limit_bytes=32 * MIB, collective_id=0, has_side_effects=True
        ),
        name="forward",
    )(w_terms, *in_hbm)

    residual, coefficient = pl.pallas_call(
        functools.partial(subgrid_kernel, slots),
        out_shape=(
            jax.ShapeDtypeStruct((slots, 2, TV, TV), BF16),
            jax.ShapeDtypeStruct((2, M, M), BF16),
        ),
        in_specs=[SMEM_SPEC, HBM_SPEC] + [VMEM_SPEC] * 9,
        out_specs=(HBM_SPEC, VMEM_SPEC),
        scratch_shapes=[
            VMEM((SG, 2 * M), BF16), VMEM((SG, 2 * SG), BF16),
            VMEM((2, SG // 128, deep, 128), F32), VMEM((2, SG // 128, deep, 128), F32),
            VMEM((slots, 2, TV, TV), BF16),
            pltpu.SMEM((2, slots), jnp.int32), DMA((slots // GROUP,)), DMA,
        ],
        compiler_params=plain,
        name="subgrid",
    )(tile_count, in_hbm[2], summed, screen, wide, wide_t, pad, pad_t, ker, ker_t, observed)

    pieces = pl.pallas_call(
        functools.partial(gather_kernel, n),
        out_shape=jax.ShapeDtypeStruct((n, M, 2 * F), BF16),
        in_specs=[VMEM_SPEC, HBM_SPEC, VMEM_SPEC, VMEM_SPEC, VMEM_SPEC],
        out_specs=VMEM_SPEC,
        scratch_shapes=[
            VMEM((n, 2, M, M), BF16), VMEM((2, M, M), F32),
            pltpu.SMEM((1, 2), jnp.int32),
            *[DMA((2, quads))] * 2, *[DMA((quads,))] * 4, DMA, DMA,
        ],
        compiler_params=pltpu.CompilerParams(
            vmem_limit_bytes=24 * MIB, collective_id=1, has_side_effects=True
        ),
        name="gather",
    )(coefficient, in_hbm[0], taper, turned, wave)

    update = pl.pallas_call(
        functools.partial(backward_kernel, n),
        out_shape=jax.ShapeDtypeStruct((2, F, F), BF16),
        in_specs=[SMEM_SPEC, VMEM_SPEC, VMEM_SPEC],
        out_specs=HBM_SPEC,
        scratch_shapes=[
            VMEM((2, F // M, WIDE, M), F32), VMEM((F, 2 * F), BF16), VMEM((2, F, F), BF16), DMA((2, 2)),
        ],
        compiler_params=plain,
        name="backward",
    )(soff_t, pieces, basis)
    return (residual, update[None])


def solution(mesh):
    placed = (
        P(("groups", "facet"), None, None, None),
        P(("groups", "facet"), None),
        P("groups", None),
        P(("groups", "facet")),
        P(("groups", "facet")),
        P(("groups", "facet"), None),
        P(("groups", "facet"), None, None, None),
    )
    return jax.shard_map(
        per_device,
        mesh=mesh,
        in_specs=placed,
        out_specs=(
            P(("groups", "facet"), None, None, None),
            P(("groups", "facet"), None, None, None),
        ),
        check_vma=False,
    )
```

```python
import functools
import math

import jax
import jax.numpy as jnp
import ml_dtypes
import numpy as np
from jax import lax
from jax.experimental import pallas as pl
from jax.experimental.pallas import tpu as pltpu
from jax.sharding import PartitionSpec as P

F = 512
M = 128
SG = 512
TV = 128
WIDE = F + M
GROUP = 4

BF16 = jnp.bfloat16
F32 = jnp.float32
TWO_PI = 2.0 * math.pi
MESH = pl.DeviceIdType.MESH
VMEM = pltpu.VMEM
MIB = 1024 * 1024


def basis_table():
    index = np.arange(F)
    angle = -TWO_PI * (index[:, None] * index[None, :] % F) / F
    scale = 1.0 / math.sqrt(F)
    return np.stack([np.cos(angle) * scale, np.sin(angle) * scale]).astype(ml_dtypes.bfloat16)


def padding_table(facet_count):
    angle = TWO_PI * (np.arange(SG)[:, None] * np.arange(M)[None, :] % SG) / SG
    scale = (M * math.sqrt(facet_count)) ** (-0.5)
    return np.stack([np.cos(angle) * scale, np.sin(angle) * scale]).astype(ml_dtypes.bfloat16)


def taper_square():
    taper = 0.6 + 0.4 * np.sin(math.pi * (np.arange(M) + 0.5) / M)
    return (taper[:, None] * taper[None, :]).astype(np.float32)


def dot(left, right):
    return jnp.dot(left, right, preferred_element_type=F32)


def cos_sin_turns(turns):
    quarter = jnp.floor(turns * 4.0 + 0.5)
    y = (turns - quarter * 0.25) * TWO_PI
    y2 = y * y
    sine = y * (1.0 + y2 * (-1.0 / 6 + y2 * (1.0 / 120 + y2 * (-1.0 / 5040 + y2 * (1.0 / 362880)))))
    cosine = 1.0 + y2 * (
        -0.5 + y2 * (1.0 / 24 + y2 * (-1.0 / 720 + y2 * (1.0 / 40320 - y2 * (1.0 / 3628800))))
    )
    which = quarter.astype(jnp.int32) & 3
    odd = (which & 1) == 1
    first = jnp.where(odd, sine, cosine)
    second = jnp.where(odd, cosine, sine)
    cos_value = jnp.where((which == 1) | (which == 2), -first, first)
    sin_value = jnp.where(which >= 2, -second, second)
    return cos_value, sin_value


def tapered_phase(offset_ref, taper_ref):
    rows = lax.broadcasted_iota(jnp.int32, (M, M), 0)
    columns = lax.broadcasted_iota(jnp.int32, (M, M), 1)
    total = (rows * offset_ref[0, 0] + columns * offset_ref[0, 1]) & (F - 1)
    cos_value, sin_value = cos_sin_turns(total.astype(F32) * (1.0 / F))
    taper = taper_ref[...]
    return cos_value * taper, sin_value * taper


def place(n):
    me = lax.axis_index("facet")
    quads = n // 4
    far_first = [1 + (t + quads // 2 - 1) % (quads - 1) for t in range(quads - 1)]
    return quads, me // 4, lax.rem(me // 2, 2), lax.rem(me, 2), far_first


def index(quad, middle, core):
    return quad * 4 + middle * 2 + core


def greet(peers):
    barrier = pltpu.get_barrier_semaphore()
    for peer in peers:
        pl.semaphore_signal(barrier, inc=1, device_id={"facet": peer}, device_id_type=MESH)
    pl.semaphore_wait(barrier, len(peers))


def send(src, dst, send_sem, recv_sem, peer):
    return pltpu.make_async_remote_copy(
        src_ref=src, dst_ref=dst, send_sem=send_sem, recv_sem=recv_sem,
        device_id={"facet": peer}, device_id_type=MESH,
    )


def fill_screen(w_value, screen):
    @pl.loop(0, 4)
    def _(c):
        rows = pl.ds(pl.multiple_of(c * 128, 128), 128)
        u = (lax.broadcasted_iota(jnp.int32, (128, SG), 0) + (c * 128 - 256)).astype(F32)
        v = (lax.broadcasted_iota(jnp.int32, (128, SG), 1) - 256).astype(F32)
        radius = (u * u + v * v) * (1.0 / (SG * SG))
        cos_value, sin_value = cos_sin_turns(w_value * (jnp.sqrt(1.0 + radius) - 1.0))
        screen[0, rows, :] = cos_value
        screen[1, rows, :] = sin_value


def tap_values():
    taps = np.arange(5, dtype=np.float32)
    value = 0.75 * np.exp(-(taps / 1.5) * (taps / 1.5))
    return [float(x) for x in value.astype(ml_dtypes.bfloat16).astype(np.float32)]


def smooth_table():
    order = np.concatenate([np.arange(0, SG, 2), np.arange(1, SG, 2)])
    distance = np.abs(np.arange(SG)[None, :] - order[:, None])
    taps = np.array(tap_values() + [0.0], np.float32)
    return taps[np.minimum(distance, 5)].astype(ml_dtypes.bfloat16)


def kernel_table():
    distance = np.abs(np.arange(2 * TV)[None, :] - 2 * np.arange(TV)[:, None] - 1)
    taps = np.array(tap_values() + [0.0], np.float32)
    return taps[np.minimum(distance, 5)].astype(ml_dtypes.bfloat16)


def edge_values(position, offset, spot):
    i = spot & 7
    slot = jnp.where(i < 2, i, i + (TV - 8))
    distance = jnp.abs(position - offset - 2 * slot - 1)
    value = jnp.zeros(distance.shape, F32)
    for step, tap in enumerate(tap_values()):
        value = jnp.where(distance == step, tap, value)
    inside = (position >= offset) & (position < offset + 2 * TV) & ((i < 2) | (i >= 6))
    return jnp.where(inside, value, 0.0).astype(BF16)


def fill_rows(slots, toff, wide):
    @pl.loop(0, slots // 2)
    def _(c):
        spot = lax.broadcasted_iota(jnp.int32, (16, SG), 0)
        lane = lax.broadcasted_iota(jnp.int32, (16, SG), 1)
        offset = jnp.where(spot < 8, toff[0, 2 * c], toff[0, 2 * c + 1])
        wide[pl.ds(pl.multiple_of(SG + c * 16, 16), 16), :] = edge_values(lane, offset, spot)


def fill_columns(slots, toff, wide_t):
    lane = lax.broadcasted_iota(jnp.int32, (1, 8 * slots), 1)
    offset = jnp.zeros_like(lane)
    for t in range(slots):
        offset = jnp.where(lane >> 3 == t, toff[0, t], offset)

    @pl.loop(0, SG // 64)
    def _(c):
        position = lax.broadcasted_iota(jnp.int32, (64, 8 * slots), 0) + c * 64
        spot = lax.broadcasted_iota(jnp.int32, (64, 8 * slots), 1)
        wide_t[pl.ds(pl.multiple_of(c * 64, 64), 64), SG:] = edge_values(position, offset, spot)


def forward_kernel(
    n, slots, w_ref, foff_h, soff_h, toff_h, facet_h, basis_h, taper_h, smooth_h, smooth_t_h,
    pad_h, pad_t_h, ker_h, ker_t_h, turned_h, cutter_h, observed_h,
    summed, screen, wide, wide_t, basis, taper, pad, pad_t, ker, ker_t, turned, observed, wave,
    spec, phase, foff, soff, toff, facet, cutter,
    outgoing, own, near, pair, mid, quad_sum, relay, far,
    load_s, near_s, near_r, mid_s, mid_r, relay_s, relay_r, far_s, far_r
):
    pairs = (
        (foff_h, foff), (taper_h, taper), (soff_h, soff), (basis_h, basis), (facet_h, facet),
        (toff_h, toff), (cutter_h, cutter), (smooth_h, wide.at[0:SG]), (smooth_t_h, wide_t.at[:, 0:SG]), (observed_h, observed),
        (pad_h, pad), (pad_t_h, pad_t), (ker_h, ker), (ker_t_h, ker_t), (turned_h, turned),
    )
    loads = [pltpu.make_async_copy(src, dst, load_s.at[i]) for i, (src, dst) in enumerate(pairs)]
    for load in loads[:7]:
        load.start()

    quads = n // 4
    me = lax.axis_index("facet")
    quad, middle, core = me // 4, lax.rem(me // 2, 2), lax.rem(me, 2)
    other, odd, group = 1 - middle, lax.rem(quad, 2), quad // 2
    mate = quad + 1 - 2 * odd
    sibling, beside = index(quad, middle, 1 - core), index(quad, other, core)
    high = quad // (quads // 2)
    inner_side = jnp.where(high == odd, 0, 1)

    def turn(k):
        spot = quads - 2 - inner_side
        far_k = jnp.where(k > spot, k - 1, k)
        down = quads - 1 - far_k
        down = jnp.where(down < 2 * group + 2, down - 2, down)
        up = jnp.where(far_k >= 2 * group, far_k + 2, far_k)
        j = jnp.where(k == spot, mate, jnp.where(high == 1, up, down))
        return jnp.where(k == quads - 1, quad, j)

    order = [turn(k) for k in range(4)] if quads == 4 else None

    def each(count, body):
        if quads == 4:
            for j in order[:count]:
                body(j)
        else:

            @pl.loop(0, count)
            def _(k):
                body(turn(k))

    barrier = pltpu.get_barrier_semaphore()
    peers = [index(lax.rem(quad + k, quads), middle, core) for k in range(1, quads)] + [beside, sibling]
    for peer in peers:
        pl.semaphore_signal(barrier, inc=1, device_id={"facet": peer}, device_id_type=MESH)

    loads[0].wait()
    loads[1].wait()
    phase[0], phase[1] = tapered_phase(foff, taper)
    loads[2].wait()
    lane = lax.broadcasted_iota(jnp.int32, (8, F), 1)

    @pl.loop(0, n, unroll=2)
    def _(s):
        turns = ((lane * soff[1, s]) & (F - 1)).astype(F32) * (1.0 / F)
        wave[s, 0], wave[s, 1] = cos_sin_turns(turns)

    loads[3].wait()
    loads[4].wait()
    for load in loads[7:]:
        load.start()

    @pl.loop(0, 2)
    def _(c):
        cols = pl.ds(pl.multiple_of(c * 256, 256), 256)
        xr, xi = facet[0, :, cols], facet[1, :, cols]
        real = dot(basis[0], xr) - dot(basis[1], xi)
        imag = dot(basis[0], xi) + dot(basis[1], xr)
        for side in range(2):
            part = slice(side * M, side * M + M)
            for plane, value in enumerate((real, imag)):
                spec[plane, c * 2 + side, 0:F] = value[:, part]
                spec[plane, c * 2 + side, F:WIDE] = value[0:M, part]

    loads[5].wait()
    loads[6].wait()

    def cut(s, target, where):
        rows = pl.ds(soff[0, s], M)
        real, imag = [], []
        for tile in range(F // M):
            part = slice(tile * M, tile * M + M)
            cv, sv = wave[s, 0, :, part][None], wave[s, 1, :, part][None]
            r = spec[0, tile, rows].reshape(M // 8, 8, M)
            i = spec[1, tile, rows].reshape(M // 8, 8, M)
            real.append((cv * r + sv * i).reshape(M, M).astype(BF16))
            imag.append((cv * i - sv * r).reshape(M, M).astype(BF16))
        both = dot(jnp.concatenate(real + imag, axis=1), cutter[...])
        real, imag = both[:, 0:M], both[:, M:]
        pc, ps = phase[0], phase[1]
        target[where[0], where[1], 0] = (pc * real - ps * imag).astype(BF16)
        target[where[0], where[1], 1] = (pc * imag + ps * real).astype(BF16)

    def near_copy(h, j):
        return send(outgoing.at[h, j], near.at[h, j], near_s.at[h, j], near_r.at[h, j], sibling)

    def mid_copy(j, p):
        return send(pair.at[j, p], mid.at[j, p], mid_s.at[j, p], mid_r.at[j, p], beside)

    def relay_copy(j, p):
        return send(
            quad_sum.at[j, p], relay.at[j, p], relay_s.at[j, p], relay_r.at[j, p], index(mate, middle, core)
        )

    def far_copy(j, slot, p):
        return send(quad_sum.at[j, p], far.at[slot, p], far_s.at[j, p], far_r.at[slot, p], index(j, middle, core))

    def is_mate(j):
        return j == mate

    def is_gate(j):
        return (j != mate) & (odd == jnp.where(j > quad, 1, 0))

    def is_outer(j):
        return (j != mate) & (odd != jnp.where(j > quad, 1, 0))

    def near_sum(h, j, p):
        return own[h, j, p].astype(F32) + near[h, j, p].astype(F32)

    def mid_sum(j, p):
        return near_sum(1, j, p) + mid[j, p].astype(F32)

    pl.semaphore_wait(barrier, len(peers))

    def give(h, half, j):
        cut(index(j, half, 1 - core), outgoing, (h, j))
        near_copy(h, j).start()

    def keep(h, half, j):
        cut(index(j, half, core), own, (h, j))

    def pass_on(j):
        near_copy(0, j).wait_recv()
        for p in range(2):
            pair[j, p] = near_sum(0, j, p).astype(BF16)
            mid_copy(j, p).start()

    if quads == 4:
        give(0, other, order[0])
        give(0, other, order[1])
        keep(0, other, order[0])
        give(0, other, order[2])
        keep(0, other, order[1])
        give(0, other, order[3])
        pass_on(order[0])
        keep(0, other, order[2])
        pass_on(order[1])
        keep(0, other, order[3])
        pass_on(order[2])
        pass_on(order[3])
    else:
        each(quads, lambda j: give(0, other, j))
        each(quads, lambda j: keep(0, other, j))
        each(quads, pass_on)
    each(quads, lambda j: give(1, middle, j))
    each(quads, lambda j: keep(1, middle, j))
    def combine(j):
        near_copy(1, j).wait_recv()
        for p in range(2):
            mid_copy(j, p).wait_recv()

            @pl.when(is_gate(j))
            def _():
                relay_copy(j, p).wait_recv()
                quad_sum[j, p] = (mid_sum(j, p) + relay[j, p].astype(F32)).astype(BF16)
                far_copy(j, group, p).start()

            @pl.when(is_mate(j))
            def _():
                quad_sum[j, p] = mid_sum(j, p).astype(BF16)
                far_copy(j, group, p).start()

            @pl.when(is_outer(j))
            def _():
                quad_sum[j, p] = mid_sum(j, p).astype(BF16)
                relay_copy(j, p).start()

    if quads == 4:
        combine(order[0])
        fill_rows(slots, toff, wide)
        combine(order[1])
        fill_columns(slots, toff, wide_t)
        combine(order[2])
    else:
        each(quads - 1, combine)
        fill_rows(slots, toff, wide)
        fill_columns(slots, toff, wide_t)
    fill_screen(w_ref[0], screen)
    near_copy(1, quad).wait_recv()
    for p in range(2):
        mid_copy(quad, p).wait_recv()
        summed[p] = mid_sum(quad, p)
    for step in range(quads // 2):
        slot = lax.rem(group + step, quads // 2)
        for p in range(2):
            far_copy(quad, slot, p).wait_recv()
            summed[p] += far[slot, p].astype(F32)
    for load in loads[7:]:
        load.wait()

    def finish(j):
        near_copy(0, j).wait_send()
        near_copy(1, j).wait_send()
        for p in range(2):
            mid_copy(j, p).wait_send()

    def finish_far(j):
        for p in range(2):

            @pl.when(is_outer(j))
            def _():
                relay_copy(j, p).wait_send()

            @pl.when(jnp.logical_not(is_outer(j)))
            def _():
                far_copy(j, group, p).wait_send()

    each(quads, finish)
    each(quads - 1, finish_far)


def subgrid_kernel(
    slots, count_ref, toff_h, summed, screen, wide, wide_t, pad, pad_t, ker, ker_t, observed,
    residual_h, coefficient, inner, model, grid, spread, sent, toff, sems, load_s
):
    load = pltpu.make_async_copy(toff_h, toff, load_s)
    load.start()
    groups = slots // GROUP
    sr, si = summed[0], summed[1]
    stacked = jnp.concatenate(
        [jnp.concatenate([sr, si], axis=1), jnp.concatenate([-si, sr], axis=1)], axis=0
    ).astype(BF16)
    inner[...] = dot(pad[...], stacked).astype(BF16)

    for c in range(2):
        cols = slice(c * 256, c * 256 + 256)
        late = slice(SG + c * 256, SG + c * 256 + 256)
        real, imag = dot(inner[...], pad_t[:, cols]), dot(inner[...], pad_t[:, late])
        cos_value, sin_value = screen[0, :, cols], screen[1, :, cols]
        model[:, cols] = (cos_value * real - sin_value * imag).astype(BF16)
        model[:, late] = (cos_value * imag + sin_value * real).astype(BF16)

    for plane in range(2):
        for c in range(2):
            start = plane * SG + c * 256
            value = dot(wide[...], model[:, start : start + 256])
            for side in range(2):
                grid[plane, c * 2 + side] = value[:, side * 128 : side * 128 + 128]
                spread[plane, c * 2 + side] = jnp.zeros(spread.shape[2:], F32)

    load.wait()
    count = count_ref[0]
    lanes = lax.broadcasted_iota(jnp.int32, (TV, TV), 1)
    subs = lax.broadcasted_iota(jnp.int32, (8, TV), 0)
    top, bottom = subs < 2, subs >= 6

    def out_copy(step):
        tiles = pl.ds(step * GROUP, GROUP)
        return pltpu.make_async_copy(sent.at[tiles], residual_h.at[tiles], sems.at[step])

    filled = (count + GROUP - 1) // GROUP

    @pl.loop(0, filled)
    def _(step):
        slot = [step * GROUP + g for g in range(GROUP)]
        spots, left = [], []
        for t in slot:
            ou, ov = toff[0, t] + 1, toff[1, t]
            rows = pl.ds((ou & 1) * (SG // 2) + (ou >> 1), TV)
            tail = pl.ds(pl.multiple_of(SG + t * 8, 8), 8)
            first, turn = ov >> 7, ov & 127
            tiles = (first, first + 1, jnp.minimum(first + 2, SG // 128 - 1))
            spots.append((rows, tail, tiles, turn))

            def pick(plane, where_rows, size):
                keep = lanes[0:size] >= turn
                part = [grid[plane, k, where_rows] for k in tiles]
                both = [jnp.where(keep, part[k], part[k + 1]) for k in range(2)]
                return jnp.concatenate([pltpu.roll(x, (TV - turn) & 127, 1) for x in both], axis=1)

            for plane in range(2):
                body, edge = pick(plane, rows, TV), pick(plane, tail, 8)
                wide_top = jnp.concatenate([top, top], axis=1)
                wide_bottom = jnp.concatenate([bottom, bottom], axis=1)
                left.append(
                    jnp.concatenate(
                        [
                            jnp.where(wide_top, edge, body[0:8]), body[8 : TV - 8],
                            jnp.where(wide_bottom, edge, body[TV - 8 :]),
                        ],
                        axis=0,
                    ).astype(BF16)
                )
        rest = []
        for g, t in enumerate(slot):
            for plane in range(2):
                predicted = dot(left[g * 2 + plane], ker_t[...])
                value = (observed[t, plane].astype(F32) - predicted).astype(BF16)
                rest.append(jnp.where(t < count, value, jnp.zeros_like(value)))
                sent[t, plane] = rest[-1]
        out_copy(step).start()
        back = [dot(value, ker[...]).astype(BF16).astype(F32) for value in rest]
        for g in range(GROUP):
            rows, tail, tiles, turn = spots[g]
            keep = lanes >= turn
            for plane in range(2):
                value = back[g * 2 + plane]
                one, two = pltpu.roll(value[:, 0:128], turn, 1), pltpu.roll(value[:, 128:], turn, 1)
                blank = jnp.zeros((TV, TV), F32)
                parts = (jnp.where(keep, one, blank), jnp.where(keep, two, one), jnp.where(keep, blank, two))
                for tile, part in zip(tiles, parts):
                    zero = blank[0:8]
                    edge = jnp.where(top, part[0:8], jnp.where(bottom, part[TV - 8 :], zero))
                    body = jnp.concatenate(
                        [jnp.where(top, zero, part[0:8]), part[8 : TV - 8], jnp.where(bottom, zero, part[TV - 8 :])],
                        axis=0,
                    )
                    spread[plane, tile, rows] += body
                    spread[plane, tile, tail] += edge

    @pl.loop(filled, groups)
    def _(step):
        for g in range(GROUP):
            sent[step * GROUP + g] = jnp.zeros(sent.shape[1:], BF16)
        out_copy(step).start()

    for c in range(2):
        cols = slice(c * 256, c * 256 + 256)
        late = slice(SG + c * 256, SG + c * 256 + 256)
        ar, ai = [
            dot(wide_t[...], jnp.concatenate([spread[p, 2 * c], spread[p, 2 * c + 1]], axis=1).astype(BF16))
            for p in range(2)
        ]
        sc, ss = screen[0, :, cols], screen[1, :, cols]
        model[:, cols] = (sc * ar + ss * ai).astype(BF16)
        model[:, late] = (sc * ai - ss * ar).astype(BF16)
    reduced = (
        dot(pad_t[:, 0:SG], model[:, 0:SG]) + dot(pad_t[:, SG:], model[:, SG:])
    ).astype(BF16)
    both = dot(reduced, pad[...])
    coefficient[0] = (both[0:M, 0:M] + both[M:, M:]).astype(BF16)
    coefficient[1] = (both[M:, 0:M] - both[0:M, M:]).astype(BF16)

    @pl.loop(0, groups)
    def _(step):
        out_copy(step).wait()


def gather_kernel(
    n, mine, foff_h, taper, turned, wave, out, arrived, phase, foff,
    near_s, near_r, mid_s, mid_r, far_s, far_r, local, load_s
):
    quads = n // 4
    me = lax.axis_index("facet")
    quad, middle, core = me // 4, lax.rem(me // 2, 2), lax.rem(me, 2)
    other = 1 - middle
    sibling, beside = index(quad, middle, 1 - core), index(quad, other, core)
    load = pltpu.make_async_copy(foff_h, foff, load_s)
    load.start()

    barrier = pltpu.get_barrier_semaphore()
    peers = [index(lax.rem(quad + k, quads), middle, core) for k in range(1, quads)] + [beside, sibling]
    for peer in peers:
        pl.semaphore_signal(barrier, inc=1, device_id={"facet": peer}, device_id_type=MESH)
    pl.semaphore_wait(barrier, len(peers))

    def away(k):
        return lax.rem(quad + 1 + lax.rem(k + quads // 2 - 1, quads - 1), quads)

    def event(i):
        back = lax.rem(quad + quads - 1 - lax.rem(i + quads // 2 - 2, quads - 1), quads)
        return jnp.where(i == 0, quad, back)

    def far_copy(slot, to):
        spot = index(slot, middle, core)
        return send(mine, arrived.at[spot], far_s.at[to], far_r.at[slot], index(to, middle, core))

    def mid_copy(j, h):
        piece = arrived.at[index(j, h, core)]
        return send(piece, piece, mid_s.at[j], mid_r.at[j], beside)

    def near_copy(h, j, side):
        piece = arrived.at[index(j, h, side)]
        return send(piece, piece, near_s.at[h, j], near_r.at[h, j], sibling)

    mid_own = send(mine, arrived.at[me], mid_s.at[quad], mid_r.at[quad], beside)
    near_own = send(mine, arrived.at[me], near_s.at[middle, quad], near_r.at[middle, quad], sibling)

    own = pltpu.make_async_copy(mine, arrived.at[me], local)
    own.start()
    for k in range(quads - 1):
        far_copy(quad, away(k)).start()
    mid_own.start()
    near_own.start()

    load.wait()
    phase[0], phase[1] = tapered_phase(foff, taper)
    own.wait()

    def transform(spot):
        pc, ps = phase[0], phase[1]
        real, imag = arrived[spot, 0].astype(F32), arrived[spot, 1].astype(F32)
        both = jnp.concatenate([pc * real + ps * imag, pc * imag - ps * real], axis=1).astype(BF16)
        for c in range(F // 256):
            cols, late = slice(c * 256, c * 256 + 256), slice(F + c * 256, F + c * 256 + 256)
            real = dot(both, turned[:, cols]).reshape(M // 8, 8, 256)
            imag = dot(both, turned[:, late]).reshape(M // 8, 8, 256)
            cv, sv = wave[spot, 0, :, cols][None], wave[spot, 1, :, cols][None]
            out[spot, :, cols] = (cv * real - sv * imag).reshape(M, 256).astype(BF16)
            out[spot, :, late] = (cv * imag + sv * real).reshape(M, 256).astype(BF16)

    transform(me)

    def take_far(j):
        far_copy(j, j).wait_recv()
        mid_copy(j, middle).start()
        near_copy(middle, j, core).start()

    def take_mid(j):
        mid_copy(j, other).wait_recv()
        near_copy(other, j, core).start()

    def wait_near(h, j):
        near_copy(h, j, 1 - core).wait_recv()

    def step(i, far, mid, late):
        one, two, three = event(i), event(jnp.maximum(i - 2, 0)), event(jnp.maximum(i - 3, 0))
        if far:
            take_far(one)
        if mid:
            take_mid(two)
            wait_near(middle, two)
        if late:
            wait_near(other, three)
        if far:
            transform(index(one, middle, core))
        if mid:
            transform(index(two, other, core))
            transform(index(two, middle, 1 - core))
        if late:
            transform(index(three, other, 1 - core))

    step(1, True, False, False)
    step(2, True, True, False)

    @pl.loop(3, quads)
    def _(i):
        step(i, True, True, True)

    step(quads, False, True, True)
    step(quads + 1, False, True, True)
    step(quads + 2, False, False, True)
    mid_own.wait_send()
    near_own.wait_send()
    near_copy(other, quad, core).wait_send()

    @pl.loop(1, quads)
    def _(i):
        j = event(i)
        far_copy(quad, j).wait_send()
        mid_copy(j, middle).wait_send()
        near_copy(middle, j, core).wait_send()
        near_copy(other, j, core).wait_send()


def backward_kernel(n, soff, pieces, basis, out_h, acc, flat, out, sems):
    acc[...] = jnp.zeros_like(acc)

    @pl.loop(0, n, unroll=2)
    def _(s):
        rows = pl.ds(soff[0, s], M)
        for plane in range(2):
            for k in range(F // M):
                acc[plane, k, rows] += pieces[s, :, plane * F + k * M : plane * F + k * M + M].astype(F32)

    for plane in range(2):
        for k in range(F // M):
            cols = slice(plane * F + k * M, plane * F + k * M + M)
            flat[0:M, cols] = (acc[plane, k, 0:M] + acc[plane, k, F:WIDE]).astype(BF16)
            flat[M:F, cols] = acc[plane, k, M:F].astype(BF16)

    copies = []
    for plane in range(2):
        for half in range(2):
            rows = slice(half * 256, half * 256 + 256)
            br, bi = basis[0, rows], basis[1, rows]
            if plane == 0:
                value = dot(br, flat[:, 0:F]) + dot(bi, flat[:, F:])
            else:
                value = dot(br, flat[:, F:]) - dot(bi, flat[:, 0:F])
            out[plane, rows] = value.astype(BF16)
            copies.append(
                pltpu.make_async_copy(out.at[plane, rows], out_h.at[plane, rows], sems.at[plane, half])
            )
            copies[-1].start()
    for copy in copies:
        copy.wait()


SMEM_SPEC = pl.BlockSpec(memory_space=pltpu.SMEM)
VMEM_SPEC = pl.BlockSpec(memory_space=pltpu.VMEM)
HBM_SPEC = pl.BlockSpec(memory_space=pltpu.HBM)
DMA = pltpu.SemaphoreType.DMA


def per_device(facets, facet_offsets, subgrid_offsets, w_terms, tile_count, tile_offsets, observed):
    n = lax.axis_size("facet")
    quads = n // 4
    soff_t, toff_t = subgrid_offsets.T, tile_offsets.T
    slots = observed.shape[0]
    basis_np = basis_table()
    basis = jnp.asarray(basis_np)
    br, bi = basis_np[:, :M]
    turned = jnp.asarray(np.block([[br, -bi], [bi, br]]))
    real, imag = padding_table(n)
    pad = jnp.asarray(np.concatenate([real, imag], axis=1))
    pad_t = jnp.asarray(np.block([[real.T, imag.T], [-imag.T, real.T]]))
    taper = jnp.asarray(taper_square())
    smooth_np = smooth_table()
    smooth, smooth_t = jnp.asarray(smooth_np), jnp.asarray(np.ascontiguousarray(smooth_np.T))
    ker_np = kernel_table()
    ker, ker_t = jnp.asarray(ker_np), jnp.asarray(np.ascontiguousarray(ker_np.T))
    plain = pltpu.CompilerParams(vmem_limit_bytes=24 * MIB)

    deep = SG + 8 * slots
    piece_shape = (2, M, M)
    cutter = jnp.asarray(np.block([[br.T, bi.T], [-bi.T, br.T]]))
    tables = (basis, taper, smooth, smooth_t, pad, pad_t, ker, ker_t, turned, cutter)
    in_hbm = [
        pltpu.with_memory_space_constraint(x, pltpu.HBM)
        for x in (facet_offsets, soff_t, toff_t, facets[0], *tables, observed)
    ]
    held = (basis, taper, pad, pad_t, ker, ker_t, turned, observed)
    summed, screen, wide, wide_t, basis, taper, pad, pad_t, ker, ker_t, turned, observed, wave = pl.pallas_call(
        functools.partial(forward_kernel, n, slots),
        out_shape=(
            jax.ShapeDtypeStruct((2, M, M), F32), jax.ShapeDtypeStruct((2, SG, SG), F32),
            jax.ShapeDtypeStruct((deep, SG), BF16), jax.ShapeDtypeStruct((SG, deep), BF16),
            *[jax.ShapeDtypeStruct(x.shape, x.dtype) for x in held],
            jax.ShapeDtypeStruct((n, 2, 8, F), F32),
        ),
        in_specs=[SMEM_SPEC] + [HBM_SPEC] * 15,
        out_specs=(VMEM_SPEC,) * 13,
        scratch_shapes=[
            VMEM((2, F // M, WIDE, M), F32), VMEM((2, M, M), F32),
            pltpu.SMEM((1, 2), jnp.int32), pltpu.SMEM((2, n), jnp.int32),
            pltpu.SMEM((2, slots), jnp.int32),
            VMEM((2, F, F), BF16), VMEM((2 * F, 2 * M), BF16),
            *[VMEM((2, quads, *piece_shape), BF16)] * 3,
            *[VMEM((quads, *piece_shape), BF16)] * 4, VMEM((quads // 2, *piece_shape), BF16),
            DMA((15,)), *[DMA((2, quads))] * 2, *[DMA((quads, 2))] * 5, DMA((quads // 2, 2)),
        ],
        compiler_params=pltpu.CompilerParams(
            vmem_limit_bytes=32 * MIB, collective_id=0, has_side_effects=True
        ),
        name="forward",
    )(w_terms, *in_hbm)

    residual, coefficient = pl.pallas_call(
        functools.partial(subgrid_kernel, slots),
        out_shape=(
            jax.ShapeDtypeStruct((slots, 2, TV, TV), BF16),
            jax.ShapeDtypeStruct((2, M, M), BF16),
        ),
        in_specs=[SMEM_SPEC, HBM_SPEC] + [VMEM_SPEC] * 9,
        out_specs=(HBM_SPEC, VMEM_SPEC),
        scratch_shapes=[
            VMEM((SG, 2 * M), BF16), VMEM((SG, 2 * SG), BF16),
            VMEM((2, SG // 128, deep, 128), F32), VMEM((2, SG // 128, deep, 128), F32),
            VMEM((slots, 2, TV, TV), BF16),
            pltpu.SMEM((2, slots), jnp.int32), DMA((slots // GROUP,)), DMA,
        ],
        compiler_params=plain,
        name="subgrid",
    )(tile_count, in_hbm[2], summed, screen, wide, wide_t, pad, pad_t, ker, ker_t, observed)

    pieces = pl.pallas_call(
        functools.partial(gather_kernel, n),
        out_shape=jax.ShapeDtypeStruct((n, M, 2 * F), BF16),
        in_specs=[VMEM_SPEC, HBM_SPEC, VMEM_SPEC, VMEM_SPEC, VMEM_SPEC],
        out_specs=VMEM_SPEC,
        scratch_shapes=[
            VMEM((n, 2, M, M), BF16), VMEM((2, M, M), F32),
            pltpu.SMEM((1, 2), jnp.int32),
            *[DMA((2, quads))] * 2, *[DMA((quads,))] * 4, DMA, DMA,
        ],
        compiler_params=pltpu.CompilerParams(
            vmem_limit_bytes=24 * MIB, collective_id=1, has_side_effects=True
        ),
        name="gather",
    )(coefficient, in_hbm[0], taper, turned, wave)

    update = pl.pallas_call(
        functools.partial(backward_kernel, n),
        out_shape=jax.ShapeDtypeStruct((2, F, F), BF16),
        in_specs=[SMEM_SPEC, VMEM_SPEC, VMEM_SPEC],
        out_specs=HBM_SPEC,
        scratch_shapes=[
            VMEM((2, F // M, WIDE, M), F32), VMEM((F, 2 * F), BF16), VMEM((2, F, F), BF16), DMA((2, 2)),
        ],
        compiler_params=plain,
        name="backward",
    )(soff_t, pieces, basis)
    return (residual, update[None])


def solution(mesh):
    placed = (
        P(("groups", "facet"), None, None, None),
        P(("groups", "facet"), None),
        P("groups", None),
        P(("groups", "facet")),
        P(("groups", "facet")),
        P(("groups", "facet"), None),
        P(("groups", "facet"), None, None, None),
    )
    return jax.shard_map(
        per_device,
        mesh=mesh,
        in_specs=placed,
        out_specs=(
            P(("groups", "facet"), None, None, None),
            P(("groups", "facet"), None, None, None),
        ),
        check_vma=False,
    )
```

```python
import functools
import math

import jax
import jax.numpy as jnp
import ml_dtypes
import numpy as np
from jax import lax
from jax.experimental import pallas as pl
from jax.experimental.pallas import tpu as pltpu
from jax.sharding import PartitionSpec as P

F = 512
M = 128
SG = 512
TV = 128
WIDE = F + M
HALF, BLOCK = F // 2, (F + M) // 2
GROUP = 4

BF16 = jnp.bfloat16
F32 = jnp.float32
TWO_PI = 2.0 * math.pi
MESH = pl.DeviceIdType.MESH
VMEM = pltpu.VMEM
MIB = 1024 * 1024


def basis_table():
    index = np.arange(F)
    angle = -TWO_PI * (index[:, None] * index[None, :] % F) / F
    scale = 1.0 / math.sqrt(F)
    return np.stack([np.cos(angle) * scale, np.sin(angle) * scale]).astype(ml_dtypes.bfloat16)


def padding_table(facet_count):
    angle = TWO_PI * (np.arange(SG)[:, None] * np.arange(M)[None, :] % SG) / SG
    scale = (M * math.sqrt(facet_count)) ** (-0.5)
    return np.stack([np.cos(angle) * scale, np.sin(angle) * scale]).astype(ml_dtypes.bfloat16)


def taper_square():
    taper = 0.6 + 0.4 * np.sin(math.pi * (np.arange(M) + 0.5) / M)
    return (taper[:, None] * taper[None, :]).astype(np.float32)


def dot(left, right):
    return jnp.dot(left, right, preferred_element_type=F32)


def cos_sin_turns(turns):
    quarter = jnp.floor(turns * 4.0 + 0.5)
    y = (turns - quarter * 0.25) * TWO_PI
    y2 = y * y
    sine = y * (1.0 + y2 * (-1.0 / 6 + y2 * (1.0 / 120 + y2 * (-1.0 / 5040 + y2 * (1.0 / 362880)))))
    cosine = 1.0 + y2 * (
        -0.5 + y2 * (1.0 / 24 + y2 * (-1.0 / 720 + y2 * (1.0 / 40320 - y2 * (1.0 / 3628800))))
    )
    which = quarter.astype(jnp.int32) & 3
    odd = (which & 1) == 1
    first = jnp.where(odd, sine, cosine)
    second = jnp.where(odd, cosine, sine)
    cos_value = jnp.where((which == 1) | (which == 2), -first, first)
    sin_value = jnp.where(which >= 2, -second, second)
    return cos_value, sin_value


def tapered_phase(offset_ref, taper_ref):
    spot = lax.broadcasted_iota(jnp.int32, (M, M), 0)
    rows = 2 * (spot & (M // 2 - 1)) + spot // (M // 2)
    columns = lax.broadcasted_iota(jnp.int32, (M, M), 1)
    total = (rows * offset_ref[0, 0] + columns * offset_ref[0, 1]) & (F - 1)
    cos_value, sin_value = cos_sin_turns(total.astype(F32) * (1.0 / F))
    taper = taper_ref[...]
    return cos_value * taper, sin_value * taper


def place(n):
    me = lax.axis_index("facet")
    quads = n // 4
    far_first = [1 + (t + quads // 2 - 1) % (quads - 1) for t in range(quads - 1)]
    return quads, me // 4, lax.rem(me // 2, 2), lax.rem(me, 2), far_first


def index(quad, middle, core):
    return quad * 4 + middle * 2 + core


def greet(peers):
    barrier = pltpu.get_barrier_semaphore()
    for peer in peers:
        pl.semaphore_signal(barrier, inc=1, device_id={"facet": peer}, device_id_type=MESH)
    pl.semaphore_wait(barrier, len(peers))


def send(src, dst, send_sem, recv_sem, peer):
    return pltpu.make_async_remote_copy(
        src_ref=src, dst_ref=dst, send_sem=send_sem, recv_sem=recv_sem,
        device_id={"facet": peer}, device_id_type=MESH,
    )


def fill_screen(w_value, screen):
    @pl.loop(0, 4)
    def _(c):
        rows = pl.ds(pl.multiple_of(c * 128, 128), 128)
        u = (lax.broadcasted_iota(jnp.int32, (128, SG), 0) + (c * 128 - 256)).astype(F32)
        v = (lax.broadcasted_iota(jnp.int32, (128, SG), 1) - 256).astype(F32)
        radius = (u * u + v * v) * (1.0 / (SG * SG))
        cos_value, sin_value = cos_sin_turns(w_value * (jnp.sqrt(1.0 + radius) - 1.0))
        screen[0, rows, :] = cos_value
        screen[1, rows, :] = sin_value


def tap_values():
    taps = np.arange(5, dtype=np.float32)
    value = 0.75 * np.exp(-(taps / 1.5) * (taps / 1.5))
    return [float(x) for x in value.astype(ml_dtypes.bfloat16).astype(np.float32)]


def smooth_table():
    order = np.concatenate([np.arange(0, SG, 2), np.arange(1, SG, 2)])
    distance = np.abs(np.arange(SG)[None, :] - order[:, None])
    taps = np.array(tap_values() + [0.0], np.float32)
    return taps[np.minimum(distance, 5)].astype(ml_dtypes.bfloat16)


def kernel_table():
    distance = np.abs(np.arange(2 * TV)[None, :] - 2 * np.arange(TV)[:, None] - 1)
    taps = np.array(tap_values() + [0.0], np.float32)
    return taps[np.minimum(distance, 5)].astype(ml_dtypes.bfloat16)


def edge_values(position, offset, spot):
    i = spot & 7
    slot = jnp.where(i < 2, i, i + (TV - 8))
    distance = jnp.abs(position - offset - 2 * slot - 1)
    value = jnp.zeros(distance.shape, F32)
    for step, tap in enumerate(tap_values()):
        value = jnp.where(distance == step, tap, value)
    inside = (position >= offset) & (position < offset + 2 * TV) & ((i < 2) | (i >= 6))
    return jnp.where(inside, value, 0.0).astype(BF16)


def fill_rows(slots, toff, wide):
    @pl.loop(0, slots // 2)
    def _(c):
        spot = lax.broadcasted_iota(jnp.int32, (16, SG), 0)
        lane = lax.broadcasted_iota(jnp.int32, (16, SG), 1)
        offset = jnp.where(spot < 8, toff[0, 2 * c], toff[0, 2 * c + 1])
        wide[pl.ds(pl.multiple_of(SG + c * 16, 16), 16), :] = edge_values(lane, offset, spot)


def fill_columns(slots, toff, wide_t):
    lane = lax.broadcasted_iota(jnp.int32, (1, 8 * slots), 1)
    offset = jnp.zeros_like(lane)
    for t in range(slots):
        offset = jnp.where(lane >> 3 == t, toff[0, t], offset)

    @pl.loop(0, SG // 64)
    def _(c):
        position = lax.broadcasted_iota(jnp.int32, (64, 8 * slots), 0) + c * 64
        spot = lax.broadcasted_iota(jnp.int32, (64, 8 * slots), 1)
        wide_t[pl.ds(pl.multiple_of(c * 64, 64), 64), SG:] = edge_values(position, offset, spot)


def forward_kernel(
    n, slots, w_ref, foff_h, soff_h, toff_h, facet_h, fold_h, taper_h, smooth_h, smooth_t_h,
    pad_h, pad_t_h, pad_a_h, pad_at_h, ker_h, ker_t_h, turned_h, fold_t_h, cutter_h, observed_h,
    summed, screen, wide, wide_t, fold_t, taper, pad, pad_t, pad_a, pad_at, ker, ker_t, turned, observed, wave,
    spec, phase, foff, soff, toff, facet, fold, cutter,
    outgoing, own, near, pair, mid, quad_sum, far,
    load_s, near_s, near_r, mid_s, mid_r, far_s, far_r
):
    pairs = (
        (foff_h, foff), (taper_h, taper), (soff_h, soff), (fold_h, fold), (facet_h, facet),
        (toff_h, toff), (cutter_h, cutter), (smooth_h, wide.at[0:SG]), (smooth_t_h, wide_t.at[:, 0:SG]), (observed_h, observed),
        (pad_h, pad), (pad_t_h, pad_t), (ker_h, ker), (ker_t_h, ker_t), (turned_h, turned),
        (pad_a_h, pad_a), (pad_at_h, pad_at), (fold_t_h, fold_t),
    )
    loads = [pltpu.make_async_copy(src, dst, load_s.at[i]) for i, (src, dst) in enumerate(pairs)]
    for load in loads[:7]:
        load.start()

    quads = n // 4
    me = lax.axis_index("facet")
    quad, middle, core = me // 4, lax.rem(me // 2, 2), lax.rem(me, 2)
    other, odd, group = 1 - middle, lax.rem(quad, 2), quad // 2
    mate = quad + 1 - 2 * odd
    sibling, beside = index(quad, middle, 1 - core), index(quad, other, core)
    high = quad // (quads // 2)
    inner_side = jnp.where(high == odd, 0, 1)

    def turn(k):
        spot = quads - 2 - inner_side
        far_k = jnp.where(k > spot, k - 1, k)
        down = quads - 1 - far_k
        down = jnp.where(down < 2 * group + 2, down - 2, down)
        up = jnp.where(far_k >= 2 * group, far_k + 2, far_k)
        j = jnp.where(k == spot, mate, jnp.where(high == 1, up, down))
        return jnp.where(k == quads - 1, quad, j)

    order = [turn(k) for k in range(4)] if quads == 4 else None

    def each(count, body):
        if quads == 4:
            for j in order[:count]:
                body(j)
        else:

            @pl.loop(0, count)
            def _(k):
                body(turn(k))

    barrier = pltpu.get_barrier_semaphore()
    peers = [index(lax.rem(quad + k, quads), middle, core) for k in range(1, quads)] + [beside, sibling]
    for peer in peers:
        pl.semaphore_signal(barrier, inc=1, device_id={"facet": peer}, device_id_type=MESH)

    loads[0].wait()
    loads[1].wait()
    phase[0], phase[1] = tapered_phase(foff, taper)
    loads[2].wait()
    lane = lax.broadcasted_iota(jnp.int32, (8, F), 1)

    @pl.loop(0, n, unroll=2)
    def _(s):
        turns = ((lane * soff[1, s]) & (F - 1)).astype(F32) * (1.0 / F)
        wave[s, 0], wave[s, 1] = cos_sin_turns(turns)

    loads[3].wait()
    loads[4].wait()
    for load in loads[7:]:
        load.start()

    @pl.loop(0, 2)
    def _(c):
        cols = pl.ds(pl.multiple_of(c * 256, 256), 256)
        upper = [facet[plane, 0:HALF, cols].astype(F32) for plane in range(2)]
        lower = [facet[plane, HALF:F, cols].astype(F32) for plane in range(2)]
        for parity in range(2):
            xr, xi = [
                (u - v if parity else u + v).astype(BF16) for u, v in zip(upper, lower)
            ]
            rows = slice(parity * HALF, parity * HALF + HALF)
            real = dot(fold[0, rows], xr) - dot(fold[1, rows], xi)
            imag = dot(fold[0, rows], xi) + dot(fold[1, rows], xr)
            base = parity * BLOCK
            for side in range(2):
                part = slice(side * M, side * M + M)
                for plane, value in enumerate((real, imag)):
                    spec[plane, c * 2 + side, base : base + HALF] = value[:, part]
                    spec[plane, c * 2 + side, base + HALF : base + BLOCK] = value[0 : M // 2, part]

    loads[5].wait()
    loads[6].wait()

    def cut(s, target, where):
        sx = soff[0, s]
        parity = sx & 1
        starts = (parity * BLOCK + (sx >> 1), (1 - parity) * BLOCK + ((sx + 1) >> 1))
        real, imag = [], []
        for tile in range(F // M):
            part = slice(tile * M, tile * M + M)
            cv, sv = wave[s, 0, :, part][None], wave[s, 1, :, part][None]
            r, i = [
                jnp.concatenate([spec[plane, tile, pl.ds(start, M // 2)] for start in starts], axis=0).reshape(
                    M // 8, 8, M
                )
                for plane in range(2)
            ]
            real.append((cv * r + sv * i).reshape(M, M).astype(BF16))
            imag.append((cv * i - sv * r).reshape(M, M).astype(BF16))
        both = dot(jnp.concatenate(real + imag, axis=1), cutter[...])
        real, imag = both[:, 0:M], both[:, M:]
        pc, ps = phase[0], phase[1]
        target[where[0], where[1], 0] = (pc * real - ps * imag).astype(BF16)
        target[where[0], where[1], 1] = (pc * imag + ps * real).astype(BF16)

    def near_copy(h, j):
        return send(outgoing.at[h, j], near.at[h, j], near_s.at[h, j], near_r.at[h, j], sibling)

    def mid_copy(j, p):
        return send(pair.at[j, p], mid.at[j, p], mid_s.at[j, p], mid_r.at[j, p], beside)

    def far_copy(j, slot, p):
        return send(quad_sum.at[j, p], far.at[slot, p], far_s.at[j, p], far_r.at[slot, p], index(j, middle, core))

    def near_sum(h, j, p):
        return own[h, j, p].astype(F32) + near[h, j, p].astype(F32)

    def mid_sum(j, p):
        return near_sum(1, j, p) + mid[j, p].astype(F32)

    pl.semaphore_wait(barrier, len(peers))

    def give(h, half, j):
        cut(index(j, half, 1 - core), outgoing, (h, j))
        near_copy(h, j).start()

    def keep(h, half, j):
        cut(index(j, half, core), own, (h, j))

    def pass_on(j):
        near_copy(0, j).wait_recv()
        for p in range(2):
            pair[j, p] = near_sum(0, j, p).astype(BF16)
            mid_copy(j, p).start()

    if quads == 4:
        give(0, other, order[0])
        give(0, other, order[1])
        keep(0, other, order[0])
        give(0, other, order[2])
        keep(0, other, order[1])
        give(0, other, order[3])
        pass_on(order[0])
        keep(0, other, order[2])
        pass_on(order[1])
        keep(0, other, order[3])
        pass_on(order[2])
        pass_on(order[3])
    else:
        each(quads, lambda j: give(0, other, j))
        each(quads, lambda j: keep(0, other, j))
        each(quads, pass_on)
    each(quads, lambda j: give(1, middle, j))
    each(quads, lambda j: keep(1, middle, j))
    def combine(j):
        near_copy(1, j).wait_recv()
        for p in range(2):
            mid_copy(j, p).wait_recv()

            quad_sum[j, p] = mid_sum(j, p).astype(BF16)
            far_copy(j, quad, p).start()

    if quads == 4:
        combine(order[0])
        fill_rows(slots, toff, wide)
        combine(order[1])
        fill_columns(slots, toff, wide_t)
        combine(order[2])
    else:
        each(quads - 1, combine)
        fill_rows(slots, toff, wide)
        fill_columns(slots, toff, wide_t)
    fill_screen(w_ref[0], screen)
    near_copy(1, quad).wait_recv()
    for p in range(2):
        mid_copy(quad, p).wait_recv()
        summed[p] = mid_sum(quad, p)
    for k in range(quads - 1):
        slot = order[2 - k] if quads == 4 else turn(k)
        for p in range(2):
            far_copy(quad, slot, p).wait_recv()
            summed[p] += far[slot, p].astype(F32)
    for load in loads[7:]:
        load.wait()

    def finish(j):
        near_copy(0, j).wait_send()
        near_copy(1, j).wait_send()
        for p in range(2):
            mid_copy(j, p).wait_send()

    def finish_far(j):
        for p in range(2):

            far_copy(j, quad, p).wait_send()

    each(quads, finish)
    each(quads - 1, finish_far)


def subgrid_kernel(
    slots, count_ref, toff_h, summed, screen, wide, wide_t, pad, pad_t, pad_a, pad_at, ker, ker_t, observed,
    residual_h, coefficient, inner, model, grid, spread, sent, toff, sems, load_s
):
    load = pltpu.make_async_copy(toff_h, toff, load_s)
    load.start()
    groups = slots // GROUP
    sr, si = summed[0], summed[1]
    stacked = jnp.concatenate(
        [jnp.concatenate([sr, si], axis=1), jnp.concatenate([-si, sr], axis=1)], axis=0
    ).astype(BF16)
    inner[...] = dot(pad_a[...], stacked).astype(BF16)

    for c in range(2):
        cols = slice(c * 256, c * 256 + 256)
        late = slice(SG + c * 256, SG + c * 256 + 256)
        real, imag = dot(inner[...], pad_t[:, cols]), dot(inner[...], pad_t[:, late])
        cos_value, sin_value = screen[0, :, cols], screen[1, :, cols]
        model[:, cols] = (cos_value * real - sin_value * imag).astype(BF16)
        model[:, late] = (cos_value * imag + sin_value * real).astype(BF16)

    for plane in range(2):
        for c in range(2):
            start = plane * SG + c * 256
            value = dot(wide[...], model[:, start : start + 256])
            for side in range(2):
                grid[plane, c * 2 + side] = value[:, side * 128 : side * 128 + 128]
                spread[plane, c * 2 + side] = jnp.zeros(spread.shape[2:], F32)

    load.wait()
    count = count_ref[0]
    lanes = lax.broadcasted_iota(jnp.int32, (TV, TV), 1)
    subs = lax.broadcasted_iota(jnp.int32, (8, TV), 0)
    top, bottom = subs < 2, subs >= 6

    def out_copy(step):
        tiles = pl.ds(step * GROUP, GROUP)
        return pltpu.make_async_copy(sent.at[tiles], residual_h.at[tiles], sems.at[step])

    filled = (count + GROUP - 1) // GROUP

    @pl.loop(0, filled)
    def _(step):
        slot = [step * GROUP + g for g in range(GROUP)]
        spots, left = [], []
        for t in slot:
            ou, ov = toff[0, t] + 1, toff[1, t]
            rows = pl.ds((ou & 1) * (SG // 2) + (ou >> 1), TV)
            tail = pl.ds(pl.multiple_of(SG + t * 8, 8), 8)
            first, turn = ov >> 7, ov & 127
            tiles = (first, first + 1, jnp.minimum(first + 2, SG // 128 - 1))
            spots.append((rows, tail, tiles, turn))

            def pick(plane, where_rows, size):
                keep = lanes[0:size] >= turn
                part = [grid[plane, k, where_rows] for k in tiles]
                both = [jnp.where(keep, part[k], part[k + 1]) for k in range(2)]
                return jnp.concatenate([pltpu.roll(x, (TV - turn) & 127, 1) for x in both], axis=1)

            for plane in range(2):
                body, edge = pick(plane, rows, TV), pick(plane, tail, 8)
                wide_top = jnp.concatenate([top, top], axis=1)
                wide_bottom = jnp.concatenate([bottom, bottom], axis=1)
                left.append(
                    jnp.concatenate(
                        [
                            jnp.where(wide_top, edge, body[0:8]), body[8 : TV - 8],
                            jnp.where(wide_bottom, edge, body[TV - 8 :]),
                        ],
                        axis=0,
                    ).astype(BF16)
                )
        rest = []
        for g, t in enumerate(slot):
            for plane in range(2):
                predicted = dot(left[g * 2 + plane], ker_t[...])
                value = (observed[t, plane].astype(F32) - predicted).astype(BF16)
                rest.append(jnp.where(t < count, value, jnp.zeros_like(value)))
                sent[t, plane] = rest[-1]
        out_copy(step).start()
        back = [dot(value, ker[...]).astype(BF16).astype(F32) for value in rest]
        for g in range(GROUP):
            rows, tail, tiles, turn = spots[g]
            keep = lanes >= turn
            for plane in range(2):
                value = back[g * 2 + plane]
                one, two = pltpu.roll(value[:, 0:128], turn, 1), pltpu.roll(value[:, 128:], turn, 1)
                blank = jnp.zeros((TV, TV), F32)
                parts = (jnp.where(keep, one, blank), jnp.where(keep, two, one), jnp.where(keep, blank, two))
                for tile, part in zip(tiles, parts):
                    zero = blank[0:8]
                    edge = jnp.where(top, part[0:8], jnp.where(bottom, part[TV - 8 :], zero))
                    body = jnp.concatenate(
                        [jnp.where(top, zero, part[0:8]), part[8 : TV - 8], jnp.where(bottom, zero, part[TV - 8 :])],
                        axis=0,
                    )
                    spread[plane, tile, rows] += body
                    spread[plane, tile, tail] += edge

    @pl.loop(filled, groups)
    def _(step):
        for g in range(GROUP):
            sent[step * GROUP + g] = jnp.zeros(sent.shape[1:], BF16)
        out_copy(step).start()

    for c in range(2):
        cols = slice(c * 256, c * 256 + 256)
        late = slice(SG + c * 256, SG + c * 256 + 256)
        ar, ai = [
            dot(wide_t[...], jnp.concatenate([spread[p, 2 * c], spread[p, 2 * c + 1]], axis=1).astype(BF16))
            for p in range(2)
        ]
        sc, ss = screen[0, :, cols], screen[1, :, cols]
        model[:, cols] = (sc * ar + ss * ai).astype(BF16)
        model[:, late] = (sc * ai - ss * ar).astype(BF16)
    reduced = (
        dot(pad_at[:, 0:SG], model[:, 0:SG]) + dot(pad_at[:, SG:], model[:, SG:])
    ).astype(BF16)
    both = dot(reduced, pad[...])
    coefficient[0] = (both[0:M, 0:M] + both[M:, M:]).astype(BF16)
    coefficient[1] = (both[M:, 0:M] - both[0:M, M:]).astype(BF16)

    @pl.loop(0, groups)
    def _(step):
        out_copy(step).wait()


def gather_kernel(
    n, mine, foff_h, taper, turned, wave, out, arrived, phase, foff,
    near_s, near_r, mid_s, mid_r, far_s, far_r, local, load_s
):
    quads = n // 4
    me = lax.axis_index("facet")
    quad, middle, core = me // 4, lax.rem(me // 2, 2), lax.rem(me, 2)
    other = 1 - middle
    sibling, beside = index(quad, middle, 1 - core), index(quad, other, core)
    load = pltpu.make_async_copy(foff_h, foff, load_s)
    load.start()

    barrier = pltpu.get_barrier_semaphore()
    peers = [index(lax.rem(quad + k, quads), middle, core) for k in range(1, quads)] + [beside, sibling]
    for peer in peers:
        pl.semaphore_signal(barrier, inc=1, device_id={"facet": peer}, device_id_type=MESH)
    pl.semaphore_wait(barrier, len(peers))

    def away(k):
        return lax.rem(quad + 1 + lax.rem(k + quads // 2 - 1, quads - 1), quads)

    def event(i):
        back = lax.rem(quad + quads - 1 - lax.rem(i + quads // 2 - 2, quads - 1), quads)
        return jnp.where(i == 0, quad, back)

    def far_copy(slot, to, p):
        spot = index(slot, middle, core)
        return send(
            mine.at[p], arrived.at[spot, p], far_s.at[to, p], far_r.at[slot, p], index(to, middle, core)
        )

    def mid_copy(j, h, p):
        piece = arrived.at[index(j, h, core), p]
        return send(piece, piece, mid_s.at[j, p], mid_r.at[j, p], beside)

    def near_copy(h, j, side, p):
        piece = arrived.at[index(j, h, side), p]
        return send(piece, piece, near_s.at[h, j, p], near_r.at[h, j, p], sibling)

    def mid_own(p):
        return send(mine.at[p], arrived.at[me, p], mid_s.at[quad, p], mid_r.at[quad, p], beside)

    def near_own(p):
        return send(
            mine.at[p], arrived.at[me, p], near_s.at[middle, quad, p], near_r.at[middle, quad, p], sibling
        )

    own = pltpu.make_async_copy(mine, arrived.at[me], local)
    own.start()
    for k in range(quads - 1):
        for p in range(2):
            far_copy(quad, away(k), p).start()
    for p in range(2):
        mid_own(p).start()
        near_own(p).start()

    load.wait()
    phase[0], phase[1] = tapered_phase(foff, taper)
    own.wait()

    def transform(spot):
        pc, ps = phase[0], phase[1]
        real, imag = arrived[spot, 0].astype(F32), arrived[spot, 1].astype(F32)
        both = jnp.concatenate([pc * real + ps * imag, pc * imag - ps * real], axis=1).astype(BF16)
        for c in range(F // 256):
            cols, late = slice(c * 256, c * 256 + 256), slice(F + c * 256, F + c * 256 + 256)
            real = dot(both, turned[:, cols]).reshape(M // 8, 8, 256)
            imag = dot(both, turned[:, late]).reshape(M // 8, 8, 256)
            cv, sv = wave[spot, 0, :, cols][None], wave[spot, 1, :, cols][None]
            out[spot, :, cols] = (cv * real - sv * imag).reshape(M, 256).astype(BF16)
            out[spot, :, late] = (cv * imag + sv * real).reshape(M, 256).astype(BF16)

    transform(me)

    def take_far(j):
        for p in range(2):
            far_copy(j, j, p).wait_recv()
            mid_copy(j, middle, p).start()
            near_copy(middle, j, core, p).start()

    def take_mid(j):
        for p in range(2):
            mid_copy(j, other, p).wait_recv()
            near_copy(other, j, core, p).start()

    def wait_near(h, j):
        for p in range(2):
            near_copy(h, j, 1 - core, p).wait_recv()

    def step(i, far, mid, late):
        one, two, three = event(i), event(jnp.maximum(i - 2, 0)), event(jnp.maximum(i - 3, 0))
        if far:
            take_far(one)
        if mid:
            take_mid(two)
            wait_near(middle, two)
        if late:
            wait_near(other, three)
        if far:
            transform(index(one, middle, core))
        if mid:
            transform(index(two, other, core))
            transform(index(two, middle, 1 - core))
        if late:
            transform(index(three, other, 1 - core))

    step(1, True, False, False)
    step(2, True, True, False)

    if quads == 4:
        step(3, True, True, True)
    else:

        @pl.loop(3, quads)
        def _(i):
            step(i, True, True, True)

    step(quads, False, True, True)
    step(quads + 1, False, True, True)
    step(quads + 2, False, False, True)
    for p in range(2):
        mid_own(p).wait_send()
        near_own(p).wait_send()
        near_copy(other, quad, core, p).wait_send()

    @pl.loop(1, quads)
    def _(i):
        j = event(i)
        for p in range(2):
            far_copy(quad, j, p).wait_send()
            mid_copy(j, middle, p).wait_send()
            near_copy(middle, j, core, p).wait_send()
            near_copy(other, j, core, p).wait_send()


def backward_kernel(n, soff, pieces, fold_t, out_h, acc, flat, out, sems):
    acc[...] = jnp.zeros_like(acc)

    @pl.loop(0, n, unroll=2)
    def _(s):
        sx = soff[0, s]
        parity = sx & 1
        starts = (parity * BLOCK + (sx >> 1), (1 - parity) * BLOCK + ((sx + 1) >> 1))
        for odd in range(2):
            rows, lines = pl.ds(starts[odd], M // 2), slice(odd * M // 2, odd * M // 2 + M // 2)
            for plane in range(2):
                for k in range(F // M):
                    cols = slice(plane * F + k * M, plane * F + k * M + M)
                    acc[plane, k, rows] += pieces[s, lines, cols].astype(F32)

    for plane in range(2):
        for k in range(F // M):
            cols = slice(plane * F + k * M, plane * F + k * M + M)
            for parity in range(2):
                base, to = parity * BLOCK, parity * HALF
                flat[to : to + M // 2, cols] = (
                    acc[plane, k, base : base + M // 2] + acc[plane, k, base + HALF : base + BLOCK]
                ).astype(BF16)
                flat[to + M // 2 : to + HALF, cols] = acc[plane, k, base + M // 2 : base + HALF].astype(BF16)

    copies = []
    for plane in range(2):
        for c in range(2):
            halves = []
            for parity in range(2):
                lines = slice(parity * HALF, parity * HALF + HALF)
                br, bi = fold_t[0, :, lines], fold_t[1, :, lines]
                real = flat[lines, c * 256 : c * 256 + 256]
                imag = flat[lines, F + c * 256 : F + c * 256 + 256]
                halves.append(dot(br, imag) - dot(bi, real) if plane else dot(br, real) + dot(bi, imag))
            cols = slice(c * 256, c * 256 + 256)
            out[plane, 0:HALF, cols] = (halves[0] + halves[1]).astype(BF16)
            out[plane, HALF:F, cols] = (halves[0] - halves[1]).astype(BF16)
        copies.append(pltpu.make_async_copy(out.at[plane], out_h.at[plane], sems.at[plane]))
        copies[-1].start()
    for copy in copies:
        copy.wait()


SMEM_SPEC = pl.BlockSpec(memory_space=pltpu.SMEM)
VMEM_SPEC = pl.BlockSpec(memory_space=pltpu.VMEM)
HBM_SPEC = pl.BlockSpec(memory_space=pltpu.HBM)
DMA = pltpu.SemaphoreType.DMA


def per_device(facets, facet_offsets, subgrid_offsets, w_terms, tile_count, tile_offsets, observed):
    n = lax.axis_size("facet")
    quads = n // 4
    soff_t, toff_t = subgrid_offsets.T, tile_offsets.T
    slots = observed.shape[0]
    basis_np = basis_table()
    split = np.concatenate([np.arange(0, F, 2), np.arange(1, F, 2)])
    split_m = split[split < M]
    fold = jnp.asarray(np.ascontiguousarray(basis_np[:, split, :HALF]))
    fold_t = jnp.asarray(np.ascontiguousarray(basis_np[:, :HALF, split]))
    br, bi = basis_np[:, :M]
    turned = jnp.asarray(np.block([[br, -bi], [bi, br]]))
    real, imag = padding_table(n)
    pad = jnp.asarray(np.concatenate([real, imag], axis=1))
    pad_t = jnp.asarray(np.block([[real.T, imag.T], [-imag.T, real.T]]))
    ra, ia = real[:, split_m], imag[:, split_m]
    pad_a = jnp.asarray(np.concatenate([ra, ia], axis=1))
    pad_at = jnp.asarray(np.block([[ra.T, ia.T], [-ia.T, ra.T]]))
    taper = jnp.asarray(np.ascontiguousarray(taper_square()[split_m]))
    smooth_np = smooth_table()
    smooth, smooth_t = jnp.asarray(smooth_np), jnp.asarray(np.ascontiguousarray(smooth_np.T))
    ker_np = kernel_table()
    ker, ker_t = jnp.asarray(ker_np), jnp.asarray(np.ascontiguousarray(ker_np.T))
    plain = pltpu.CompilerParams(vmem_limit_bytes=24 * MIB)

    deep = SG + 8 * slots
    piece_shape = (2, M, M)
    cutter = jnp.asarray(np.block([[br.T, bi.T], [-bi.T, br.T]]))
    tables = (fold, taper, smooth, smooth_t, pad, pad_t, pad_a, pad_at, ker, ker_t, turned, fold_t, cutter)
    in_hbm = [
        pltpu.with_memory_space_constraint(x, pltpu.HBM)
        for x in (facet_offsets, soff_t, toff_t, facets[0], *tables, observed)
    ]
    held = (fold_t, taper, pad, pad_t, pad_a, pad_at, ker, ker_t, turned, observed)
    summed, screen, wide, wide_t, fold_t, taper, pad, pad_t, pad_a, pad_at, ker, ker_t, turned, observed, wave = pl.pallas_call(
        functools.partial(forward_kernel, n, slots),
        out_shape=(
            jax.ShapeDtypeStruct((2, M, M), F32), jax.ShapeDtypeStruct((2, SG, SG), F32),
            jax.ShapeDtypeStruct((deep, SG), BF16), jax.ShapeDtypeStruct((SG, deep), BF16),
            *[jax.ShapeDtypeStruct(x.shape, x.dtype) for x in held],
            jax.ShapeDtypeStruct((n, 2, 8, F), F32),
        ),
        in_specs=[SMEM_SPEC] + [HBM_SPEC] * 18,
        out_specs=(VMEM_SPEC,) * 15,
        scratch_shapes=[
            VMEM((2, F // M, WIDE, M), F32), VMEM((2, M, M), F32),
            pltpu.SMEM((1, 2), jnp.int32), pltpu.SMEM((2, n), jnp.int32),
            pltpu.SMEM((2, slots), jnp.int32),
            VMEM((2, F, F), BF16), VMEM((2, F, HALF), BF16), VMEM((2 * F, 2 * M), BF16),
            *[VMEM((2, quads, *piece_shape), BF16)] * 3,
            *[VMEM((quads, *piece_shape), BF16)] * 4,
            DMA((18,)), *[DMA((2, quads))] * 2, *[DMA((quads, 2))] * 4,
        ],
        compiler_params=pltpu.CompilerParams(
            vmem_limit_bytes=32 * MIB, collective_id=0, has_side_effects=True
        ),
        name="forward",
    )(w_terms, *in_hbm)

    residual, coefficient = pl.pallas_call(
        functools.partial(subgrid_kernel, slots),
        out_shape=(
            jax.ShapeDtypeStruct((slots, 2, TV, TV), BF16),
            jax.ShapeDtypeStruct((2, M, M), BF16),
        ),
        in_specs=[SMEM_SPEC, HBM_SPEC] + [VMEM_SPEC] * 11,
        out_specs=(HBM_SPEC, VMEM_SPEC),
        scratch_shapes=[
            VMEM((SG, 2 * M), BF16), VMEM((SG, 2 * SG), BF16),
            VMEM((2, SG // 128, deep, 128), F32), VMEM((2, SG // 128, deep, 128), F32),
            VMEM((slots, 2, TV, TV), BF16),
            pltpu.SMEM((2, slots), jnp.int32), DMA((slots // GROUP,)), DMA,
        ],
        compiler_params=plain,
        name="subgrid",
    )(tile_count, in_hbm[2], summed, screen, wide, wide_t, pad, pad_t, pad_a, pad_at, ker, ker_t, observed)

    pieces = pl.pallas_call(
        functools.partial(gather_kernel, n),
        out_shape=jax.ShapeDtypeStruct((n, M, 2 * F), BF16),
        in_specs=[VMEM_SPEC, HBM_SPEC, VMEM_SPEC, VMEM_SPEC, VMEM_SPEC],
        out_specs=VMEM_SPEC,
        scratch_shapes=[
            VMEM((n, 2, M, M), BF16), VMEM((2, M, M), F32),
            pltpu.SMEM((1, 2), jnp.int32),
            *[DMA((2, quads, 2))] * 2, *[DMA((quads, 2))] * 4, DMA, DMA,
        ],
        compiler_params=pltpu.CompilerParams(
            vmem_limit_bytes=24 * MIB, collective_id=1, has_side_effects=True
        ),
        name="gather",
    )(coefficient, in_hbm[0], taper, turned, wave)

    update = pl.pallas_call(
        functools.partial(backward_kernel, n),
        out_shape=jax.ShapeDtypeStruct((2, F, F), BF16),
        in_specs=[SMEM_SPEC, VMEM_SPEC, VMEM_SPEC],
        out_specs=HBM_SPEC,
        scratch_shapes=[
            VMEM((2, F // M, WIDE, M), F32), VMEM((F, 2 * F), BF16), VMEM((2, F, F), BF16), DMA((2,)),
        ],
        compiler_params=plain,
        name="backward",
    )(soff_t, pieces, fold_t)
    return (residual, update[None])


def solution(mesh):
    placed = (
        P(("groups", "facet"), None, None, None),
        P(("groups", "facet"), None),
        P("groups", None),
        P(("groups", "facet")),
        P(("groups", "facet")),
        P(("groups", "facet"), None),
        P(("groups", "facet"), None, None, None),
    )
    return jax.shard_map(
        per_device,
        mesh=mesh,
        in_specs=placed,
        out_specs=(
            P(("groups", "facet"), None, None, None),
            P(("groups", "facet"), None, None, None),
        ),
        check_vma=False,
    )
```

```python
import functools
import math

import jax
import jax.numpy as jnp
import ml_dtypes
import numpy as np
from jax import lax
from jax.experimental import pallas as pl
from jax.experimental.pallas import tpu as pltpu
from jax.sharding import PartitionSpec as P

F = 512
M = 128
SG = 512
TV = 128
WIDE = F + M
HALF, BLOCK = F // 2, (F + M) // 2
GROUP = 4

BF16 = jnp.bfloat16
F32 = jnp.float32
TWO_PI = 2.0 * math.pi
MESH = pl.DeviceIdType.MESH
VMEM = pltpu.VMEM
MIB = 1024 * 1024


def basis_table():
    index = np.arange(F)
    angle = -TWO_PI * (index[:, None] * index[None, :] % F) / F
    scale = 1.0 / math.sqrt(F)
    return np.stack([np.cos(angle) * scale, np.sin(angle) * scale]).astype(ml_dtypes.bfloat16)


def padding_table(facet_count):
    angle = TWO_PI * (np.arange(SG)[:, None] * np.arange(M)[None, :] % SG) / SG
    scale = (M * math.sqrt(facet_count)) ** (-0.5)
    return np.stack([np.cos(angle) * scale, np.sin(angle) * scale]).astype(ml_dtypes.bfloat16)


def taper_square():
    taper = 0.6 + 0.4 * np.sin(math.pi * (np.arange(M) + 0.5) / M)
    return (taper[:, None] * taper[None, :]).astype(np.float32)


def dot(left, right):
    return jnp.dot(left, right, preferred_element_type=F32)


def cos_sin_turns(turns):
    quarter = jnp.floor(turns * 4.0 + 0.5)
    y = (turns - quarter * 0.25) * TWO_PI
    y2 = y * y
    sine = y * (1.0 + y2 * (-1.0 / 6 + y2 * (1.0 / 120 + y2 * (-1.0 / 5040 + y2 * (1.0 / 362880)))))
    cosine = 1.0 + y2 * (
        -0.5 + y2 * (1.0 / 24 + y2 * (-1.0 / 720 + y2 * (1.0 / 40320 - y2 * (1.0 / 3628800))))
    )
    which = quarter.astype(jnp.int32) & 3
    odd = (which & 1) == 1
    first = jnp.where(odd, sine, cosine)
    second = jnp.where(odd, cosine, sine)
    cos_value = jnp.where((which == 1) | (which == 2), -first, first)
    sin_value = jnp.where(which >= 2, -second, second)
    return cos_value, sin_value


def tapered_phase(offset_ref, taper_ref):
    spot = lax.broadcasted_iota(jnp.int32, (M, M), 0)
    rows = 2 * (spot & (M // 2 - 1)) + spot // (M // 2)
    columns = lax.broadcasted_iota(jnp.int32, (M, M), 1)
    total = (rows * offset_ref[0, 0] + columns * offset_ref[0, 1]) & (F - 1)
    cos_value, sin_value = cos_sin_turns(total.astype(F32) * (1.0 / F))
    taper = taper_ref[...]
    return cos_value * taper, sin_value * taper


def place(n):
    me = lax.axis_index("facet")
    quads = n // 4
    far_first = [1 + (t + quads // 2 - 1) % (quads - 1) for t in range(quads - 1)]
    return quads, me // 4, lax.rem(me // 2, 2), lax.rem(me, 2), far_first


def index(quad, middle, core):
    return quad * 4 + middle * 2 + core


def greet(peers):
    barrier = pltpu.get_barrier_semaphore()
    for peer in peers:
        pl.semaphore_signal(barrier, inc=1, device_id={"facet": peer}, device_id_type=MESH)
    pl.semaphore_wait(barrier, len(peers))


def send(src, dst, send_sem, recv_sem, peer):
    return pltpu.make_async_remote_copy(
        src_ref=src, dst_ref=dst, send_sem=send_sem, recv_sem=recv_sem,
        device_id={"facet": peer}, device_id_type=MESH,
    )


def fill_screen(w_value, screen):
    @pl.loop(0, 4)
    def _(c):
        rows = pl.ds(pl.multiple_of(c * 128, 128), 128)
        u = (lax.broadcasted_iota(jnp.int32, (128, SG), 0) + (c * 128 - 256)).astype(F32)
        v = (lax.broadcasted_iota(jnp.int32, (128, SG), 1) - 256).astype(F32)
        radius = (u * u + v * v) * (1.0 / (SG * SG))
        cos_value, sin_value = cos_sin_turns(w_value * (jnp.sqrt(1.0 + radius) - 1.0))
        screen[0, rows, :] = cos_value
        screen[1, rows, :] = sin_value


def tap_values():
    taps = np.arange(5, dtype=np.float32)
    value = 0.75 * np.exp(-(taps / 1.5) * (taps / 1.5))
    return [float(x) for x in value.astype(ml_dtypes.bfloat16).astype(np.float32)]


def smooth_table():
    order = np.concatenate([np.arange(0, SG, 2), np.arange(1, SG, 2)])
    distance = np.abs(np.arange(SG)[None, :] - order[:, None])
    taps = np.array(tap_values() + [0.0], np.float32)
    return taps[np.minimum(distance, 5)].astype(ml_dtypes.bfloat16)


def kernel_table():
    distance = np.abs(np.arange(2 * TV)[None, :] - 2 * np.arange(TV)[:, None] - 1)
    taps = np.array(tap_values() + [0.0], np.float32)
    return taps[np.minimum(distance, 5)].astype(ml_dtypes.bfloat16)


def edge_values(position, offset, spot):
    i = spot & 7
    slot = jnp.where(i < 2, i, i + (TV - 8))
    distance = jnp.abs(position - offset - 2 * slot - 1)
    value = jnp.zeros(distance.shape, F32)
    for step, tap in enumerate(tap_values()):
        value = jnp.where(distance == step, tap, value)
    inside = (position >= offset) & (position < offset + 2 * TV) & ((i < 2) | (i >= 6))
    return jnp.where(inside, value, 0.0).astype(BF16)


def fill_rows(slots, toff, wide):
    @pl.loop(0, slots // 2)
    def _(c):
        spot = lax.broadcasted_iota(jnp.int32, (16, SG), 0)
        lane = lax.broadcasted_iota(jnp.int32, (16, SG), 1)
        offset = jnp.where(spot < 8, toff[0, 2 * c], toff[0, 2 * c + 1])
        wide[pl.ds(pl.multiple_of(SG + c * 16, 16), 16), :] = edge_values(lane, offset, spot)


def fill_columns(slots, toff, wide_t):
    lane = lax.broadcasted_iota(jnp.int32, (1, 8 * slots), 1)
    offset = jnp.zeros_like(lane)
    for t in range(slots):
        offset = jnp.where(lane >> 3 == t, toff[0, t], offset)

    @pl.loop(0, SG // 64)
    def _(c):
        position = lax.broadcasted_iota(jnp.int32, (64, 8 * slots), 0) + c * 64
        spot = lax.broadcasted_iota(jnp.int32, (64, 8 * slots), 1)
        wide_t[pl.ds(pl.multiple_of(c * 64, 64), 64), SG:] = edge_values(position, offset, spot)


def forward_kernel(
    n, slots, w_ref, foff_h, soff_h, toff_h, facet_h, fold_h, taper_h, smooth_h, smooth_t_h,
    pad_h, pad_t_h, pad_a_h, pad_at_h, ker_h, ker_t_h, turned_h, fold_t_h, cutter_h, observed_h,
    summed, screen, wide, wide_t, fold_t, taper, pad, pad_t, pad_a, pad_at, ker, ker_t, turned, observed, wave,
    spec, phase, foff, soff, toff, facet, fold, cutter,
    outgoing, own, near, pair, mid, quad_sum, far,
    load_s, near_s, near_r, mid_s, mid_r, far_s, far_r
):
    pairs = (
        (foff_h, foff), (taper_h, taper), (soff_h, soff), (fold_h, fold), (facet_h, facet),
        (toff_h, toff), (cutter_h, cutter), (smooth_h, wide.at[0:SG]), (smooth_t_h, wide_t.at[:, 0:SG]), (observed_h, observed),
        (pad_h, pad), (pad_t_h, pad_t), (ker_h, ker), (ker_t_h, ker_t), (turned_h, turned),
        (pad_a_h, pad_a), (pad_at_h, pad_at), (fold_t_h, fold_t),
    )
    loads = [pltpu.make_async_copy(src, dst, load_s.at[i]) for i, (src, dst) in enumerate(pairs)]
    for load in loads[:7]:
        load.start()

    quads = n // 4
    me = lax.axis_index("facet")
    quad, middle, core = me // 4, lax.rem(me // 2, 2), lax.rem(me, 2)
    other, odd, group = 1 - middle, lax.rem(quad, 2), quad // 2
    mate = quad + 1 - 2 * odd
    sibling, beside = index(quad, middle, 1 - core), index(quad, other, core)
    high = quad // (quads // 2)
    inner_side = jnp.where(high == odd, 0, 1)

    def turn(k):
        spot = quads - 2 - inner_side
        far_k = jnp.where(k > spot, k - 1, k)
        down = quads - 1 - far_k
        down = jnp.where(down < 2 * group + 2, down - 2, down)
        up = jnp.where(far_k >= 2 * group, far_k + 2, far_k)
        j = jnp.where(k == spot, mate, jnp.where(high == 1, up, down))
        return jnp.where(k == quads - 1, quad, j)

    order = [turn(k) for k in range(4)] if quads == 4 else None

    def each(count, body):
        if quads == 4:
            for j in order[:count]:
                body(j)
        else:

            @pl.loop(0, count)
            def _(k):
                body(turn(k))

    barrier = pltpu.get_barrier_semaphore()
    peers = [index(lax.rem(quad + k, quads), middle, core) for k in range(1, quads)] + [beside, sibling]
    for peer in peers:
        pl.semaphore_signal(barrier, inc=1, device_id={"facet": peer}, device_id_type=MESH)

    loads[0].wait()
    loads[1].wait()
    phase[0], phase[1] = tapered_phase(foff, taper)
    loads[2].wait()
    lane = lax.broadcasted_iota(jnp.int32, (8, F), 1)

    @pl.loop(0, n, unroll=2)
    def _(s):
        turns = ((lane * soff[1, s]) & (F - 1)).astype(F32) * (1.0 / F)
        wave[s, 0], wave[s, 1] = cos_sin_turns(turns)

    loads[3].wait()
    loads[4].wait()
    for load in loads[7:]:
        load.start()

    @pl.loop(0, 2)
    def _(c):
        cols = pl.ds(pl.multiple_of(c * 256, 256), 256)
        upper = [facet[plane, 0:HALF, cols].astype(F32) for plane in range(2)]
        lower = [facet[plane, HALF:F, cols].astype(F32) for plane in range(2)]
        for parity in range(2):
            xr, xi = [
                (u - v if parity else u + v).astype(BF16) for u, v in zip(upper, lower)
            ]
            rows = slice(parity * HALF, parity * HALF + HALF)
            real = dot(fold[0, rows], xr) - dot(fold[1, rows], xi)
            imag = dot(fold[0, rows], xi) + dot(fold[1, rows], xr)
            base = parity * BLOCK
            for side in range(2):
                part = slice(side * M, side * M + M)
                for plane, value in enumerate((real, imag)):
                    spec[plane, c * 2 + side, base : base + HALF] = value[:, part]
                    spec[plane, c * 2 + side, base + HALF : base + BLOCK] = value[0 : M // 2, part]

    loads[5].wait()
    loads[6].wait()

    def cut(s, target, where):
        sx = soff[0, s]
        parity = sx & 1
        starts = (parity * BLOCK + (sx >> 1), (1 - parity) * BLOCK + ((sx + 1) >> 1))
        real, imag = [], []
        for tile in range(F // M):
            part = slice(tile * M, tile * M + M)
            cv, sv = wave[s, 0, :, part][None], wave[s, 1, :, part][None]
            r, i = [
                jnp.concatenate([spec[plane, tile, pl.ds(start, M // 2)] for start in starts], axis=0).reshape(
                    M // 8, 8, M
                )
                for plane in range(2)
            ]
            real.append((cv * r + sv * i).reshape(M, M).astype(BF16))
            imag.append((cv * i - sv * r).reshape(M, M).astype(BF16))
        both = dot(jnp.concatenate(real + imag, axis=1), cutter[...])
        real, imag = both[:, 0:M], both[:, M:]
        pc, ps = phase[0], phase[1]
        target[where[0], where[1], 0] = (pc * real - ps * imag).astype(BF16)
        target[where[0], where[1], 1] = (pc * imag + ps * real).astype(BF16)

    def near_copy(h, j):
        return send(outgoing.at[h, j], near.at[h, j], near_s.at[h, j], near_r.at[h, j], sibling)

    def mid_copy(j, p):
        return send(pair.at[j, p], mid.at[j, p], mid_s.at[j, p], mid_r.at[j, p], beside)

    def far_copy(j, slot, p):
        return send(quad_sum.at[j, p], far.at[slot, p], far_s.at[j, p], far_r.at[slot, p], index(j, middle, core))

    def near_sum(h, j, p):
        return own[h, j, p].astype(F32) + near[h, j, p].astype(F32)

    def mid_sum(j, p):
        return near_sum(1, j, p) + mid[j, p].astype(F32)

    pl.semaphore_wait(barrier, len(peers))

    def give(h, half, j):
        cut(index(j, half, 1 - core), outgoing, (h, j))
        near_copy(h, j).start()

    def keep(h, half, j):
        cut(index(j, half, core), own, (h, j))

    def pass_on(j):
        near_copy(0, j).wait_recv()
        for p in range(2):
            pair[j, p] = near_sum(0, j, p).astype(BF16)
            mid_copy(j, p).start()

    if quads == 4:
        give(0, other, order[0])
        give(0, other, order[1])
        keep(0, other, order[0])
        give(0, other, order[2])
        keep(0, other, order[1])
        give(0, other, order[3])
        pass_on(order[0])
        keep(0, other, order[2])
        pass_on(order[1])
        keep(0, other, order[3])
        pass_on(order[2])
        pass_on(order[3])
    else:
        each(quads, lambda j: give(0, other, j))
        each(quads, lambda j: keep(0, other, j))
        each(quads, pass_on)
    each(quads, lambda j: give(1, middle, j))
    each(quads, lambda j: keep(1, middle, j))
    def combine(j):
        near_copy(1, j).wait_recv()
        for p in range(2):
            mid_copy(j, p).wait_recv()

            quad_sum[j, p] = mid_sum(j, p).astype(BF16)
            far_copy(j, quad, p).start()

    if quads == 4:
        combine(order[0])
        fill_rows(slots, toff, wide)
        combine(order[1])
        fill_columns(slots, toff, wide_t)
        combine(order[2])
    else:
        each(quads - 1, combine)
        fill_rows(slots, toff, wide)
        fill_columns(slots, toff, wide_t)
    fill_screen(w_ref[0], screen)
    near_copy(1, quad).wait_recv()
    for p in range(2):
        mid_copy(quad, p).wait_recv()
        summed[p] = mid_sum(quad, p)
    for k in range(quads - 1):
        slot = order[2 - k] if quads == 4 else turn(k)
        for p in range(2):
            far_copy(quad, slot, p).wait_recv()
            summed[p] += far[slot, p].astype(F32)
    for load in loads[7:]:
        load.wait()

    def finish(j):
        near_copy(0, j).wait_send()
        near_copy(1, j).wait_send()
        for p in range(2):
            mid_copy(j, p).wait_send()

    def finish_far(j):
        for p in range(2):

            far_copy(j, quad, p).wait_send()

    each(quads, finish)
    each(quads - 1, finish_far)


def subgrid_kernel(
    slots, count_ref, toff_h, summed, screen, wide, wide_t, pad, pad_t, pad_a, pad_at, ker, ker_t, observed,
    residual_h, coefficient, inner, model, grid, spread, sent, toff, sems, load_s
):
    load = pltpu.make_async_copy(toff_h, toff, load_s)
    load.start()
    groups = slots // GROUP
    sr, si = summed[0], summed[1]
    stacked = jnp.concatenate(
        [jnp.concatenate([sr, si], axis=1), jnp.concatenate([-si, sr], axis=1)], axis=0
    ).astype(BF16)
    inner[...] = dot(pad_a[...], stacked).astype(BF16)

    for c in range(2):
        cols = slice(c * 256, c * 256 + 256)
        late = slice(SG + c * 256, SG + c * 256 + 256)
        real, imag = dot(inner[...], pad_t[:, cols]), dot(inner[...], pad_t[:, late])
        cos_value, sin_value = screen[0, :, cols], screen[1, :, cols]
        model[:, cols] = (cos_value * real - sin_value * imag).astype(BF16)
        model[:, late] = (cos_value * imag + sin_value * real).astype(BF16)

    for plane in range(2):
        for c in range(2):
            start = plane * SG + c * 256
            value = dot(wide[...], model[:, start : start + 256])
            for side in range(2):
                grid[plane, c * 2 + side] = value[:, side * 128 : side * 128 + 128]
                spread[plane, c * 2 + side] = jnp.zeros(spread.shape[2:], F32)

    load.wait()
    count = count_ref[0]
    lanes = lax.broadcasted_iota(jnp.int32, (TV, TV), 1)
    subs = lax.broadcasted_iota(jnp.int32, (8, TV), 0)
    top, bottom = subs < 2, subs >= 6

    def out_copy(step):
        tiles = pl.ds(step * GROUP, GROUP)
        return pltpu.make_async_copy(sent.at[tiles], residual_h.at[tiles], sems.at[step])

    filled = (count + GROUP - 1) // GROUP

    @pl.loop(0, filled)
    def _(step):
        slot = [step * GROUP + g for g in range(GROUP)]
        spots, left = [], []
        for t in slot:
            ou, ov = toff[0, t] + 1, toff[1, t]
            rows = pl.ds((ou & 1) * (SG // 2) + (ou >> 1), TV)
            tail = pl.ds(pl.multiple_of(SG + t * 8, 8), 8)
            first, turn = ov >> 7, ov & 127
            tiles = (first, first + 1, jnp.minimum(first + 2, SG // 128 - 1))
            spots.append((rows, tail, tiles, turn))

            def pick(plane, where_rows, size):
                keep = lanes[0:size] >= turn
                part = [grid[plane, k, where_rows] for k in tiles]
                both = [jnp.where(keep, part[k], part[k + 1]) for k in range(2)]
                return jnp.concatenate([pltpu.roll(x, (TV - turn) & 127, 1) for x in both], axis=1)

            for plane in range(2):
                body, edge = pick(plane, rows, TV), pick(plane, tail, 8)
                wide_top = jnp.concatenate([top, top], axis=1)
                wide_bottom = jnp.concatenate([bottom, bottom], axis=1)
                left.append(
                    jnp.concatenate(
                        [
                            jnp.where(wide_top, edge, body[0:8]), body[8 : TV - 8],
                            jnp.where(wide_bottom, edge, body[TV - 8 :]),
                        ],
                        axis=0,
                    ).astype(BF16)
                )
        rest = []
        for g, t in enumerate(slot):
            for plane in range(2):
                predicted = dot(left[g * 2 + plane], ker_t[...])
                value = (observed[t, plane].astype(F32) - predicted).astype(BF16)
                rest.append(jnp.where(t < count, value, jnp.zeros_like(value)))
                sent[t, plane] = rest[-1]
        out_copy(step).start()
        back = [dot(value, ker[...]).astype(BF16).astype(F32) for value in rest]
        for g in range(GROUP):
            rows, tail, tiles, turn = spots[g]
            keep = lanes >= turn
            for plane in range(2):
                value = back[g * 2 + plane]
                one, two = pltpu.roll(value[:, 0:128], turn, 1), pltpu.roll(value[:, 128:], turn, 1)
                blank = jnp.zeros((TV, TV), F32)
                parts = (jnp.where(keep, one, blank), jnp.where(keep, two, one), jnp.where(keep, blank, two))
                for tile, part in zip(tiles, parts):
                    zero = blank[0:8]
                    edge = jnp.where(top, part[0:8], jnp.where(bottom, part[TV - 8 :], zero))
                    body = jnp.concatenate(
                        [jnp.where(top, zero, part[0:8]), part[8 : TV - 8], jnp.where(bottom, zero, part[TV - 8 :])],
                        axis=0,
                    )
                    spread[plane, tile, rows] += body
                    spread[plane, tile, tail] += edge

    @pl.loop(filled, groups)
    def _(step):
        for g in range(GROUP):
            sent[step * GROUP + g] = jnp.zeros(sent.shape[1:], BF16)
        out_copy(step).start()

    for c in range(2):
        cols = slice(c * 256, c * 256 + 256)
        late = slice(SG + c * 256, SG + c * 256 + 256)
        ar, ai = [
            dot(wide_t[...], jnp.concatenate([spread[p, 2 * c], spread[p, 2 * c + 1]], axis=1).astype(BF16))
            for p in range(2)
        ]
        sc, ss = screen[0, :, cols], screen[1, :, cols]
        model[:, cols] = (sc * ar + ss * ai).astype(BF16)
        model[:, late] = (sc * ai - ss * ar).astype(BF16)
    reduced = (
        dot(pad_at[:, 0:SG], model[:, 0:SG]) + dot(pad_at[:, SG:], model[:, SG:])
    ).astype(BF16)
    both = dot(reduced, pad[...])
    coefficient[0] = (both[0:M, 0:M] + both[M:, M:]).astype(BF16)
    coefficient[1] = (both[M:, 0:M] - both[0:M, M:]).astype(BF16)

    @pl.loop(0, groups)
    def _(step):
        out_copy(step).wait()


def gather_kernel(
    n, mine, foff_h, taper, turned, wave, out, blank, arrived, phase, foff,
    near_s, near_r, mid_s, mid_r, far_s, far_r, local, load_s
):
    quads = n // 4
    me = lax.axis_index("facet")
    quad, middle, core = me // 4, lax.rem(me // 2, 2), lax.rem(me, 2)
    other = 1 - middle
    sibling, beside = index(quad, middle, 1 - core), index(quad, other, core)
    load = pltpu.make_async_copy(foff_h, foff, load_s)
    load.start()

    barrier = pltpu.get_barrier_semaphore()
    peers = [index(lax.rem(quad + k, quads), middle, core) for k in range(1, quads)] + [beside, sibling]
    for peer in peers:
        pl.semaphore_signal(barrier, inc=1, device_id={"facet": peer}, device_id_type=MESH)
    pl.semaphore_wait(barrier, len(peers))

    def away(k):
        return lax.rem(quad + 1 + lax.rem(k + quads // 2 - 1, quads - 1), quads)

    def event(i):
        back = lax.rem(quad + quads - 1 - lax.rem(i + quads // 2 - 2, quads - 1), quads)
        return jnp.where(i == 0, quad, back)

    def far_copy(slot, to, p):
        spot = index(slot, middle, core)
        return send(
            mine.at[p], arrived.at[spot, p], far_s.at[to, p], far_r.at[slot, p], index(to, middle, core)
        )

    def mid_copy(j, h, p):
        piece = arrived.at[index(j, h, core), p]
        return send(piece, piece, mid_s.at[j, p], mid_r.at[j, p], beside)

    def near_copy(h, j, side, p):
        piece = arrived.at[index(j, h, side), p]
        return send(piece, piece, near_s.at[h, j, p], near_r.at[h, j, p], sibling)

    def mid_own(p):
        return send(mine.at[p], arrived.at[me, p], mid_s.at[quad, p], mid_r.at[quad, p], beside)

    def near_own(p):
        return send(
            mine.at[p], arrived.at[me, p], near_s.at[middle, quad, p], near_r.at[middle, quad, p], sibling
        )

    own = pltpu.make_async_copy(mine, arrived.at[me], local)
    own.start()
    for k in range(quads - 1):
        for p in range(2):
            far_copy(quad, away(k), p).start()
    for p in range(2):
        mid_own(p).start()
        near_own(p).start()

    load.wait()
    phase[0], phase[1] = tapered_phase(foff, taper)
    own.wait()

    def transform(spot):
        pc, ps = phase[0], phase[1]
        real, imag = arrived[spot, 0].astype(F32), arrived[spot, 1].astype(F32)
        both = jnp.concatenate([pc * real + ps * imag, pc * imag - ps * real], axis=1).astype(BF16)
        for c in range(F // 256):
            cols, late = slice(c * 256, c * 256 + 256), slice(F + c * 256, F + c * 256 + 256)
            real = dot(both, turned[:, cols]).reshape(M // 8, 8, 256)
            imag = dot(both, turned[:, late]).reshape(M // 8, 8, 256)
            cv, sv = wave[spot, 0, :, cols][None], wave[spot, 1, :, cols][None]
            out[spot, :, cols] = (cv * real - sv * imag).reshape(M, 256).astype(BF16)
            out[spot, :, late] = (cv * imag + sv * real).reshape(M, 256).astype(BF16)

    transform(me)
    blank[...] = jnp.zeros_like(blank)

    def take_far(j):
        for p in range(2):
            far_copy(j, j, p).wait_recv()
            mid_copy(j, middle, p).start()
            near_copy(middle, j, core, p).start()

    def take_mid(j):
        for p in range(2):
            mid_copy(j, other, p).wait_recv()
            near_copy(other, j, core, p).start()

    def wait_near(h, j):
        for p in range(2):
            near_copy(h, j, 1 - core, p).wait_recv()

    def step(i, far, mid, late):
        one, two, three = event(i), event(jnp.maximum(i - 2, 0)), event(jnp.maximum(i - 3, 0))
        if far:
            take_far(one)
        if mid:
            take_mid(two)
            wait_near(middle, two)
        if late:
            wait_near(other, three)
        if far:
            transform(index(one, middle, core))
        if mid:
            transform(index(two, other, core))
            transform(index(two, middle, 1 - core))
        if late:
            transform(index(three, other, 1 - core))

    step(1, True, False, False)
    step(2, True, True, False)

    if quads == 4:
        step(3, True, True, True)
    else:

        @pl.loop(3, quads)
        def _(i):
            step(i, True, True, True)

    step(quads, False, True, True)
    step(quads + 1, False, True, True)
    step(quads + 2, False, False, True)
    for p in range(2):
        mid_own(p).wait_send()
        near_own(p).wait_send()
        near_copy(other, quad, core, p).wait_send()

    @pl.loop(1, quads)
    def _(i):
        j = event(i)
        for p in range(2):
            far_copy(quad, j, p).wait_send()
            mid_copy(j, middle, p).wait_send()
            near_copy(middle, j, core, p).wait_send()
            near_copy(other, j, core, p).wait_send()


def backward_kernel(n, soff, pieces, fold_t, blank, out_h, acc, flat, out, sems):
    @pl.loop(0, n, unroll=4)
    def _(s):
        sx = soff[0, s]
        parity = sx & 1
        starts = (parity * BLOCK + (sx >> 1), (1 - parity) * BLOCK + ((sx + 1) >> 1))
        for odd in range(2):
            rows, lines = pl.ds(starts[odd], M // 2), slice(odd * M // 2, odd * M // 2 + M // 2)
            for plane in range(2):
                for k in range(F // M):
                    cols = slice(plane * F + k * M, plane * F + k * M + M)
                    acc[plane, k, rows] += pieces[s, lines, cols].astype(F32)

    for plane in range(2):
        for k in range(F // M):
            cols = slice(plane * F + k * M, plane * F + k * M + M)
            for parity in range(2):
                base, to = parity * BLOCK, parity * HALF
                flat[to : to + M // 2, cols] = (
                    acc[plane, k, base : base + M // 2] + acc[plane, k, base + HALF : base + BLOCK]
                ).astype(BF16)
                flat[to + M // 2 : to + HALF, cols] = acc[plane, k, base + M // 2 : base + HALF].astype(BF16)

    copies = []
    for plane in range(2):
        for c in range(2):
            halves = []
            for parity in range(2):
                lines = slice(parity * HALF, parity * HALF + HALF)
                br, bi = fold_t[0, :, lines], fold_t[1, :, lines]
                real = flat[lines, c * 256 : c * 256 + 256]
                imag = flat[lines, F + c * 256 : F + c * 256 + 256]
                halves.append(dot(br, imag) - dot(bi, real) if plane else dot(br, real) + dot(bi, imag))
            cols = slice(c * 256, c * 256 + 256)
            out[plane, 0:HALF, cols] = (halves[0] + halves[1]).astype(BF16)
            out[plane, HALF:F, cols] = (halves[0] - halves[1]).astype(BF16)
        copies.append(pltpu.make_async_copy(out.at[plane], out_h.at[plane], sems.at[plane]))
        copies[-1].start()
    for copy in copies:
        copy.wait()


SMEM_SPEC = pl.BlockSpec(memory_space=pltpu.SMEM)
VMEM_SPEC = pl.BlockSpec(memory_space=pltpu.VMEM)
HBM_SPEC = pl.BlockSpec(memory_space=pltpu.HBM)
DMA = pltpu.SemaphoreType.DMA


def per_device(facets, facet_offsets, subgrid_offsets, w_terms, tile_count, tile_offsets, observed):
    n = lax.axis_size("facet")
    quads = n // 4
    soff_t, toff_t = subgrid_offsets.T, tile_offsets.T
    slots = observed.shape[0]
    basis_np = basis_table()
    split = np.concatenate([np.arange(0, F, 2), np.arange(1, F, 2)])
    split_m = split[split < M]
    fold = jnp.asarray(np.ascontiguousarray(basis_np[:, split, :HALF]))
    fold_t = jnp.asarray(np.ascontiguousarray(basis_np[:, :HALF, split]))
    br, bi = basis_np[:, :M]
    turned = jnp.asarray(np.block([[br, -bi], [bi, br]]))
    real, imag = padding_table(n)
    pad = jnp.asarray(np.concatenate([real, imag], axis=1))
    pad_t = jnp.asarray(np.block([[real.T, imag.T], [-imag.T, real.T]]))
    ra, ia = real[:, split_m], imag[:, split_m]
    pad_a = jnp.asarray(np.concatenate([ra, ia], axis=1))
    pad_at = jnp.asarray(np.block([[ra.T, ia.T], [-ia.T, ra.T]]))
    taper = jnp.asarray(np.ascontiguousarray(taper_square()[split_m]))
    smooth_np = smooth_table()
    smooth, smooth_t = jnp.asarray(smooth_np), jnp.asarray(np.ascontiguousarray(smooth_np.T))
    ker_np = kernel_table()
    ker, ker_t = jnp.asarray(ker_np), jnp.asarray(np.ascontiguousarray(ker_np.T))
    plain = pltpu.CompilerParams(vmem_limit_bytes=24 * MIB)

    deep = SG + 8 * slots
    piece_shape = (2, M, M)
    cutter = jnp.asarray(np.block([[br.T, bi.T], [-bi.T, br.T]]))
    tables = (fold, taper, smooth, smooth_t, pad, pad_t, pad_a, pad_at, ker, ker_t, turned, fold_t, cutter)
    in_hbm = [
        pltpu.with_memory_space_constraint(x, pltpu.HBM)
        for x in (facet_offsets, soff_t, toff_t, facets[0], *tables, observed)
    ]
    held = (fold_t, taper, pad, pad_t, pad_a, pad_at, ker, ker_t, turned, observed)
    summed, screen, wide, wide_t, fold_t, taper, pad, pad_t, pad_a, pad_at, ker, ker_t, turned, observed, wave = pl.pallas_call(
        functools.partial(forward_kernel, n, slots),
        out_shape=(
            jax.ShapeDtypeStruct((2, M, M), F32), jax.ShapeDtypeStruct((2, SG, SG), F32),
            jax.ShapeDtypeStruct((deep, SG), BF16), jax.ShapeDtypeStruct((SG, deep), BF16),
            *[jax.ShapeDtypeStruct(x.shape, x.dtype) for x in held],
            jax.ShapeDtypeStruct((n, 2, 8, F), F32),
        ),
        in_specs=[SMEM_SPEC] + [HBM_SPEC] * 18,
        out_specs=(VMEM_SPEC,) * 15,
        scratch_shapes=[
            VMEM((2, F // M, WIDE, M), F32), VMEM((2, M, M), F32),
            pltpu.SMEM((1, 2), jnp.int32), pltpu.SMEM((2, n), jnp.int32),
            pltpu.SMEM((2, slots), jnp.int32),
            VMEM((2, F, F), BF16), VMEM((2, F, HALF), BF16), VMEM((2 * F, 2 * M), BF16),
            *[VMEM((2, quads, *piece_shape), BF16)] * 3,
            *[VMEM((quads, *piece_shape), BF16)] * 4,
            DMA((18,)), *[DMA((2, quads))] * 2, *[DMA((quads, 2))] * 4,
        ],
        compiler_params=pltpu.CompilerParams(
            vmem_limit_bytes=32 * MIB, collective_id=0, has_side_effects=True
        ),
        name="forward",
    )(w_terms, *in_hbm)

    residual, coefficient = pl.pallas_call(
        functools.partial(subgrid_kernel, slots),
        out_shape=(
            jax.ShapeDtypeStruct((slots, 2, TV, TV), BF16),
            jax.ShapeDtypeStruct((2, M, M), BF16),
        ),
        in_specs=[SMEM_SPEC, HBM_SPEC] + [VMEM_SPEC] * 11,
        out_specs=(HBM_SPEC, VMEM_SPEC),
        scratch_shapes=[
            VMEM((SG, 2 * M), BF16), VMEM((SG, 2 * SG), BF16),
            VMEM((2, SG // 128, deep, 128), F32), VMEM((2, SG // 128, deep, 128), F32),
            VMEM((slots, 2, TV, TV), BF16),
            pltpu.SMEM((2, slots), jnp.int32), DMA((slots // GROUP,)), DMA,
        ],
        compiler_params=plain,
        name="subgrid",
    )(tile_count, in_hbm[2], summed, screen, wide, wide_t, pad, pad_t, pad_a, pad_at, ker, ker_t, observed)

    sheet = jax.ShapeDtypeStruct((2, F // M, WIDE, M), F32)
    pieces, blank = pl.pallas_call(
        functools.partial(gather_kernel, n),
        out_shape=(jax.ShapeDtypeStruct((n, M, 2 * F), BF16), sheet),
        in_specs=[VMEM_SPEC, HBM_SPEC, VMEM_SPEC, VMEM_SPEC, VMEM_SPEC],
        out_specs=(VMEM_SPEC, VMEM_SPEC),
        scratch_shapes=[
            VMEM((n, 2, M, M), BF16), VMEM((2, M, M), F32),
            pltpu.SMEM((1, 2), jnp.int32),
            *[DMA((2, quads, 2))] * 2, *[DMA((quads, 2))] * 4, DMA, DMA,
        ],
        compiler_params=pltpu.CompilerParams(
            vmem_limit_bytes=24 * MIB, collective_id=1, has_side_effects=True
        ),
        name="gather",
    )(coefficient, in_hbm[0], taper, turned, wave)

    update, _ = pl.pallas_call(
        functools.partial(backward_kernel, n),
        out_shape=(jax.ShapeDtypeStruct((2, F, F), BF16), sheet),
        in_specs=[SMEM_SPEC, VMEM_SPEC, VMEM_SPEC, VMEM_SPEC],
        out_specs=(HBM_SPEC, VMEM_SPEC),
        scratch_shapes=[VMEM((F, 2 * F), BF16), VMEM((2, F, F), BF16), DMA((2,))],
        input_output_aliases={3: 1},
        compiler_params=plain,
        name="backward",
    )(soff_t, pieces, fold_t, blank)
    return (residual, update[None])


def solution(mesh):
    placed = (
        P(("groups", "facet"), None, None, None),
        P(("groups", "facet"), None),
        P("groups", None),
        P(("groups", "facet")),
        P(("groups", "facet")),
        P(("groups", "facet"), None),
        P(("groups", "facet"), None, None, None),
    )
    return jax.shard_map(
        per_device,
        mesh=mesh,
        in_specs=placed,
        out_specs=(
            P(("groups", "facet"), None, None, None),
            P(("groups", "facet"), None, None, None),
        ),
        check_vma=False,
    )
```

```python
import functools
import math

import jax
import jax.numpy as jnp
import ml_dtypes
import numpy as np
from jax import lax
from jax.experimental import pallas as pl
from jax.experimental.pallas import tpu as pltpu
from jax.sharding import PartitionSpec as P

F = 512
M = 128
SG = 512
TV = 128
WIDE = F + M
HALF, BLOCK = F // 2, (F + M) // 2
GROUP = 4

BF16 = jnp.bfloat16
F32 = jnp.float32
TWO_PI = 2.0 * math.pi
MESH = pl.DeviceIdType.MESH
VMEM = pltpu.VMEM
MIB = 1024 * 1024


def basis_table():
    index = np.arange(F)
    angle = -TWO_PI * (index[:, None] * index[None, :] % F) / F
    scale = 1.0 / math.sqrt(F)
    return np.stack([np.cos(angle) * scale, np.sin(angle) * scale]).astype(ml_dtypes.bfloat16)


def padding_table(facet_count):
    angle = TWO_PI * (np.arange(SG)[:, None] * np.arange(M)[None, :] % SG) / SG
    scale = (M * math.sqrt(facet_count)) ** (-0.5)
    return np.stack([np.cos(angle) * scale, np.sin(angle) * scale]).astype(ml_dtypes.bfloat16)


def taper_square():
    taper = 0.6 + 0.4 * np.sin(math.pi * (np.arange(M) + 0.5) / M)
    return (taper[:, None] * taper[None, :]).astype(np.float32)


def dot(left, right):
    return jnp.dot(left, right, preferred_element_type=F32)


def cos_sin_turns(turns):
    quarter = jnp.floor(turns * 4.0 + 0.5)
    y = (turns - quarter * 0.25) * TWO_PI
    y2 = y * y
    sine = y * (1.0 + y2 * (-1.0 / 6 + y2 * (1.0 / 120 + y2 * (-1.0 / 5040 + y2 * (1.0 / 362880)))))
    cosine = 1.0 + y2 * (
        -0.5 + y2 * (1.0 / 24 + y2 * (-1.0 / 720 + y2 * (1.0 / 40320 - y2 * (1.0 / 3628800))))
    )
    which = quarter.astype(jnp.int32) & 3
    odd = (which & 1) == 1
    first = jnp.where(odd, sine, cosine)
    second = jnp.where(odd, cosine, sine)
    cos_value = jnp.where((which == 1) | (which == 2), -first, first)
    sin_value = jnp.where(which >= 2, -second, second)
    return cos_value, sin_value


def tapered_phase(offset_ref, taper_ref):
    spot = lax.broadcasted_iota(jnp.int32, (M, M), 0)
    rows = 2 * (spot & (M // 2 - 1)) + spot // (M // 2)
    columns = lax.broadcasted_iota(jnp.int32, (M, M), 1)
    total = (rows * offset_ref[0, 0] + columns * offset_ref[0, 1]) & (F - 1)
    cos_value, sin_value = cos_sin_turns(total.astype(F32) * (1.0 / F))
    taper = taper_ref[...]
    return cos_value * taper, sin_value * taper


def place(n):
    me = lax.axis_index("facet")
    quads = n // 4
    far_first = [1 + (t + quads // 2 - 1) % (quads - 1) for t in range(quads - 1)]
    return quads, me // 4, lax.rem(me // 2, 2), lax.rem(me, 2), far_first


def index(quad, middle, core):
    return quad * 4 + middle * 2 + core


def greet(peers):
    barrier = pltpu.get_barrier_semaphore()
    for peer in peers:
        pl.semaphore_signal(barrier, inc=1, device_id={"facet": peer}, device_id_type=MESH)
    pl.semaphore_wait(barrier, len(peers))


def send(src, dst, send_sem, recv_sem, peer):
    return pltpu.make_async_remote_copy(
        src_ref=src, dst_ref=dst, send_sem=send_sem, recv_sem=recv_sem,
        device_id={"facet": peer}, device_id_type=MESH,
    )


def fill_screen(w_value, screen):
    @pl.loop(0, 4)
    def _(c):
        rows = pl.ds(pl.multiple_of(c * 128, 128), 128)
        u = (lax.broadcasted_iota(jnp.int32, (128, SG), 0) + (c * 128 - 256)).astype(F32)
        v = (lax.broadcasted_iota(jnp.int32, (128, SG), 1) - 256).astype(F32)
        radius = (u * u + v * v) * (1.0 / (SG * SG))
        cos_value, sin_value = cos_sin_turns(w_value * (jnp.sqrt(1.0 + radius) - 1.0))
        screen[0, rows, :] = cos_value
        screen[1, rows, :] = sin_value


def tap_values():
    taps = np.arange(5, dtype=np.float32)
    value = 0.75 * np.exp(-(taps / 1.5) * (taps / 1.5))
    return [float(x) for x in value.astype(ml_dtypes.bfloat16).astype(np.float32)]


def smooth_table():
    order = np.concatenate([np.arange(0, SG, 2), np.arange(1, SG, 2)])
    distance = np.abs(np.arange(SG)[None, :] - order[:, None])
    taps = np.array(tap_values() + [0.0], np.float32)
    return taps[np.minimum(distance, 5)].astype(ml_dtypes.bfloat16)


def kernel_table():
    distance = np.abs(np.arange(2 * TV)[None, :] - 2 * np.arange(TV)[:, None] - 1)
    taps = np.array(tap_values() + [0.0], np.float32)
    return taps[np.minimum(distance, 5)].astype(ml_dtypes.bfloat16)


def edge_values(position, offset, spot):
    i = spot & 7
    slot = jnp.where(i < 2, i, i + (TV - 8))
    distance = jnp.abs(position - offset - 2 * slot - 1)
    value = jnp.zeros(distance.shape, F32)
    for step, tap in enumerate(tap_values()):
        value = jnp.where(distance == step, tap, value)
    inside = (position >= offset) & (position < offset + 2 * TV) & ((i < 2) | (i >= 6))
    return jnp.where(inside, value, 0.0).astype(BF16)


def fill_rows(slots, toff, wide):
    @pl.loop(0, slots // 2)
    def _(c):
        spot = lax.broadcasted_iota(jnp.int32, (16, SG), 0)
        lane = lax.broadcasted_iota(jnp.int32, (16, SG), 1)
        offset = jnp.where(spot < 8, toff[0, 2 * c], toff[0, 2 * c + 1])
        wide[pl.ds(pl.multiple_of(SG + c * 16, 16), 16), :] = edge_values(lane, offset, spot)


def fill_columns(slots, toff, wide_t):
    lane = lax.broadcasted_iota(jnp.int32, (1, 8 * slots), 1)
    offset = jnp.zeros_like(lane)
    for t in range(slots):
        offset = jnp.where(lane >> 3 == t, toff[0, t], offset)

    @pl.loop(0, SG // 64)
    def _(c):
        position = lax.broadcasted_iota(jnp.int32, (64, 8 * slots), 0) + c * 64
        spot = lax.broadcasted_iota(jnp.int32, (64, 8 * slots), 1)
        wide_t[pl.ds(pl.multiple_of(c * 64, 64), 64), SG:] = edge_values(position, offset, spot)


def forward_kernel(
    n, slots, w_ref, foff_h, soff_h, toff_h, facet_h, fold_h, taper_h, smooth_h, smooth_t_h,
    pad_h, pad_t_h, pad_a_h, pad_at_h, ker_h, ker_t_h, turned_h, fold_t_h, cutter_h, observed_h,
    summed, screen, wide, wide_t, fold_t, taper, pad, pad_t, pad_a, pad_at, ker, ker_t, turned, observed, wave, blank,
    spec, phase, foff, soff, toff, facet, fold, cutter,
    outgoing, own, near, pair, mid, quad_sum, far,
    load_s, near_s, near_r, mid_s, mid_r, far_s, far_r
):
    pairs = (
        (foff_h, foff), (taper_h, taper), (soff_h, soff), (fold_h, fold), (facet_h, facet),
        (toff_h, toff), (cutter_h, cutter), (smooth_h, wide.at[0:SG]), (smooth_t_h, wide_t.at[:, 0:SG]), (observed_h, observed),
        (pad_h, pad), (pad_t_h, pad_t), (ker_h, ker), (ker_t_h, ker_t), (turned_h, turned),
        (pad_a_h, pad_a), (pad_at_h, pad_at), (fold_t_h, fold_t),
    )
    loads = [pltpu.make_async_copy(src, dst, load_s.at[i]) for i, (src, dst) in enumerate(pairs)]
    for load in loads[:7]:
        load.start()

    quads = n // 4
    me = lax.axis_index("facet")
    quad, middle, core = me // 4, lax.rem(me // 2, 2), lax.rem(me, 2)
    other, odd, group = 1 - middle, lax.rem(quad, 2), quad // 2
    mate = quad + 1 - 2 * odd
    sibling, beside = index(quad, middle, 1 - core), index(quad, other, core)
    high = quad // (quads // 2)
    inner_side = jnp.where(high == odd, 0, 1)

    def turn(k):
        spot = quads - 2 - inner_side
        far_k = jnp.where(k > spot, k - 1, k)
        down = quads - 1 - far_k
        down = jnp.where(down < 2 * group + 2, down - 2, down)
        up = jnp.where(far_k >= 2 * group, far_k + 2, far_k)
        j = jnp.where(k == spot, mate, jnp.where(high == 1, up, down))
        return jnp.where(k == quads - 1, quad, j)

    order = [turn(k) for k in range(4)] if quads == 4 else None

    def each(count, body):
        if quads == 4:
            for j in order[:count]:
                body(j)
        else:

            @pl.loop(0, count)
            def _(k):
                body(turn(k))

    barrier = pltpu.get_barrier_semaphore()
    peers = [index(lax.rem(quad + k, quads), middle, core) for k in range(1, quads)] + [beside, sibling]
    for peer in peers:
        pl.semaphore_signal(barrier, inc=1, device_id={"facet": peer}, device_id_type=MESH)

    loads[0].wait()
    loads[1].wait()
    phase[0], phase[1] = tapered_phase(foff, taper)
    loads[2].wait()
    lane = lax.broadcasted_iota(jnp.int32, (8, F), 1)

    @pl.loop(0, n, unroll=2)
    def _(s):
        turns = ((lane * soff[1, s]) & (F - 1)).astype(F32) * (1.0 / F)
        wave[s, 0], wave[s, 1] = cos_sin_turns(turns)

    loads[3].wait()
    loads[4].wait()
    for load in loads[7:]:
        load.start()

    @pl.loop(0, 2)
    def _(c):
        cols = pl.ds(pl.multiple_of(c * 256, 256), 256)
        upper = [facet[plane, 0:HALF, cols].astype(F32) for plane in range(2)]
        lower = [facet[plane, HALF:F, cols].astype(F32) for plane in range(2)]
        for parity in range(2):
            xr, xi = [
                (u - v if parity else u + v).astype(BF16) for u, v in zip(upper, lower)
            ]
            rows = slice(parity * HALF, parity * HALF + HALF)
            real = dot(fold[0, rows], xr) - dot(fold[1, rows], xi)
            imag = dot(fold[0, rows], xi) + dot(fold[1, rows], xr)
            base = parity * BLOCK
            for side in range(2):
                part = slice(side * M, side * M + M)
                for plane, value in enumerate((real, imag)):
                    spec[plane, c * 2 + side, base : base + HALF] = value[:, part]
                    spec[plane, c * 2 + side, base + HALF : base + BLOCK] = value[0 : M // 2, part]

    loads[5].wait()
    loads[6].wait()

    def cut(s, target, where):
        sx = soff[0, s]
        parity = sx & 1
        starts = (parity * BLOCK + (sx >> 1), (1 - parity) * BLOCK + ((sx + 1) >> 1))
        real, imag = [], []
        for tile in range(F // M):
            part = slice(tile * M, tile * M + M)
            cv, sv = wave[s, 0, :, part][None], wave[s, 1, :, part][None]
            r, i = [
                jnp.concatenate([spec[plane, tile, pl.ds(start, M // 2)] for start in starts], axis=0).reshape(
                    M // 8, 8, M
                )
                for plane in range(2)
            ]
            real.append((cv * r + sv * i).reshape(M, M).astype(BF16))
            imag.append((cv * i - sv * r).reshape(M, M).astype(BF16))
        both = dot(jnp.concatenate(real + imag, axis=1), cutter[...])
        real, imag = both[:, 0:M], both[:, M:]
        pc, ps = phase[0], phase[1]
        target[where[0], where[1], 0] = (pc * real - ps * imag).astype(BF16)
        target[where[0], where[1], 1] = (pc * imag + ps * real).astype(BF16)

    def near_copy(h, j):
        return send(outgoing.at[h, j], near.at[h, j], near_s.at[h, j], near_r.at[h, j], sibling)

    def mid_copy(j, p):
        return send(pair.at[j, p], mid.at[j, p], mid_s.at[j, p], mid_r.at[j, p], beside)

    def far_copy(j, slot, p):
        return send(quad_sum.at[j, p], far.at[slot, p], far_s.at[j, p], far_r.at[slot, p], index(j, middle, core))

    def near_sum(h, j, p):
        return own[h, j, p].astype(F32) + near[h, j, p].astype(F32)

    def mid_sum(j, p):
        return near_sum(1, j, p) + mid[j, p].astype(F32)

    pl.semaphore_wait(barrier, len(peers))

    def give(h, half, j):
        cut(index(j, half, 1 - core), outgoing, (h, j))
        near_copy(h, j).start()

    def keep(h, half, j):
        cut(index(j, half, core), own, (h, j))

    def pass_on(j):
        near_copy(0, j).wait_recv()
        for p in range(2):
            pair[j, p] = near_sum(0, j, p).astype(BF16)
            mid_copy(j, p).start()

    if quads == 4:
        give(0, other, order[0])
        give(0, other, order[1])
        keep(0, other, order[0])
        give(0, other, order[2])
        keep(0, other, order[1])
        give(0, other, order[3])
        pass_on(order[0])
        keep(0, other, order[2])
        pass_on(order[1])
        keep(0, other, order[3])
        pass_on(order[2])
        pass_on(order[3])
    else:
        each(quads, lambda j: give(0, other, j))
        each(quads, lambda j: keep(0, other, j))
        each(quads, pass_on)
    each(quads, lambda j: give(1, middle, j))
    each(quads, lambda j: keep(1, middle, j))
    def combine(j):
        near_copy(1, j).wait_recv()
        for p in range(2):
            mid_copy(j, p).wait_recv()

            quad_sum[j, p] = mid_sum(j, p).astype(BF16)
            far_copy(j, quad, p).start()

    if quads == 4:
        combine(order[0])
        fill_rows(slots, toff, wide)
        blank[...] = jnp.zeros_like(blank)
        combine(order[1])
        fill_columns(slots, toff, wide_t)
        combine(order[2])
    else:
        each(quads - 1, combine)
        fill_rows(slots, toff, wide)
        blank[...] = jnp.zeros_like(blank)
        fill_columns(slots, toff, wide_t)
    fill_screen(w_ref[0], screen)
    near_copy(1, quad).wait_recv()
    for p in range(2):
        mid_copy(quad, p).wait_recv()
        summed[p] = mid_sum(quad, p)
    for k in range(quads - 1):
        slot = order[2 - k] if quads == 4 else turn(k)
        for p in range(2):
            far_copy(quad, slot, p).wait_recv()
            summed[p] += far[slot, p].astype(F32)
    for load in loads[7:]:
        load.wait()

    def finish(j):
        near_copy(0, j).wait_send()
        near_copy(1, j).wait_send()
        for p in range(2):
            mid_copy(j, p).wait_send()

    def finish_far(j):
        for p in range(2):

            far_copy(j, quad, p).wait_send()

    each(quads, finish)
    each(quads - 1, finish_far)


def subgrid_kernel(
    slots, count_ref, toff_h, summed, screen, wide, wide_t, pad, pad_t, pad_a, pad_at, ker, ker_t, observed, blank,
    residual_h, coefficient, spread, inner, model, grid, sent, toff, sems, load_s
):
    load = pltpu.make_async_copy(toff_h, toff, load_s)
    load.start()
    groups = slots // GROUP
    sr, si = summed[0], summed[1]
    stacked = jnp.concatenate(
        [jnp.concatenate([sr, si], axis=1), jnp.concatenate([-si, sr], axis=1)], axis=0
    ).astype(BF16)
    inner[...] = dot(pad_a[...], stacked).astype(BF16)

    for c in range(2):
        cols = slice(c * 256, c * 256 + 256)
        late = slice(SG + c * 256, SG + c * 256 + 256)
        real, imag = dot(inner[...], pad_t[:, cols]), dot(inner[...], pad_t[:, late])
        cos_value, sin_value = screen[0, :, cols], screen[1, :, cols]
        model[:, cols] = (cos_value * real - sin_value * imag).astype(BF16)
        model[:, late] = (cos_value * imag + sin_value * real).astype(BF16)

    for plane in range(2):
        for c in range(2):
            start = plane * SG + c * 256
            value = dot(wide[...], model[:, start : start + 256])
            for side in range(2):
                grid[plane, c * 2 + side] = value[:, side * 128 : side * 128 + 128]

    load.wait()
    count = count_ref[0]
    lanes = lax.broadcasted_iota(jnp.int32, (TV, TV), 1)
    subs = lax.broadcasted_iota(jnp.int32, (8, TV), 0)
    top, bottom = subs < 2, subs >= 6

    def out_copy(step):
        tiles = pl.ds(step * GROUP, GROUP)
        return pltpu.make_async_copy(sent.at[tiles], residual_h.at[tiles], sems.at[step])

    filled = (count + GROUP - 1) // GROUP

    @pl.loop(0, filled)
    def _(step):
        slot = [step * GROUP + g for g in range(GROUP)]
        spots, left = [], []
        for t in slot:
            ou, ov = toff[0, t] + 1, toff[1, t]
            rows = pl.ds((ou & 1) * (SG // 2) + (ou >> 1), TV)
            tail = pl.ds(pl.multiple_of(SG + t * 8, 8), 8)
            first, turn = ov >> 7, ov & 127
            tiles = (first, first + 1, jnp.minimum(first + 2, SG // 128 - 1))
            spots.append((rows, tail, tiles, turn))

            def pick(plane, where_rows, size):
                keep = lanes[0:size] >= turn
                part = [grid[plane, k, where_rows] for k in tiles]
                both = [jnp.where(keep, part[k], part[k + 1]) for k in range(2)]
                return jnp.concatenate([pltpu.roll(x, (TV - turn) & 127, 1) for x in both], axis=1)

            for plane in range(2):
                body, edge = pick(plane, rows, TV), pick(plane, tail, 8)
                wide_top = jnp.concatenate([top, top], axis=1)
                wide_bottom = jnp.concatenate([bottom, bottom], axis=1)
                left.append(
                    jnp.concatenate(
                        [
                            jnp.where(wide_top, edge, body[0:8]), body[8 : TV - 8],
                            jnp.where(wide_bottom, edge, body[TV - 8 :]),
                        ],
                        axis=0,
                    ).astype(BF16)
                )
        rest = []
        for g, t in enumerate(slot):
            for plane in range(2):
                predicted = dot(left[g * 2 + plane], ker_t[...])
                value = (observed[t, plane].astype(F32) - predicted).astype(BF16)
                rest.append(jnp.where(t < count, value, jnp.zeros_like(value)))
                sent[t, plane] = rest[-1]
        out_copy(step).start()
        back = [dot(value, ker[...]).astype(BF16).astype(F32) for value in rest]
        for g in range(GROUP):
            rows, tail, tiles, turn = spots[g]
            keep = lanes >= turn
            for plane in range(2):
                value = back[g * 2 + plane]
                one, two = pltpu.roll(value[:, 0:128], turn, 1), pltpu.roll(value[:, 128:], turn, 1)
                blank = jnp.zeros((TV, TV), F32)
                parts = (jnp.where(keep, one, blank), jnp.where(keep, two, one), jnp.where(keep, blank, two))
                for tile, part in zip(tiles, parts):
                    zero = blank[0:8]
                    edge = jnp.where(top, part[0:8], jnp.where(bottom, part[TV - 8 :], zero))
                    body = jnp.concatenate(
                        [jnp.where(top, zero, part[0:8]), part[8 : TV - 8], jnp.where(bottom, zero, part[TV - 8 :])],
                        axis=0,
                    )
                    spread[plane, tile, rows] += body
                    spread[plane, tile, tail] += edge

    @pl.loop(filled, groups)
    def _(step):
        for g in range(GROUP):
            sent[step * GROUP + g] = jnp.zeros(sent.shape[1:], BF16)
        out_copy(step).start()

    for c in range(2):
        cols = slice(c * 256, c * 256 + 256)
        late = slice(SG + c * 256, SG + c * 256 + 256)
        ar, ai = [
            dot(wide_t[...], jnp.concatenate([spread[p, 2 * c], spread[p, 2 * c + 1]], axis=1).astype(BF16))
            for p in range(2)
        ]
        sc, ss = screen[0, :, cols], screen[1, :, cols]
        model[:, cols] = (sc * ar + ss * ai).astype(BF16)
        model[:, late] = (sc * ai - ss * ar).astype(BF16)
    reduced = (
        dot(pad_at[:, 0:SG], model[:, 0:SG]) + dot(pad_at[:, SG:], model[:, SG:])
    ).astype(BF16)
    both = dot(reduced, pad[...])
    coefficient[0] = (both[0:M, 0:M] + both[M:, M:]).astype(BF16)
    coefficient[1] = (both[M:, 0:M] - both[0:M, M:]).astype(BF16)

    @pl.loop(0, groups)
    def _(step):
        out_copy(step).wait()


def gather_kernel(
    n, mine, foff_h, taper, turned, wave, out, blank, arrived, phase, foff,
    near_s, near_r, mid_s, mid_r, far_s, far_r, local, load_s
):
    quads = n // 4
    me = lax.axis_index("facet")
    quad, middle, core = me // 4, lax.rem(me // 2, 2), lax.rem(me, 2)
    other = 1 - middle
    sibling, beside = index(quad, middle, 1 - core), index(quad, other, core)
    load = pltpu.make_async_copy(foff_h, foff, load_s)
    load.start()

    barrier = pltpu.get_barrier_semaphore()
    peers = [index(lax.rem(quad + k, quads), middle, core) for k in range(1, quads)] + [beside, sibling]
    for peer in peers:
        pl.semaphore_signal(barrier, inc=1, device_id={"facet": peer}, device_id_type=MESH)
    pl.semaphore_wait(barrier, len(peers))

    def away(k):
        return lax.rem(quad + 1 + lax.rem(k + quads // 2 - 1, quads - 1), quads)

    def event(i):
        back = lax.rem(quad + quads - 1 - lax.rem(i + quads // 2 - 2, quads - 1), quads)
        return jnp.where(i == 0, quad, back)

    def far_copy(slot, to, p):
        spot = index(slot, middle, core)
        return send(
            mine.at[p], arrived.at[spot, p], far_s.at[to, p], far_r.at[slot, p], index(to, middle, core)
        )

    def mid_copy(j, h, p):
        piece = arrived.at[index(j, h, core), p]
        return send(piece, piece, mid_s.at[j, p], mid_r.at[j, p], beside)

    def near_copy(h, j, side, p):
        piece = arrived.at[index(j, h, side), p]
        return send(piece, piece, near_s.at[h, j, p], near_r.at[h, j, p], sibling)

    def mid_own(p):
        return send(mine.at[p], arrived.at[me, p], mid_s.at[quad, p], mid_r.at[quad, p], beside)

    def near_own(p):
        return send(
            mine.at[p], arrived.at[me, p], near_s.at[middle, quad, p], near_r.at[middle, quad, p], sibling
        )

    own = pltpu.make_async_copy(mine, arrived.at[me], local)
    own.start()
    for k in range(quads - 1):
        for p in range(2):
            far_copy(quad, away(k), p).start()
    for p in range(2):
        mid_own(p).start()
        near_own(p).start()

    load.wait()
    phase[0], phase[1] = tapered_phase(foff, taper)
    own.wait()

    def transform(spot):
        pc, ps = phase[0], phase[1]
        real, imag = arrived[spot, 0].astype(F32), arrived[spot, 1].astype(F32)
        both = jnp.concatenate([pc * real + ps * imag, pc * imag - ps * real], axis=1).astype(BF16)
        for c in range(F // 256):
            cols, late = slice(c * 256, c * 256 + 256), slice(F + c * 256, F + c * 256 + 256)
            real = dot(both, turned[:, cols]).reshape(M // 8, 8, 256)
            imag = dot(both, turned[:, late]).reshape(M // 8, 8, 256)
            cv, sv = wave[spot, 0, :, cols][None], wave[spot, 1, :, cols][None]
            out[spot, :, cols] = (cv * real - sv * imag).reshape(M, 256).astype(BF16)
            out[spot, :, late] = (cv * imag + sv * real).reshape(M, 256).astype(BF16)

    transform(me)
    blank[...] = jnp.zeros_like(blank)

    def take_far(j):
        for p in range(2):
            far_copy(j, j, p).wait_recv()
            mid_copy(j, middle, p).start()
            near_copy(middle, j, core, p).start()

    def take_mid(j):
        for p in range(2):
            mid_copy(j, other, p).wait_recv()
            near_copy(other, j, core, p).start()

    def wait_near(h, j):
        for p in range(2):
            near_copy(h, j, 1 - core, p).wait_recv()

    def step(i, far, mid, late):
        one, two, three = event(i), event(jnp.maximum(i - 2, 0)), event(jnp.maximum(i - 3, 0))
        if far:
            take_far(one)
        if mid:
            take_mid(two)
            wait_near(middle, two)
        if late:
            wait_near(other, three)
        if far:
            transform(index(one, middle, core))
        if mid:
            transform(index(two, other, core))
            transform(index(two, middle, 1 - core))
        if late:
            transform(index(three, other, 1 - core))

    step(1, True, False, False)
    step(2, True, True, False)

    if quads == 4:
        step(3, True, True, True)
    else:

        @pl.loop(3, quads)
        def _(i):
            step(i, True, True, True)

    step(quads, False, True, True)
    step(quads + 1, False, True, True)
    step(quads + 2, False, False, True)
    for p in range(2):
        mid_own(p).wait_send()
        near_own(p).wait_send()
        near_copy(other, quad, core, p).wait_send()

    @pl.loop(1, quads)
    def _(i):
        j = event(i)
        for p in range(2):
            far_copy(quad, j, p).wait_send()
            mid_copy(j, middle, p).wait_send()
            near_copy(middle, j, core, p).wait_send()
            near_copy(other, j, core, p).wait_send()


def backward_kernel(n, soff, pieces, fold_t, blank, out_h, acc, flat, out, sems):
    @pl.loop(0, n, unroll=4)
    def _(s):
        sx = soff[0, s]
        parity = sx & 1
        starts = (parity * BLOCK + (sx >> 1), (1 - parity) * BLOCK + ((sx + 1) >> 1))
        for odd in range(2):
            rows, lines = pl.ds(starts[odd], M // 2), slice(odd * M // 2, odd * M // 2 + M // 2)
            for plane in range(2):
                for k in range(F // M):
                    cols = slice(plane * F + k * M, plane * F + k * M + M)
                    acc[plane, k, rows] += pieces[s, lines, cols].astype(F32)

    for plane in range(2):
        for k in range(F // M):
            cols = slice(plane * F + k * M, plane * F + k * M + M)
            for parity in range(2):
                base, to = parity * BLOCK, parity * HALF
                flat[to : to + M // 2, cols] = (
                    acc[plane, k, base : base + M // 2] + acc[plane, k, base + HALF : base + BLOCK]
                ).astype(BF16)
                flat[to + M // 2 : to + HALF, cols] = acc[plane, k, base + M // 2 : base + HALF].astype(BF16)

    copies = []
    for plane in range(2):
        for c in range(2):
            halves = []
            for parity in range(2):
                lines = slice(parity * HALF, parity * HALF + HALF)
                br, bi = fold_t[0, :, lines], fold_t[1, :, lines]
                real = flat[lines, c * 256 : c * 256 + 256]
                imag = flat[lines, F + c * 256 : F + c * 256 + 256]
                halves.append(dot(br, imag) - dot(bi, real) if plane else dot(br, real) + dot(bi, imag))
            cols = slice(c * 256, c * 256 + 256)
            out[plane, 0:HALF, cols] = (halves[0] + halves[1]).astype(BF16)
            out[plane, HALF:F, cols] = (halves[0] - halves[1]).astype(BF16)
        copies.append(pltpu.make_async_copy(out.at[plane], out_h.at[plane], sems.at[plane]))
        copies[-1].start()
    for copy in copies:
        copy.wait()


SMEM_SPEC = pl.BlockSpec(memory_space=pltpu.SMEM)
VMEM_SPEC = pl.BlockSpec(memory_space=pltpu.VMEM)
HBM_SPEC = pl.BlockSpec(memory_space=pltpu.HBM)
DMA = pltpu.SemaphoreType.DMA


def per_device(facets, facet_offsets, subgrid_offsets, w_terms, tile_count, tile_offsets, observed):
    n = lax.axis_size("facet")
    quads = n // 4
    soff_t, toff_t = subgrid_offsets.T, tile_offsets.T
    slots = observed.shape[0]
    basis_np = basis_table()
    split = np.concatenate([np.arange(0, F, 2), np.arange(1, F, 2)])
    split_m = split[split < M]
    fold = jnp.asarray(np.ascontiguousarray(basis_np[:, split, :HALF]))
    fold_t = jnp.asarray(np.ascontiguousarray(basis_np[:, :HALF, split]))
    br, bi = basis_np[:, :M]
    turned = jnp.asarray(np.block([[br, -bi], [bi, br]]))
    real, imag = padding_table(n)
    pad = jnp.asarray(np.concatenate([real, imag], axis=1))
    pad_t = jnp.asarray(np.block([[real.T, imag.T], [-imag.T, real.T]]))
    ra, ia = real[:, split_m], imag[:, split_m]
    pad_a = jnp.asarray(np.concatenate([ra, ia], axis=1))
    pad_at = jnp.asarray(np.block([[ra.T, ia.T], [-ia.T, ra.T]]))
    taper = jnp.asarray(np.ascontiguousarray(taper_square()[split_m]))
    smooth_np = smooth_table()
    smooth, smooth_t = jnp.asarray(smooth_np), jnp.asarray(np.ascontiguousarray(smooth_np.T))
    ker_np = kernel_table()
    ker, ker_t = jnp.asarray(ker_np), jnp.asarray(np.ascontiguousarray(ker_np.T))
    plain = pltpu.CompilerParams(vmem_limit_bytes=24 * MIB)

    deep = SG + 8 * slots
    piece_shape = (2, M, M)
    cutter = jnp.asarray(np.block([[br.T, bi.T], [-bi.T, br.T]]))
    tables = (fold, taper, smooth, smooth_t, pad, pad_t, pad_a, pad_at, ker, ker_t, turned, fold_t, cutter)
    in_hbm = [
        pltpu.with_memory_space_constraint(x, pltpu.HBM)
        for x in (facet_offsets, soff_t, toff_t, facets[0], *tables, observed)
    ]
    held = (fold_t, taper, pad, pad_t, pad_a, pad_at, ker, ker_t, turned, observed)
    summed, screen, wide, wide_t, fold_t, taper, pad, pad_t, pad_a, pad_at, ker, ker_t, turned, observed, wave, blank = pl.pallas_call(
        functools.partial(forward_kernel, n, slots),
        out_shape=(
            jax.ShapeDtypeStruct((2, M, M), F32), jax.ShapeDtypeStruct((2, SG, SG), F32),
            jax.ShapeDtypeStruct((deep, SG), BF16), jax.ShapeDtypeStruct((SG, deep), BF16),
            *[jax.ShapeDtypeStruct(x.shape, x.dtype) for x in held],
            jax.ShapeDtypeStruct((n, 2, 8, F), F32),
            jax.ShapeDtypeStruct((2, SG // 128, deep, 128), F32),
        ),
        in_specs=[SMEM_SPEC] + [HBM_SPEC] * 18,
        out_specs=(VMEM_SPEC,) * 16,
        scratch_shapes=[
            VMEM((2, F // M, WIDE, M), F32), VMEM((2, M, M), F32),
            pltpu.SMEM((1, 2), jnp.int32), pltpu.SMEM((2, n), jnp.int32),
            pltpu.SMEM((2, slots), jnp.int32),
            VMEM((2, F, F), BF16), VMEM((2, F, HALF), BF16), VMEM((2 * F, 2 * M), BF16),
            *[VMEM((2, quads, *piece_shape), BF16)] * 3,
            *[VMEM((quads, *piece_shape), BF16)] * 4,
            DMA((18,)), *[DMA((2, quads))] * 2, *[DMA((quads, 2))] * 4,
        ],
        compiler_params=pltpu.CompilerParams(
            vmem_limit_bytes=32 * MIB, collective_id=0, has_side_effects=True
        ),
        name="forward",
    )(w_terms, *in_hbm)

    residual, coefficient, _ = pl.pallas_call(
        functools.partial(subgrid_kernel, slots),
        out_shape=(
            jax.ShapeDtypeStruct((slots, 2, TV, TV), BF16),
            jax.ShapeDtypeStruct((2, M, M), BF16),
            jax.ShapeDtypeStruct((2, SG // 128, deep, 128), F32),
        ),
        in_specs=[SMEM_SPEC, HBM_SPEC] + [VMEM_SPEC] * 12,
        out_specs=(HBM_SPEC, VMEM_SPEC, VMEM_SPEC),
        input_output_aliases={13: 2},
        scratch_shapes=[
            VMEM((SG, 2 * M), BF16), VMEM((SG, 2 * SG), BF16),
            VMEM((2, SG // 128, deep, 128), F32),
            VMEM((slots, 2, TV, TV), BF16),
            pltpu.SMEM((2, slots), jnp.int32), DMA((slots // GROUP,)), DMA,
        ],
        compiler_params=plain,
        name="subgrid",
    )(tile_count, in_hbm[2], summed, screen, wide, wide_t, pad, pad_t, pad_a, pad_at, ker, ker_t, observed, blank)

    sheet = jax.ShapeDtypeStruct((2, F // M, WIDE, M), F32)
    pieces, blank = pl.pallas_call(
        functools.partial(gather_kernel, n),
        out_shape=(jax.ShapeDtypeStruct((n, M, 2 * F), BF16), sheet),
        in_specs=[VMEM_SPEC, HBM_SPEC, VMEM_SPEC, VMEM_SPEC, VMEM_SPEC],
        out_specs=(VMEM_SPEC, VMEM_SPEC),
        scratch_shapes=[
            VMEM((n, 2, M, M), BF16), VMEM((2, M, M), F32),
            pltpu.SMEM((1, 2), jnp.int32),
            *[DMA((2, quads, 2))] * 2, *[DMA((quads, 2))] * 4, DMA, DMA,
        ],
        compiler_params=pltpu.CompilerParams(
            vmem_limit_bytes=24 * MIB, collective_id=1, has_side_effects=True
        ),
        name="gather",
    )(coefficient, in_hbm[0], taper, turned, wave)

    update, _ = pl.pallas_call(
        functools.partial(backward_kernel, n),
        out_shape=(jax.ShapeDtypeStruct((2, F, F), BF16), sheet),
        in_specs=[SMEM_SPEC, VMEM_SPEC, VMEM_SPEC, VMEM_SPEC],
        out_specs=(HBM_SPEC, VMEM_SPEC),
        scratch_shapes=[VMEM((F, 2 * F), BF16), VMEM((2, F, F), BF16), DMA((2,))],
        input_output_aliases={3: 1},
        compiler_params=plain,
        name="backward",
    )(soff_t, pieces, fold_t, blank)
    return (residual, update[None])


def solution(mesh):
    placed = (
        P(("groups", "facet"), None, None, None),
        P(("groups", "facet"), None),
        P("groups", None),
        P(("groups", "facet")),
        P(("groups", "facet")),
        P(("groups", "facet"), None),
        P(("groups", "facet"), None, None, None),
    )
    return jax.shard_map(
        per_device,
        mesh=mesh,
        in_specs=placed,
        out_specs=(
            P(("groups", "facet"), None, None, None),
            P(("groups", "facet"), None, None, None),
        ),
        check_vma=False,
    )
```
